32 devices in a mesh: gx: 8 (over z, y), gy: 4 (over x, core).
Axes of the slice: x: 2, y: 2, z: 4, core: 2. Of those that a mesh axis runs over, the one named last changes fastest.
Arguments:
- fields: float32 [6, 128, 96, 128], P(None, 'gx', 'gy'), may hold values from -6 to 6
- material: int32 [128, 96, 128], P('gx', 'gy'), may hold values from 0 to 15
- permittivity: float32 [16], replicated, may hold values from 1 to 4
- patch_cell: int32 [8192], P(('gx', 'gy')), may hold values from 0 to 49151
- patch_owner: int32 [8192, 1], P(('gx', 'gy')), may hold values from 0 to 31; in each aligned block of 256 rows (0 to 255, 256 to 511, ...) at most 16 rows name the same one
Outputs:
- new_fields: float32 [6, 128, 96, 128], P(None, 'gx', 'gy')
- far_field: float32 [12, 4096], P(None, ('gx', 'gy'))
The draws below stay inside these ranges and needn't reach their ends.
Inputs may be any that keep to these rules, and one draw needn't show every extreme that they name: `patch_cell`: an index into the cells of the patch's own device block, x slowest and z fastest. `patch_owner`: among the rows of one device no sector is named by more than 16 rows, a bound that some block reaches; every sector is named by some row.
All inputs are finite; a program needn't handle non-finite values.
Results may differ from the reference program's by a relative error of at most 0.00022.
Values sent between devices are 32-bit elements; how exact they have to be, the bound alone decides.
A program may use at most 128 MiB of HBM per device.

```python
import math
import jax
import jax.numpy as jnp
import numpy as np
from jax import lax

CX = 16
CY = 24
NZ = 128
P_DEV = 256
ANG_DEV = 128
COURANT = 64
MATERIALS = 16
NX = 128
NY = 96
OWNERS = 32
PATCHES = 8192
CAP = 16
N_GX = 8
N_GY = 4


def plant(drawn, stream_key, least, top_value):
    shape = drawn.shape
    index_at = [jax.random.randint(jax.random.fold_in(stream_key, axis), (), 0, shape[axis]) for axis in range(len(shape))]
    drawn = drawn.at[tuple(index_at)].set(least)
    longest = shape.index(max(shape))
    index_at[longest] = (index_at[longest] + 1) % shape[longest]
    return drawn.at[tuple(index_at)].set(top_value)


def steps_of(rng, dims, cuts, smallest, largest):
    level, own = 1.0, jax.random.fold_in(rng, 6)
    for dim, shards_of in cuts:
        heights = jnp.exp(jax.random.uniform(jax.random.fold_in(own, dim), (shards_of,), jnp.float32, smallest / len(cuts), largest / len(cuts)))
        level = level * jnp.repeat(heights, dims[dim] // shards_of).reshape([-1 if axis == dim else 1 for axis in range(len(dims))])
    return level


def deal_out(stream_key, own, number, rows, count, top, most, skew):
    sequence = jax.random.permutation(stream_key, count)
    packed, usual = portions_of(count, rows * top, most, skew, True), portions_of(count, rows * top, most, skew, False)
    places = jnp.arange(count)

    def named(lengths, turn):
        used = int((lengths > 0).sum())
        fixed = max(1, used // 4)
        passed = fixed + (places - fixed + turn * (used - fixed)) % max(1, count - fixed)
        return jnp.zeros((count,), jnp.int32).at[sequence[jnp.where(places < fixed, places, passed)]].set(jnp.asarray(lengths, jnp.int32))

    lengths = jnp.where(number % 4 == 0, named(packed, number // 4), named(usual, number - number // 4 - 1))
    mixed = jax.random.permutation(jax.random.fold_in(own, 3), count)
    giver, taker = mixed[0:count // 2 * 2:2], mixed[1:count // 2 * 2:2]
    room = jnp.minimum(lengths[giver] - 1, most - lengths[taker]) // 2
    room = jnp.where((giver == sequence[0]) | (taker == sequence[0]) | (lengths[taker] == 0), 0, jnp.maximum(room, 0))
    passed = jax.random.randint(jax.random.fold_in(own, 4), (count // 2,), 0, 1 << 20) % (room + 1)
    lengths = lengths.at[giver].add(-passed).at[taker].add(passed)
    labels = jnp.searchsorted(jnp.cumsum(lengths), jnp.arange(rows * top), side="right").astype(jnp.int32)
    grid = labels.reshape(top, rows).T
    grid = grid[jax.random.permutation(jax.random.fold_in(own, 1), rows)]
    turn = jax.random.randint(jax.random.fold_in(own, 2), (rows, 1), 0, top)
    return jnp.take_along_axis(grid, (jnp.arange(top)[None, :] + turn) % top, axis=1)


def portions_of(count, total, bound, skew, full):
    loads = [(1 << 20) // math.isqrt(rank ** skew) + 1 for rank in range(1, count + 1)]
    largest = bound if full else min(bound, max(-(-total // count), total * loads[0] // sum(loads)))
    least = 1 if total - largest >= count - 1 else 0
    given, spare = [largest] + [least] * (count - 1), total - largest - least * (count - 1)
    while spare > 0:
        movable = [i for i in range(1, count) if given[i] < largest] or [i for i in range(1, count) if given[i] < bound]
        mass, remaining = sum([loads[i] for i in movable]), spare
        for i in movable:
            more = min(bound - given[i], max(1, remaining * loads[i] // mass), spare)
            given[i] = given[i] + more
            spare = spare - more
    return np.array(given)


def bell_draw(stream_key, shape, deviation, limit, shards=(), held_as=jnp.bfloat16):
    result = jax.random.normal(stream_key, shape, jnp.float32) * deviation
    if len(shards) > 0:
        result = steps_of(stream_key, shape, shards, -0.22, 0.18) * result
    return jnp.clip(result, min=-limit, max=limit).astype(held_as)


def setup_inputs(seed: int = 0) -> dict:
    streams_of = jax.random.split(jax.random.key(seed), 6)
    fields = bell_draw(streams_of[0], (6, NX, NY, NZ), 1.0, 6.0, ((1, 8), (2, 4)), jnp.float32)
    material = plant(jax.random.randint(streams_of[1], (NX, NY, NZ), 0, MATERIALS), jax.random.fold_in(streams_of[1], 1), 0, MATERIALS - 1).astype(jnp.int32)
    permittivity = jnp.clip(jnp.exp(jax.random.uniform(streams_of[2], (MATERIALS,), jnp.float32, math.log(1.0), math.log(4.0))), 1.0, 4.0)
    patch_cell = plant(jax.random.randint(streams_of[3], (PATCHES,), 0, CX * CY * NZ), jax.random.fold_in(streams_of[3], 1), 0, (CX * CY * NZ) - 1).astype(jnp.int32)
    patch_owner_keys = jax.random.split(jax.random.fold_in(streams_of[4], 1), PATCHES // P_DEV)
    patch_owner_turns = jax.random.permutation(jax.random.fold_in(streams_of[4], 3), PATCHES // P_DEV)
    patch_owner = jax.vmap(lambda own, number: deal_out(jax.random.fold_in(streams_of[4], 2), own, number, P_DEV, OWNERS, 1, CAP, 2))(patch_owner_keys, patch_owner_turns).reshape((PATCHES, 1))
    return dict(fields=fields, material=material, permittivity=permittivity, patch_cell=patch_cell, patch_owner=patch_owner)


KAPPA = 0.5

def explicit(padded, curl_coef, half_step):
    centre = padded[:, 1:-1, 1:-1]

    def slope_x(member):
        return 0.5 * (padded[member, 2:, 1:-1] - padded[member, :-2, 1:-1])

    def slope_y(member):
        return 0.5 * (padded[member, 1:-1, 2:] - padded[member, 1:-1, :-2])

    def slope_z(member):
        ground = jnp.pad(centre[member], ((0, 0), (0, 0), (1, 1)))
        return 0.5 * (ground[:, :, 2:] - ground[:, :, :-2])
    curl_h = [slope_y(5) - slope_z(4), slope_z(3) - slope_x(5), slope_x(4) - slope_y(3)]
    curl_e = [slope_y(2) - slope_z(1), slope_z(0) - slope_x(2), slope_x(1) - slope_y(0)]
    electric = [centre[member] + curl_coef * curl_h[member] for member in range(3)]
    magnetic = [centre[3 + member] - half_step * curl_e[member] for member in range(3)]
    return jnp.stack(electric + magnetic)

def factor_lines(coef_lines):

    def advance(upper_prev, coef_row):
        pivot = 1.0 / (1.0 + 2.0 * coef_row + coef_row * upper_prev)
        upper_now = -coef_row * pivot
        return (upper_now, (upper_now, pivot))
    ignored, (uppers, pivots) = lax.scan(advance, jnp.zeros_like(coef_lines[0]), coef_lines)
    return (uppers, pivots)

def sweep_lines(coef_lines, uppers, pivots, right_lines):

    def forward(carry_prev, rows):
        coef_row, pivot, right_row = rows
        now_value = (right_row + coef_row * carry_prev) * pivot
        return (now_value, now_value)
    start_zero = jnp.zeros_like(right_lines[0] * coef_lines[0])
    ignored, reduced = lax.scan(forward, start_zero, (coef_lines, pivots, right_lines))

    def backward(next_value, rows):
        upper_row, reduced_row = rows
        now_value = reduced_row - upper_row * next_value
        return (now_value, now_value)
    ignored, solved = lax.scan(backward, start_zero, (uppers, reduced), reverse=True)
    return solved

def solve_leading(stack, coef_lines):
    uppers, pivots = factor_lines(coef_lines)

    def one_component(component):
        return sweep_lines(coef_lines, uppers, pivots, component)
    return lax.map(one_component, stack)

def far_phase(pos_x, pos_y, pos_z, owner_f, owners, angle_count):
    theta = math.pi * (jnp.arange(angle_count, dtype=jnp.float32) + 0.5) / angle_count
    azimuth = owner_f * (2.0 * math.pi / owners)
    sin_theta = jnp.sin(theta)[None, :]
    cos_theta = jnp.cos(theta)[None, :]
    cos_phi = jnp.cos(azimuth)[:, None]
    sin_phi = jnp.sin(azimuth)[:, None]
    return KAPPA * (pos_x[:, None] * sin_theta * cos_phi + pos_y[:, None] * sin_theta * sin_phi + pos_z[:, None] * cos_theta)

def reference(fields, material, permittivity, patch_cell, patch_owner):
    eps = permittivity[material]
    half_step = COURANT / 2.0
    implicit_coef = half_step * half_step / eps
    curl_coef = half_step / eps
    padded = jnp.pad(fields, ((0, 0), (1, 1), (1, 1), (0, 0)))
    first_side = explicit(padded, curl_coef, half_step)
    mid_fields = solve_leading(first_side, implicit_coef)
    padded = jnp.pad(mid_fields, ((0, 0), (1, 1), (1, 1), (0, 0)))
    second_side = explicit(padded, curl_coef, half_step)
    moved = jnp.moveaxis(second_side, 2, 1)
    coef_y = jnp.transpose(implicit_coef, (1, 0, 2))
    new_fields = jnp.moveaxis(solve_leading(moved, coef_y), 1, 2)
    owners = N_GX * N_GY
    device = jnp.arange(PATCHES, dtype=jnp.int32) // P_DEV
    block_x = device // N_GY
    block_y = device % N_GY
    grid_x = block_x * CX + patch_cell // (CY * NZ)
    grid_y = block_y * CY + patch_cell // NZ % CY
    grid_z = patch_cell % NZ
    samples = new_fields[:, grid_x, grid_y, grid_z]
    owner = patch_owner[:, 0]
    phases = far_phase(grid_x.astype(jnp.float32), grid_y.astype(jnp.float32), grid_z.astype(jnp.float32), owner.astype(jnp.float32), owners, ANG_DEV)
    cosine = jnp.cos(phases)
    sine = jnp.sin(phases)
    values_t = jnp.transpose(samples)
    terms = jnp.concatenate([values_t[:, :, None] * cosine[:, None, :], values_t[:, :, None] * sine[:, None, :]], axis=1)
    summed = jax.ops.segment_sum(terms, owner, num_segments=owners)
    far_field = jnp.transpose(summed, (1, 0, 2)).reshape(12, owners * ANG_DEV) * (1.0 / math.sqrt(P_DEV))
    return (new_fields, far_field)
```

```python
import functools
import math

import jax
import jax.numpy as jnp
from jax import lax
from jax.experimental import pallas as pl
from jax.experimental.pallas import tpu as pltpu
from jax.sharding import PartitionSpec as P

ANG_DEV = 128
COURANT = 64
KAPPA = 0.5
MESH = pl.DeviceIdType.MESH
Y_MEMBERS = (0, 2, 3, 5)
CHUNKS = ((0, 2), (2, 2), (4, 2))
SLOTS = 16


def slope_rows(value, low_row, high_row):
    rows = value.shape[0]
    at = lax.broadcasted_iota(jnp.int32, value.shape, 0)
    below = jnp.where(at == 0, low_row, pltpu.roll(value, 1, 0))
    above = jnp.where(at == rows - 1, high_row, pltpu.roll(value, rows - 1, 0))
    return 0.5 * (above - below)


def slope_lanes(value):
    lanes = value.shape[1]
    at = lax.broadcasted_iota(jnp.int32, value.shape, 1)
    below = jnp.where(at == 0, 0.0, pltpu.roll(value, 1, 1))
    above = jnp.where(at == lanes - 1, 0.0, pltpu.roll(value, lanes - 1, 1))
    return 0.5 * (above - below)


def updated(centre, slope_x, slope_y, curl_coef, half_step):
    slope_z = lambda member: slope_lanes(centre[member])
    curl_h = [slope_y(5) - slope_z(4), slope_z(3) - slope_x(5), slope_x(4) - slope_y(3)]
    curl_e = [slope_y(2) - slope_z(1), slope_z(0) - slope_x(2), slope_x(1) - slope_y(0)]
    return [centre[m] + curl_coef * curl_h[m] for m in range(3)] + [
        centre[3 + m] - half_step * curl_e[m] for m in range(3)
    ]


def factor(length, coef_at, gain_ref, pivot_ref, left_ref, right_ref):
    zero = jnp.zeros(gain_ref.shape[1:], jnp.float32)

    def forward(i, carry):
        gain_prev, left_prev = carry
        coef = coef_at(i)
        pivot = 1.0 / (1.0 + 2.0 * coef - coef * gain_prev)
        gain = coef * pivot
        left = gain * left_prev
        gain_ref[i] = gain
        pivot_ref[i] = pivot
        left_ref[i] = left
        return gain, left

    lax.fori_loop(0, length, forward, (zero, jnp.ones_like(zero)), unroll=2)

    def backward(k, carry):
        left_next, right_next = carry
        i = length - 1 - k
        gain = gain_ref[i]
        left = left_ref[i] + gain * left_next
        right = gain * right_next
        left_ref[i] = left
        right_ref[i] = right
        return left, right

    lax.fori_loop(0, length, backward, (zero, jnp.ones_like(zero)), unroll=4)


def sweep_back(length, gain_ref, solved_ref):
    def backward(k, carry):
        i = length - 1 - k
        gain = gain_ref[i]
        now = [solved_ref[m, i] + gain * carry[m] for m in range(6)]
        for m in range(6):
            solved_ref[m, i] = now[m]
        return tuple(now)

    zero = jnp.zeros(gain_ref.shape[1:], jnp.float32)
    lax.fori_loop(0, length, backward, (zero,) * 6, unroll=4)


class Line:
    def __init__(self, axis, count, refs):
        (self.mat_out, self.mat_in, self.rhs_out, self.rhs_in, self.plan, self.gains, self.ends,
         self.mat_sems, self.rhs_sems) = refs
        self.axis = axis
        self.count = count
        self.steps = count.bit_length() - 1
        self.me = lax.axis_index(axis)

    def near(self, k):
        return 1 - (self.me // 2**k) % 2

    def partner(self, k):
        return {self.axis: self.me + (2 * self.near(k) - 1) * 2**k}

    def mat_copy(self, k):
        return pltpu.make_async_remote_copy(
            self.mat_out.at[k], self.mat_in.at[k], self.mat_sems.at[0, k], self.mat_sems.at[1, k],
            device_id=self.partner(k), device_id_type=MESH)

    def rhs_copy(self, k, j):
        first, size = CHUNKS[j]
        if k == self.steps - 1:
            source = self.rhs_out.at[k, self.near(k), pl.ds(first, size)]
            target = self.rhs_in.at[k, 0, pl.ds(first, size)]
        else:
            source = self.rhs_out.at[k, :, pl.ds(first, size)]
            target = self.rhs_in.at[k, :, pl.ds(first, size)]
        return pltpu.make_async_remote_copy(
            source, target, self.rhs_sems.at[0, k, j], self.rhs_sems.at[1, k, j],
            device_id=self.partner(k), device_id_type=MESH)

    def mat_start(self, left_ref, right_ref):
        last = left_ref.shape[0] - 1
        for end, at in ((0, 0), (1, last)):
            self.mat_out[0, 2 * end] = left_ref[at]
            self.mat_out[0, 2 * end + 1] = right_ref[at]
        one, zero = jnp.ones(left_ref.shape[1:], jnp.float32), jnp.zeros(left_ref.shape[1:], jnp.float32)
        self.gains[0] = one
        self.gains[1] = zero
        self.gains[2] = zero
        self.gains[3] = one
        self.mat_copy(0).start()

    def mat_merge(self, k):
        self.mat_copy(k).wait_recv()
        n = self.near(k)
        f = 1 - n
        mine = lambda end, side: self.mat_out[k, 2 * end + side]
        other = lambda end, side: self.mat_in[k, 2 * end + side]
        m_nn, m_fn, m_nf, m_ff = mine(n, n), mine(f, n), mine(n, f), mine(f, f)
        o_nn, o_fn, o_nf, o_ff = other(f, f), other(n, f), other(f, n), other(n, n)
        inv = 1.0 / (1.0 - m_nn * o_nn)
        o_by_m = o_nn * m_nf * inv
        o_by_o = o_nf * inv
        m_by_m = m_nf * inv
        m_by_o = m_nn * o_nf * inv
        gain_in, gain_out = self.gains[n], self.gains[2 + n]
        for slot, value in enumerate((inv, o_nn * inv, m_nn * inv, m_fn, o_fn, gain_in, gain_out)):
            self.plan[k, slot] = value
        if k < self.steps - 1:
            self.mat_out[k + 1, 2 * f + f] = m_ff + m_fn * o_by_m
            self.mat_out[k + 1, 2 * f + n] = m_fn * o_by_o
            self.mat_out[k + 1, 2 * n + n] = o_ff + o_fn * m_by_o
            self.mat_out[k + 1, 2 * n + f] = o_fn * m_by_m
            self.mat_copy(k + 1).start()
            self.gains[f] = self.gains[f] + gain_in * o_by_m
            self.gains[2 + f] = self.gains[2 + f] + gain_out * o_by_m
            self.gains[n] = gain_in * o_by_o
            self.gains[2 + n] = gain_out * o_by_o

    def rhs_start(self, solved_ref):
        last = solved_ref.shape[1] - 1
        for j, (first, size) in enumerate(CHUNKS):
            for m in range(first, first + size):
                self.rhs_out[0, 0, m] = solved_ref[m, 0]
                self.rhs_out[0, 1, m] = solved_ref[m, last]
            self.rhs_copy(0, j).start()

    def rhs_merge(self, k, j):
        first, size = CHUNKS[j]
        self.rhs_copy(k, j).wait_recv()
        n = self.near(k)
        f = 1 - n
        ending = k == self.steps - 1
        inv, o_nn, m_nn, m_fn, o_fn, gain_in, gain_out = [self.plan[k, slot] for slot in range(7)]
        for m in range(first, first + size):
            mine = self.rhs_out[k, n, m]
            other = self.rhs_in[k, 0, m] if ending else self.rhs_in[k, f, m]
            o_value = other * inv + o_nn * mine
            if not ending:
                m_value = mine * inv + m_nn * other
                self.rhs_out[k + 1, f, m] = self.rhs_out[k, f, m] + m_fn * o_value
                self.rhs_out[k + 1, n, m] = self.rhs_in[k, n, m] + o_fn * m_value
            into, out_of = gain_in * o_value, gain_out * o_value
            if k > 0:
                into, out_of = self.ends[0, m] + into, self.ends[1, m] + out_of
            self.ends[0, m] = into
            self.ends[1, m] = out_of
        if not ending:
            self.rhs_copy(k + 1, j).start()

    def drain(self):
        for k in range(self.steps):
            self.mat_copy(k).wait_send()
            for j in range(len(CHUNKS)):
                self.rhs_copy(k, j).wait_send()


def both_ways(axis, count, out_low, out_high, in_low, in_high, sems):
    me = lax.axis_index(axis)
    up = lambda: pltpu.make_async_remote_copy(
        out_high, in_low, sems.at[0], sems.at[1], device_id={axis: me + 1}, device_id_type=MESH)
    down = lambda: pltpu.make_async_remote_copy(
        out_low, in_high, sems.at[2], sems.at[3], device_id={axis: me - 1}, device_id_type=MESH)

    def start():
        @pl.when(me < count - 1)
        def _():
            up().start()

        @pl.when(me > 0)
        def _():
            down().start()

        @pl.when(me == 0)
        def _():
            in_low[...] = jnp.zeros(in_low.shape, jnp.float32)

        @pl.when(me == count - 1)
        def _():
            in_high[...] = jnp.zeros(in_high.shape, jnp.float32)

    def wait():
        @pl.when(me > 0)
        def _():
            up().wait_recv()

        @pl.when(me < count - 1)
        def _():
            down().wait_recv()

    def drain():
        @pl.when(me < count - 1)
        def _():
            up().wait_send()

        @pl.when(me > 0)
        def _():
            down().wait_send()

    return start, wait, drain


def greet_all(count, ny, me, barrier):
    def hello(k, carry):
        to = (me + k) % count
        pl.semaphore_signal(barrier, inc=1, device_id=(to // ny, to % ny), device_id_type=MESH)
        return carry

    lax.fori_loop(1, count, hello, 0)


def cos_sin(angle):
    turns = jnp.floor(angle * (2.0 / math.pi) + 0.5)
    rest = ((angle - turns * 1.5703125) - turns * 4.837512969970703125e-4) - turns * 7.54978995489188216e-8
    square = rest * rest
    sine = ((-1.9515295891e-4 * square + 8.3321608736e-3) * square - 1.6666654611e-1) * square * rest + rest
    cosine = (
        (2.443315711809948e-5 * square - 1.388731625493765e-3) * square + 4.166664568298827e-2
    ) * square * square - 0.5 * square + 1.0
    quarter = turns.astype(jnp.int32) & 3
    swap = (quarter & 1) == 1
    plain_cos = jnp.where(swap, sine, cosine)
    plain_sin = jnp.where(swap, cosine, sine)
    minus_cos = (quarter == 1) | (quarter == 2)
    return jnp.where(minus_cos, -plain_cos, plain_cos), jnp.where(quarter >= 2, -plain_sin, plain_sin)


def split_bf16(value):
    high = value.astype(jnp.bfloat16)
    return high, (value - high.astype(jnp.float32)).astype(jnp.bfloat16)


def dot_rows(left, right):
    return lax.dot_general(left, right, (((1,), (1,)), ((), ())), preferred_element_type=jnp.float32)


def slot_ranks(count, owner):
    patches = owner.shape[1]
    hot = lax.broadcasted_iota(jnp.int32, (count, patches), 0) == owner
    before = lax.broadcasted_iota(jnp.int32, (patches, patches), 0) < lax.broadcasted_iota(
        jnp.int32, (patches, patches), 1)
    as_bf16 = lambda mask: jnp.where(mask, 1.0, 0.0).astype(jnp.bfloat16)
    ahead = lax.dot_general(as_bf16(hot), as_bf16(before), (((1,), (0,)), ((), ())),
                            preferred_element_type=jnp.float32)
    rank = jnp.sum(jnp.where(hot, ahead, 0.0), axis=0, keepdims=True)
    return as_bf16(hot), rank.astype(jnp.int32)


def by_owner(hot, rank, values):
    slots = lax.broadcasted_iota(jnp.int32, (SLOTS, rank.shape[1]), 0) == rank
    rows = [jnp.where(slots, value, 0.0) for value in values]
    rows += [jnp.zeros_like(rows[0])] * (8 - len(rows))
    high, low = split_bf16(jnp.concatenate(rows, axis=0))
    both = dot_rows(hot, jnp.concatenate([high, low], axis=0))
    return both[:, :8 * SLOTS] + both[:, 8 * SLOTS:]


def fields_on_rows(landed_ref):
    count, _, lanes = landed_ref.shape
    row = lax.broadcasted_iota(jnp.int32, (8, lanes), 0)
    block = lax.shift_right_logical(
        lax.broadcasted_iota(jnp.int32, (8, lanes), 1), jnp.full((8, lanes), SLOTS.bit_length() - 1, jnp.int32))
    groups = []
    for g in range(count // 8):
        value = jnp.concatenate([landed_ref[g * 8 + i] for i in range(8)], axis=0)
        for bit in (1, 2, 4):
            later = pltpu.roll(pltpu.roll(value, 8 - bit, 0), SLOTS * bit, 1)
            sooner = pltpu.roll(pltpu.roll(value, bit, 0), lanes - SLOTS * bit, 1)
            row_bit, block_bit = row & bit, block & bit
            value = jnp.where(row_bit == block_bit, value, jnp.where(row_bit == 0, later, sooner))
        groups.append(value)
    return jnp.concatenate(groups, axis=1)


def fill_weights(count, me, places, high_ref, low_ref):
    angles = high_ref.shape[0] // 2
    slots = places.shape[1]
    azimuth = jnp.full((16, 128), me.astype(jnp.float32) * (2.0 * math.pi / count))
    cos_phi, sin_phi = cos_sin(azimuth)
    pos = [jnp.broadcast_to(places[c:c + 1], (16, slots)) for c in range(3)]

    def group(g, carry):
        start = pl.multiple_of(g * 16, 16)
        index = (lax.broadcasted_iota(jnp.int32, (16, 128), 0) + start).astype(jnp.float32)
        cos_theta, sin_theta = cos_sin(math.pi * (index + 0.5) / angles)
        for part in range(0, slots, 128):
            at = slice(part, part + 128)
            phase = KAPPA * (pos[0][:, at] * sin_theta * cos_phi + pos[1][:, at] * sin_theta * sin_phi
                             + pos[2][:, at] * cos_theta)
            for s, value in enumerate(cos_sin(phase)):
                high, low = split_bf16(value)
                rows = pl.ds(pl.multiple_of(start + s * angles, 16), 16)
                high_ref[rows, at] = high
                low_ref[rows, at] = low
        return carry

    lax.fori_loop(0, angles // 16, group, 0)


def to_owners(count, ny, me, out_ref, landed_ref, sems):
    def copy(k):
        to = (me + k) % count
        return pltpu.make_async_remote_copy(
            out_ref.at[to], landed_ref.at[me], sems.at[0, k], sems.at[1, k],
            device_id=(to // ny, to % ny), device_id_type=MESH)

    def loop(act):
        def step(k, carry):
            act(copy(k))
            return carry

        lax.fori_loop(1, count, step, 0)

    def start(rows):
        for i in range(count):
            out_ref[i] = rows[i:i + 1]
        landed_ref[me] = out_ref[me]
        loop(lambda one: one.start())

    return start, lambda: loop(lambda one: one.wait_recv()), lambda: loop(lambda one: one.wait_send())


def step_kernel(nx, ny, cx, cy, cz, scale, fields_hbm, material_hbm, permit_ref, cell_smem,
                cell_row, owner_row, out_ref, far_ref, material_ref,
                grid_x, grid_y, y_out, y_low, y_high, coef_x,
                gain_x, pivot_x, left_x, right_x, solved_x,
                coef_y, gain_y, pivot_y, left_y, right_y, solved_y,
                weight_high, weight_low, place_out, place_in, value_out, value_in,
                load_sem, move_sem, halo_sems, place_sems, value_sems, *line_refs):
    half_step = COURANT / 2.0
    count = nx * ny
    me = lax.axis_index("gx") * ny + lax.axis_index("gy")
    barrier = pltpu.get_barrier_semaphore()
    load = pltpu.make_async_copy(fields_hbm, grid_x.at[:, pl.ds(1, cx)], load_sem)
    load.start()
    load_material = pltpu.make_async_copy(material_hbm, material_ref, move_sem)
    load_material.start()
    greet_all(count, ny, me, barrier)
    line_x = Line("gx", nx, line_refs[:9])
    line_y = Line("gy", ny, line_refs[9:])

    x_halo = both_ways("gx", nx, grid_x.at[pl.ds(1, 5), 1], grid_x.at[pl.ds(1, 5), cx],
                       grid_x.at[pl.ds(1, 5), 0], grid_x.at[pl.ds(1, 5), cx + 1], halo_sems.at[0])
    y_halo = both_ways("gy", ny, y_out.at[0], y_out.at[1], y_low, y_high, halo_sems.at[1])
    mid_halo = both_ways("gy", ny, grid_y.at[:, pl.ds(cx, cx)], grid_y.at[:, pl.ds(cx * cy, cx)],
                         grid_y.at[:, pl.ds(0, cx)], grid_y.at[:, pl.ds(cx * (cy + 1), cx)],
                         halo_sems.at[2])

    def coefs(i, carry):
        which = material_ref[i]
        permit = jnp.zeros(which.shape, jnp.float32)
        for entry in range(permit_ref.shape[0]):
            permit = jnp.where(which == entry, permit_ref[entry], permit)
        coef_x[pl.ds(pl.multiple_of(i * cy, 8), cy), :] = (half_step * half_step) / permit
        return carry

    load_material.wait()
    lax.fori_loop(0, cx, coefs, 0, unroll=2)
    load.wait()
    for slot, member in enumerate(Y_MEMBERS):
        y_out[0, slot] = jnp.concatenate([grid_x[member, 1 + i, 0:1] for i in range(cx)], axis=0)
        y_out[1, slot] = jnp.concatenate([grid_x[member, 1 + i, cy - 1:cy] for i in range(cx)], axis=0)
    pl.semaphore_wait(barrier, count - 1)
    x_halo[0]()
    y_halo[0]()
    coef_plane = lambda i: coef_x[pl.ds(pl.multiple_of(i * cy, 8), cy), :]
    factor(cx, coef_plane, gain_x, pivot_x, left_x, right_x)
    line_x.mat_start(left_x, right_x)
    for j in range(cy):
        coef_y[j] = coef_x[pl.ds(j, cx, stride=cy), :]
    patches = cell_smem.shape[0]
    cell = cell_row[...]
    line = lax.shift_right_logical(cell, jnp.full_like(cell, cz.bit_length() - 1))
    at_x = jnp.zeros_like(cell)
    for i in range(1, cx):
        at_x = at_x + jnp.where(line >= i * cy, 1, 0)
    places = [at_x + lax.axis_index("gx") * cx, line - at_x * cy + lax.axis_index("gy") * cy, cell - line * cz]
    hot, rank = slot_ranks(count, owner_row[...])
    place_send = to_owners(count, ny, me, place_out, place_in, place_sems)
    value_send = to_owners(count, ny, me, value_out, value_in, value_sems)
    place_send[0](by_owner(hot, rank, [place.astype(jnp.float32) for place in places]))
    factor(cy, lambda j: coef_y[j], gain_y, pivot_y, left_y, right_y)
    line_y.mat_start(left_y, right_y)
    x_halo[1]()
    y_halo[1]()
    y_slot = {member: slot for slot, member in enumerate(Y_MEMBERS)}

    def forward_x(i, carry):
        centre = [grid_x[m, i + 1] for m in range(6)]
        slope_x = lambda m: 0.5 * (grid_x[m, i + 2] - grid_x[m, i])
        slope_y = lambda m: slope_rows(
            centre[m], y_low[y_slot[m], pl.ds(i, 1), :], y_high[y_slot[m], pl.ds(i, 1), :])
        right = updated(centre, slope_x, slope_y, coef_plane(i) * (1.0 / half_step), half_step)
        gain, pivot = gain_x[i], pivot_x[i]
        now = [right[m] * pivot + gain * carry[m] for m in range(6)]
        for m in range(6):
            solved_x[m, i] = now[m]
        return tuple(now)

    lax.fori_loop(0, cx, forward_x, (jnp.zeros((cy, cz), jnp.float32),) * 6, unroll=2)
    early = min(2, line_x.steps)
    line_x.mat_merge(0)
    sweep_back(cx, gain_x, solved_x)
    line_x.rhs_start(solved_x)
    if early > 1:
        line_x.mat_merge(1)
    place_send[1]()
    fill_weights(count, me, fields_on_rows(place_in), weight_high, weight_low)
    for k in range(line_x.steps):
        if k >= early:
            line_x.mat_merge(k)
        for j in range(len(CHUNKS)):
            line_x.rhs_merge(k, j)
        if k < line_y.steps:
            line_y.mat_merge(k)
    for k in range(line_x.steps, line_y.steps):
        line_y.mat_merge(k)

    for i in range(cx):
        left, right = left_x[i], right_x[i]
        for m in range(6):
            grid_y[m, pl.ds(cx + i, cy, stride=cx), :] = (
                solved_x[m, i] + left * line_x.ends[0, m] + right * line_x.ends[1, m])
    mid_halo[0]()
    mid_halo[1]()

    y_plane = lambda m, j: grid_y[m, pl.ds(pl.multiple_of(j * cx, 8), cx), :]

    def forward_y(j, carry):
        centre = [y_plane(m, j + 1) for m in range(6)]
        slope_y = lambda m: 0.5 * (y_plane(m, j + 2) - y_plane(m, j))
        slope_x = lambda m: slope_rows(
            centre[m], line_x.ends[0, m, pl.ds(j, 1), :], line_x.ends[1, m, pl.ds(j, 1), :])
        right = updated(centre, slope_x, slope_y, coef_y[j] * (1.0 / half_step), half_step)
        gain, pivot = gain_y[j], pivot_y[j]
        now = [right[m] * pivot + gain * carry[m] for m in range(6)]
        for m in range(6):
            solved_y[m, j] = now[m]
        return tuple(now)

    lax.fori_loop(0, cy, forward_y, (jnp.zeros((cx, cz), jnp.float32),) * 6, unroll=2)
    sweep_back(cy, gain_y, solved_y)
    line_y.rhs_start(solved_y)
    for k in range(line_y.steps):
        for j in range(len(CHUNKS)):
            line_y.rhs_merge(k, j)
    for j in range(cy):
        left, right = left_y[j], right_y[j]
        for m in range(6):
            value = solved_y[m, j] + left * line_y.ends[0, m] + right * line_y.ends[1, m]
            out_ref[pl.ds(m * cx * cy + j, cx, stride=cy), :] = value

    lane = lax.broadcasted_iota(jnp.int32, (6, cz), 1)
    found = []
    for first in range(0, patches, cz):
        def fetch(q, kept):
            for u in range(16):
                at = q * 16 + u
                cell = cell_smem[first + at]
                line = cell // cz
                rows = out_ref[pl.ds(line, 6, stride=cx * cy), :]
                kept = jnp.where(lane == at, pltpu.roll(rows, (at - cell) & (cz - 1), 1), kept)
            return kept

        found.append(lax.fori_loop(0, cz // 16, fetch, jnp.zeros((6, cz), jnp.float32)))
    values = jnp.concatenate(found, axis=1)
    value_send[0](by_owner(hot, rank, [values[m:m + 1] for m in range(6)]))
    for halo in (x_halo, y_halo, mid_halo):
        halo[2]()
    line_x.drain()
    line_y.drain()
    place_send[2]()
    value_send[1]()
    high, low = split_bf16(fields_on_rows(value_in))
    both = jnp.concatenate([high, low], axis=0)
    product = dot_rows(both, weight_high[...]) + dot_rows(both, weight_low[...])
    product = (product[:8] + product[8:]) * scale
    angles = far_ref.shape[1]
    for s in range(2):
        far_ref[pl.ds(s * 6, 6), :] = product[:6, s * angles:(s + 1) * angles]
    value_send[2]()


def line_scratch(count, rows, lanes):
    steps = count.bit_length() - 1
    f32 = jnp.float32
    return [
        pltpu.VMEM((steps, 4, rows, lanes), f32),
        pltpu.VMEM((steps, 4, rows, lanes), f32),
        pltpu.VMEM((steps, 2, 6, rows, lanes), f32),
        pltpu.VMEM((steps, 2, 6, rows, lanes), f32),
        pltpu.VMEM((steps, 7, rows, lanes), f32),
        pltpu.VMEM((4, rows, lanes), f32),
        pltpu.VMEM((2, 6, rows, lanes), f32),
        pltpu.SemaphoreType.DMA((2, steps)),
        pltpu.SemaphoreType.DMA((2, steps, len(CHUNKS))),
    ]


def local(nx, ny, fields, material, permittivity, patch_cell, patch_owner):
    _, cx, cy, cz = fields.shape
    f32 = jnp.float32
    count = nx * ny
    patches = patch_cell.shape[0]
    vmem = pl.BlockSpec(memory_space=pltpu.VMEM)
    smem = pl.BlockSpec(memory_space=pltpu.SMEM)
    hbm = pl.BlockSpec(memory_space=pltpu.HBM)
    x_lines = [pltpu.VMEM((cx, cy, cz), f32)] * 4
    y_lines = [pltpu.VMEM((cy, cx, cz), f32)] * 4
    new_flat, far_field = pl.pallas_call(
        functools.partial(step_kernel, nx, ny, cx, cy, cz, 1.0 / math.sqrt(patches)),
        out_shape=(
            jax.ShapeDtypeStruct((6 * cx * cy, cz), f32),
            jax.ShapeDtypeStruct((12, ANG_DEV), f32),
        ),
        in_specs=[hbm, hbm, smem, smem, vmem, vmem],
        out_specs=(vmem, vmem),
        scratch_shapes=[
            pltpu.VMEM((cx, cy, cz), jnp.int32),
            pltpu.VMEM((6, cx + 2, cy, cz), f32),
            pltpu.VMEM((6, (cy + 2) * cx, cz), f32),
            pltpu.VMEM((2, 4, cx, cz), f32),
            pltpu.VMEM((4, cx, cz), f32),
            pltpu.VMEM((4, cx, cz), f32),
            pltpu.VMEM((cx * cy, cz), f32),
            *x_lines,
            pltpu.VMEM((6, cx, cy, cz), f32),
            pltpu.VMEM((cy, cx, cz), f32),
            *y_lines,
            pltpu.VMEM((6, cy, cx, cz), f32),
            pltpu.VMEM((2 * ANG_DEV, SLOTS * count), jnp.bfloat16),
            pltpu.VMEM((2 * ANG_DEV, SLOTS * count), jnp.bfloat16),
            *[pltpu.VMEM((count, 1, 8 * SLOTS), f32)] * 4,
            pltpu.SemaphoreType.DMA,
            pltpu.SemaphoreType.DMA,
            pltpu.SemaphoreType.DMA((3, 4)),
            pltpu.SemaphoreType.DMA((2, count)),
            pltpu.SemaphoreType.DMA((2, count)),
            *line_scratch(nx, cy, cz),
            *line_scratch(ny, cx, cz),
        ],
        compiler_params=pltpu.CompilerParams(
            collective_id=0, has_side_effects=True, vmem_limit_bytes=40 * 2**20),
        name="split_step",
    )(fields, material, permittivity, patch_cell, patch_cell[None, :], patch_owner.reshape(1, patches))
    return new_flat.reshape(fields.shape), far_field


def solution(mesh):
    return jax.shard_map(
        functools.partial(local, mesh.shape["gx"], mesh.shape["gy"]),
        mesh=mesh,
        in_specs=(
            P(None, "gx", "gy", None),
            P("gx", "gy", None),
            P(),
            P(("gx", "gy")),
            P(("gx", "gy"), None),
        ),
        out_specs=(P(None, "gx", "gy", None), P(None, ("gx", "gy"))),
        check_vma=False,
    )
```

```python
import functools
import math

import jax
import jax.numpy as jnp
from jax import lax
from jax.experimental import pallas as pl
from jax.experimental.pallas import tpu as pltpu
from jax.sharding import PartitionSpec as P

ANG_DEV = 128
COURANT = 64
KAPPA = 0.5
MESH = pl.DeviceIdType.MESH
Y_MEMBERS = (0, 2, 3, 5)
CHUNKS = ((0, 2), (2, 2), (4, 2))
SLOTS = 16


def slope_rows(value, low_row, high_row):
    rows = value.shape[0]
    at = lax.broadcasted_iota(jnp.int32, value.shape, 0)
    below = jnp.where(at == 0, low_row, pltpu.roll(value, 1, 0))
    above = jnp.where(at == rows - 1, high_row, pltpu.roll(value, rows - 1, 0))
    return 0.5 * (above - below)


def slope_lanes(value):
    lanes = value.shape[1]
    at = lax.broadcasted_iota(jnp.int32, value.shape, 1)
    below = jnp.where(at == 0, 0.0, pltpu.roll(value, 1, 1))
    above = jnp.where(at == lanes - 1, 0.0, pltpu.roll(value, lanes - 1, 1))
    return 0.5 * (above - below)


def updated(centre, slope_x, slope_y, curl_coef, half_step):
    slope_z = lambda member: slope_lanes(centre[member])
    curl_h = [slope_y(5) - slope_z(4), slope_z(3) - slope_x(5), slope_x(4) - slope_y(3)]
    curl_e = [slope_y(2) - slope_z(1), slope_z(0) - slope_x(2), slope_x(1) - slope_y(0)]
    return [centre[m] + curl_coef * curl_h[m] for m in range(3)] + [
        centre[3 + m] - half_step * curl_e[m] for m in range(3)
    ]


def factor(length, coef_at, gain_ref, pivot_ref, left_ref, right_ref):
    zero = jnp.zeros(gain_ref.shape[1:], jnp.float32)

    def forward(i, carry):
        gain_prev, left_prev = carry
        coef = coef_at(i)
        pivot = 1.0 / (1.0 + 2.0 * coef - coef * gain_prev)
        gain = coef * pivot
        left = gain * left_prev
        gain_ref[i] = gain
        pivot_ref[i] = pivot
        left_ref[i] = left
        return gain, left

    lax.fori_loop(0, length, forward, (zero, jnp.ones_like(zero)), unroll=2)

    def backward(k, carry):
        left_next, right_next = carry
        i = length - 1 - k
        gain = gain_ref[i]
        left = left_ref[i] + gain * left_next
        right = gain * right_next
        left_ref[i] = left
        right_ref[i] = right
        return left, right

    lax.fori_loop(0, length, backward, (zero, jnp.ones_like(zero)), unroll=4)


def sweep_back(length, gain_ref, solved_ref):
    def backward(k, carry):
        i = length - 1 - k
        gain = gain_ref[i]
        now = [solved_ref[m, i] + gain * carry[m] for m in range(6)]
        for m in range(6):
            solved_ref[m, i] = now[m]
        return tuple(now)

    zero = jnp.zeros(gain_ref.shape[1:], jnp.float32)
    lax.fori_loop(0, length, backward, (zero,) * 6, unroll=4)


class Line:
    def __init__(self, axis, count, refs):
        (self.mat_out, self.mat_in, self.rhs_out, self.rhs_in, self.plan, self.gains, self.ends,
         self.mat_sems, self.rhs_sems) = refs
        self.axis = axis
        self.count = count
        self.steps = count.bit_length() - 1
        self.me = lax.axis_index(axis)

    def near(self, k):
        return 1 - (self.me // 2**k) % 2

    def partner(self, k):
        return {self.axis: self.me + (2 * self.near(k) - 1) * 2**k}

    def mat_copy(self, k):
        return pltpu.make_async_remote_copy(
            self.mat_out.at[k], self.mat_in.at[k], self.mat_sems.at[0, k], self.mat_sems.at[1, k],
            device_id=self.partner(k), device_id_type=MESH)

    def rhs_copy(self, k, j):
        first, size = CHUNKS[j]
        if k == self.steps - 1:
            source = self.rhs_out.at[k, self.near(k), pl.ds(first, size)]
            target = self.rhs_in.at[k, 0, pl.ds(first, size)]
        else:
            source = self.rhs_out.at[k, :, pl.ds(first, size)]
            target = self.rhs_in.at[k, :, pl.ds(first, size)]
        return pltpu.make_async_remote_copy(
            source, target, self.rhs_sems.at[0, k, j], self.rhs_sems.at[1, k, j],
            device_id=self.partner(k), device_id_type=MESH)

    def mat_start(self, left_ref, right_ref):
        last = left_ref.shape[0] - 1
        for end, at in ((0, 0), (1, last)):
            self.mat_out[0, 2 * end] = left_ref[at]
            self.mat_out[0, 2 * end + 1] = right_ref[at]
        one, zero = jnp.ones(left_ref.shape[1:], jnp.float32), jnp.zeros(left_ref.shape[1:], jnp.float32)
        self.gains[0] = one
        self.gains[1] = zero
        self.gains[2] = zero
        self.gains[3] = one
        self.mat_copy(0).start()

    def mat_merge(self, k):
        self.mat_copy(k).wait_recv()
        n = self.near(k)
        f = 1 - n
        mine = lambda end, side: self.mat_out[k, 2 * end + side]
        other = lambda end, side: self.mat_in[k, 2 * end + side]
        m_nn, m_fn, m_nf, m_ff = mine(n, n), mine(f, n), mine(n, f), mine(f, f)
        o_nn, o_fn, o_nf, o_ff = other(f, f), other(n, f), other(f, n), other(n, n)
        inv = 1.0 / (1.0 - m_nn * o_nn)
        o_by_m = o_nn * m_nf * inv
        o_by_o = o_nf * inv
        m_by_m = m_nf * inv
        m_by_o = m_nn * o_nf * inv
        gain_in, gain_out = self.gains[n], self.gains[2 + n]
        for slot, value in enumerate((inv, o_nn * inv, m_nn * inv, m_fn, o_fn, gain_in, gain_out)):
            self.plan[k, slot] = value
        if k < self.steps - 1:
            self.mat_out[k + 1, 2 * f + f] = m_ff + m_fn * o_by_m
            self.mat_out[k + 1, 2 * f + n] = m_fn * o_by_o
            self.mat_out[k + 1, 2 * n + n] = o_ff + o_fn * m_by_o
            self.mat_out[k + 1, 2 * n + f] = o_fn * m_by_m
            self.mat_copy(k + 1).start()
            self.gains[f] = self.gains[f] + gain_in * o_by_m
            self.gains[2 + f] = self.gains[2 + f] + gain_out * o_by_m
            self.gains[n] = gain_in * o_by_o
            self.gains[2 + n] = gain_out * o_by_o

    def rhs_start(self, solved_ref):
        last = solved_ref.shape[1] - 1
        for j, (first, size) in enumerate(CHUNKS):
            for m in range(first, first + size):
                self.rhs_out[0, 0, m] = solved_ref[m, 0]
                self.rhs_out[0, 1, m] = solved_ref[m, last]
            self.rhs_copy(0, j).start()

    def rhs_merge(self, k, j):
        first, size = CHUNKS[j]
        self.rhs_copy(k, j).wait_recv()
        n = self.near(k)
        f = 1 - n
        ending = k == self.steps - 1
        inv, o_nn, m_nn, m_fn, o_fn, gain_in, gain_out = [self.plan[k, slot] for slot in range(7)]
        for m in range(first, first + size):
            mine = self.rhs_out[k, n, m]
            other = self.rhs_in[k, 0, m] if ending else self.rhs_in[k, f, m]
            o_value = other * inv + o_nn * mine
            if not ending:
                m_value = mine * inv + m_nn * other
                self.rhs_out[k + 1, f, m] = self.rhs_out[k, f, m] + m_fn * o_value
                self.rhs_out[k + 1, n, m] = self.rhs_in[k, n, m] + o_fn * m_value
            into, out_of = gain_in * o_value, gain_out * o_value
            if k > 0:
                into, out_of = self.ends[0, m] + into, self.ends[1, m] + out_of
            self.ends[0, m] = into
            self.ends[1, m] = out_of
        if not ending:
            self.rhs_copy(k + 1, j).start()

    def drain(self):
        for k in range(self.steps):
            self.mat_copy(k).wait_send()
            for j in range(len(CHUNKS)):
                self.rhs_copy(k, j).wait_send()


def both_ways(axis, count, out_low, out_high, in_low, in_high, sems):
    me = lax.axis_index(axis)
    up = lambda: pltpu.make_async_remote_copy(
        out_high, in_low, sems.at[0], sems.at[1], device_id={axis: me + 1}, device_id_type=MESH)
    down = lambda: pltpu.make_async_remote_copy(
        out_low, in_high, sems.at[2], sems.at[3], device_id={axis: me - 1}, device_id_type=MESH)

    def start():
        @pl.when(me < count - 1)
        def _():
            up().start()

        @pl.when(me > 0)
        def _():
            down().start()

        @pl.when(me == 0)
        def _():
            in_low[...] = jnp.zeros(in_low.shape, jnp.float32)

        @pl.when(me == count - 1)
        def _():
            in_high[...] = jnp.zeros(in_high.shape, jnp.float32)

    def wait():
        @pl.when(me > 0)
        def _():
            up().wait_recv()

        @pl.when(me < count - 1)
        def _():
            down().wait_recv()

    def drain():
        @pl.when(me < count - 1)
        def _():
            up().wait_send()

        @pl.when(me > 0)
        def _():
            down().wait_send()

    return start, wait, drain


def greet_all(count, ny, me, barrier):
    def hello(k, carry):
        to = (me + k) % count
        pl.semaphore_signal(barrier, inc=1, device_id=(to // ny, to % ny), device_id_type=MESH)
        return carry

    lax.fori_loop(1, count, hello, 0)


def cos_sin(angle):
    turns = jnp.floor(angle * (2.0 / math.pi) + 0.5)
    rest = ((angle - turns * 1.5703125) - turns * 4.837512969970703125e-4) - turns * 7.54978995489188216e-8
    square = rest * rest
    sine = ((-1.9515295891e-4 * square + 8.3321608736e-3) * square - 1.6666654611e-1) * square * rest + rest
    cosine = (
        (2.443315711809948e-5 * square - 1.388731625493765e-3) * square + 4.166664568298827e-2
    ) * square * square - 0.5 * square + 1.0
    quarter = turns.astype(jnp.int32) & 3
    swap = (quarter & 1) == 1
    plain_cos = jnp.where(swap, sine, cosine)
    plain_sin = jnp.where(swap, cosine, sine)
    minus_cos = (quarter == 1) | (quarter == 2)
    return jnp.where(minus_cos, -plain_cos, plain_cos), jnp.where(quarter >= 2, -plain_sin, plain_sin)


def split_bf16(value):
    high = value.astype(jnp.bfloat16)
    return high, (value - high.astype(jnp.float32)).astype(jnp.bfloat16)


def dot_rows(left, right):
    return lax.dot_general(left, right, (((1,), (1,)), ((), ())), preferred_element_type=jnp.float32)


def slot_ranks(count, owner):
    patches = owner.shape[1]
    hot = lax.broadcasted_iota(jnp.int32, (count, patches), 0) == owner
    before = lax.broadcasted_iota(jnp.int32, (patches, patches), 0) < lax.broadcasted_iota(
        jnp.int32, (patches, patches), 1)
    as_bf16 = lambda mask: jnp.where(mask, 1.0, 0.0).astype(jnp.bfloat16)
    ahead = lax.dot_general(as_bf16(hot), as_bf16(before), (((1,), (0,)), ((), ())),
                            preferred_element_type=jnp.float32)
    rank = jnp.sum(jnp.where(hot, ahead, 0.0), axis=0, keepdims=True)
    return as_bf16(hot), rank.astype(jnp.int32)


def by_owner(hot, rank, values):
    slots = lax.broadcasted_iota(jnp.int32, (SLOTS, rank.shape[1]), 0) == rank
    rows = [jnp.where(slots, value, 0.0) for value in values]
    rows += [jnp.zeros_like(rows[0])] * (8 - len(rows))
    high, low = split_bf16(jnp.concatenate(rows, axis=0))
    both = dot_rows(hot, jnp.concatenate([high, low], axis=0))
    return both[:, :8 * SLOTS] + both[:, 8 * SLOTS:]


def fields_on_rows(landed_ref):
    count, _, lanes = landed_ref.shape
    row = lax.broadcasted_iota(jnp.int32, (8, lanes), 0)
    block = lax.shift_right_logical(
        lax.broadcasted_iota(jnp.int32, (8, lanes), 1), jnp.full((8, lanes), SLOTS.bit_length() - 1, jnp.int32))
    groups = []
    for g in range(count // 8):
        value = jnp.concatenate([landed_ref[g * 8 + i] for i in range(8)], axis=0)
        for bit in (1, 2, 4):
            later = pltpu.roll(pltpu.roll(value, 8 - bit, 0), SLOTS * bit, 1)
            sooner = pltpu.roll(pltpu.roll(value, bit, 0), lanes - SLOTS * bit, 1)
            row_bit, block_bit = row & bit, block & bit
            value = jnp.where(row_bit == block_bit, value, jnp.where(row_bit == 0, later, sooner))
        groups.append(value)
    return jnp.concatenate(groups, axis=1)


def fill_weights(count, me, places, high_ref, low_ref):
    angles = high_ref.shape[0] // 2
    slots = places.shape[1]
    azimuth = jnp.full((16, 128), me.astype(jnp.float32) * (2.0 * math.pi / count))
    cos_phi, sin_phi = cos_sin(azimuth)
    pos = [jnp.broadcast_to(places[c:c + 1], (16, slots)) for c in range(3)]

    def group(g, carry):
        start = pl.multiple_of(g * 16, 16)
        index = (lax.broadcasted_iota(jnp.int32, (16, 128), 0) + start).astype(jnp.float32)
        cos_theta, sin_theta = cos_sin(math.pi * (index + 0.5) / angles)
        for part in range(0, slots, 128):
            at = slice(part, part + 128)
            phase = KAPPA * (pos[0][:, at] * sin_theta * cos_phi + pos[1][:, at] * sin_theta * sin_phi
                             + pos[2][:, at] * cos_theta)
            for s, value in enumerate(cos_sin(phase)):
                high, low = split_bf16(value)
                rows = pl.ds(pl.multiple_of(start + s * angles, 16), 16)
                high_ref[rows, at] = high
                low_ref[rows, at] = low
        return carry

    lax.fori_loop(0, angles // 16, group, 0)


def to_owners(count, ny, me, out_ref, landed_ref, sems):
    def copy(k):
        to = (me + k) % count
        return pltpu.make_async_remote_copy(
            out_ref.at[to], landed_ref.at[me], sems.at[0, k], sems.at[1, k],
            device_id=(to // ny, to % ny), device_id_type=MESH)

    def loop(act):
        def step(k, carry):
            act(copy(k))
            return carry

        lax.fori_loop(1, count, step, 0)

    def start(rows):
        for i in range(count):
            out_ref[i] = rows[i:i + 1]
        landed_ref[me] = out_ref[me]
        loop(lambda one: one.start())

    return start, lambda: loop(lambda one: one.wait_recv()), lambda: loop(lambda one: one.wait_send())


def step_kernel(nx, ny, cx, cy, cz, scale, fields_hbm, material_hbm, permit_ref, cell_smem,
                cell_row, owner_row, out_ref, far_ref, material_ref,
                grid_x, grid_y, y_out, y_low, y_high, coef_x,
                gain_x, pivot_x, left_x, right_x, solved_x,
                coef_y, gain_y, pivot_y, left_y, right_y, solved_y,
                weight_high, weight_low, place_out, place_in, value_out, value_in,
                load_sem, move_sem, halo_sems, place_sems, value_sems, *line_refs):
    half_step = COURANT / 2.0
    count = nx * ny
    me = lax.axis_index("gx") * ny + lax.axis_index("gy")
    barrier = pltpu.get_barrier_semaphore()
    load = pltpu.make_async_copy(fields_hbm, grid_x.at[:, pl.ds(1, cx)], load_sem)
    load.start()
    load_material = pltpu.make_async_copy(material_hbm, material_ref, move_sem)
    load_material.start()
    greet_all(count, ny, me, barrier)
    line_x = Line("gx", nx, line_refs[:9])
    line_y = Line("gy", ny, line_refs[9:])

    x_halo = both_ways("gx", nx, grid_x.at[pl.ds(1, 5), 1], grid_x.at[pl.ds(1, 5), cx],
                       grid_x.at[pl.ds(1, 5), 0], grid_x.at[pl.ds(1, 5), cx + 1], halo_sems.at[0])
    y_halo = both_ways("gy", ny, y_out.at[0], y_out.at[1], y_low, y_high, halo_sems.at[1])
    mid_halo = both_ways("gy", ny, grid_y.at[:, pl.ds(cx, cx)], grid_y.at[:, pl.ds(cx * cy, cx)],
                         grid_y.at[:, pl.ds(0, cx)], grid_y.at[:, pl.ds(cx * (cy + 1), cx)],
                         halo_sems.at[2])

    def coefs(i, carry):
        which = material_ref[i]
        permit = jnp.zeros(which.shape, jnp.float32)
        for entry in range(permit_ref.shape[0]):
            permit = jnp.where(which == entry, permit_ref[entry], permit)
        coef_x[pl.ds(pl.multiple_of(i * cy, 8), cy), :] = (half_step * half_step) / permit
        return carry

    load_material.wait()
    lax.fori_loop(0, cx, coefs, 0, unroll=2)
    load.wait()
    for slot, member in enumerate(Y_MEMBERS):
        y_out[0, slot] = jnp.concatenate([grid_x[member, 1 + i, 0:1] for i in range(cx)], axis=0)
        y_out[1, slot] = jnp.concatenate([grid_x[member, 1 + i, cy - 1:cy] for i in range(cx)], axis=0)
    pl.semaphore_wait(barrier, count - 1)
    x_halo[0]()
    y_halo[0]()
    coef_plane = lambda i: coef_x[pl.ds(pl.multiple_of(i * cy, 8), cy), :]
    factor(cx, coef_plane, gain_x, pivot_x, left_x, right_x)
    line_x.mat_start(left_x, right_x)
    for j in range(cy):
        coef_y[j] = coef_x[pl.ds(j, cx, stride=cy), :]
    patches = cell_smem.shape[0]
    cell = cell_row[...]
    line = lax.shift_right_logical(cell, jnp.full_like(cell, cz.bit_length() - 1))
    at_x = jnp.zeros_like(cell)
    for i in range(1, cx):
        at_x = at_x + jnp.where(line >= i * cy, 1, 0)
    places = [at_x + lax.axis_index("gx") * cx, line - at_x * cy + lax.axis_index("gy") * cy, cell - line * cz]
    hot, rank = slot_ranks(count, owner_row[...])
    place_send = to_owners(count, ny, me, place_out, place_in, place_sems)
    value_send = to_owners(count, ny, me, value_out, value_in, value_sems)
    place_send[0](by_owner(hot, rank, [place.astype(jnp.float32) for place in places]))
    factor(cy, lambda j: coef_y[j], gain_y, pivot_y, left_y, right_y)
    line_y.mat_start(left_y, right_y)
    x_halo[1]()
    y_halo[1]()
    y_slot = {member: slot for slot, member in enumerate(Y_MEMBERS)}

    def forward_x(i, carry):
        centre = [grid_x[m, i + 1] for m in range(6)]
        slope_x = lambda m: 0.5 * (grid_x[m, i + 2] - grid_x[m, i])
        slope_y = lambda m: slope_rows(
            centre[m], y_low[y_slot[m], pl.ds(i, 1), :], y_high[y_slot[m], pl.ds(i, 1), :])
        right = updated(centre, slope_x, slope_y, coef_plane(i) * (1.0 / half_step), half_step)
        gain, pivot = gain_x[i], pivot_x[i]
        now = [right[m] * pivot + gain * carry[m] for m in range(6)]
        for m in range(6):
            solved_x[m, i] = now[m]
        return tuple(now)

    lax.fori_loop(0, cx, forward_x, (jnp.zeros((cy, cz), jnp.float32),) * 6, unroll=2)
    early = min(2, line_x.steps)
    line_x.mat_merge(0)
    sweep_back(cx, gain_x, solved_x)
    line_x.rhs_start(solved_x)
    if early > 1:
        line_x.mat_merge(1)
    place_send[1]()
    fill_weights(count, me, fields_on_rows(place_in), weight_high, weight_low)
    for k in range(line_x.steps):
        if k >= early:
            line_x.mat_merge(k)
        for j in range(len(CHUNKS)):
            line_x.rhs_merge(k, j)
        if k < line_y.steps:
            line_y.mat_merge(k)
    for k in range(line_x.steps, line_y.steps):
        line_y.mat_merge(k)

    for i in range(cx):
        left, right = left_x[i], right_x[i]
        for m in range(6):
            grid_y[m, pl.ds(cx + i, cy, stride=cx), :] = (
                solved_x[m, i] + left * line_x.ends[0, m] + right * line_x.ends[1, m])
    mid_halo[0]()
    mid_halo[1]()

    y_plane = lambda m, j: grid_y[m, pl.ds(pl.multiple_of(j * cx, 8), cx), :]

    def forward_y(j, carry):
        centre = [y_plane(m, j + 1) for m in range(6)]
        slope_y = lambda m: 0.5 * (y_plane(m, j + 2) - y_plane(m, j))
        slope_x = lambda m: slope_rows(
            centre[m], line_x.ends[0, m, pl.ds(j, 1), :], line_x.ends[1, m, pl.ds(j, 1), :])
        right = updated(centre, slope_x, slope_y, coef_y[j] * (1.0 / half_step), half_step)
        gain, pivot = gain_y[j], pivot_y[j]
        now = [right[m] * pivot + gain * carry[m] for m in range(6)]
        for m in range(6):
            solved_y[m, j] = now[m]
        return tuple(now)

    lax.fori_loop(0, cy, forward_y, (jnp.zeros((cx, cz), jnp.float32),) * 6, unroll=2)
    sweep_back(cy, gain_y, solved_y)
    line_y.rhs_start(solved_y)
    for k in range(line_y.steps):
        for j in range(len(CHUNKS)):
            line_y.rhs_merge(k, j)
    for j in range(cy):
        left, right = left_y[j], right_y[j]
        for m in range(6):
            value = solved_y[m, j] + left * line_y.ends[0, m] + right * line_y.ends[1, m]
            out_ref[pl.ds(m * cx * cy + j, cx, stride=cy), :] = value

    lane = lax.broadcasted_iota(jnp.int32, (6, cz), 1)
    found = []
    for first in range(0, patches, cz):
        def fetch(q, kept):
            for u in range(16):
                at = q * 16 + u
                cell = cell_smem[first + at]
                line = cell // cz
                rows = out_ref[pl.ds(line, 6, stride=cx * cy), :]
                kept = jnp.where(lane == at, pltpu.roll(rows, (at - cell) & (cz - 1), 1), kept)
            return kept

        found.append(lax.fori_loop(0, cz // 16, fetch, jnp.zeros((6, cz), jnp.float32)))
    values = jnp.concatenate(found, axis=1)
    value_send[0](by_owner(hot, rank, [values[m:m + 1] for m in range(6)]))
    for halo in (x_halo, y_halo, mid_halo):
        halo[2]()
    line_x.drain()
    line_y.drain()
    place_send[2]()
    value_send[1]()
    high, low = split_bf16(fields_on_rows(value_in))
    both = jnp.concatenate([high, low], axis=0)
    product = dot_rows(both, weight_high[...]) + dot_rows(both, weight_low[...])
    product = (product[:8] + product[8:]) * scale
    angles = far_ref.shape[1]
    for s in range(2):
        far_ref[pl.ds(s * 6, 6), :] = product[:6, s * angles:(s + 1) * angles]
    value_send[2]()


def store_kernel(new_ref, far_ref, new_hbm, far_hbm, sems):
    copies = [pltpu.make_async_copy(new_ref, new_hbm, sems.at[0]), pltpu.make_async_copy(far_ref, far_hbm, sems.at[1])]
    for one in copies:
        one.start()
    for one in copies:
        one.wait()


def line_scratch(count, rows, lanes):
    steps = count.bit_length() - 1
    f32 = jnp.float32
    return [
        pltpu.VMEM((steps, 4, rows, lanes), f32),
        pltpu.VMEM((steps, 4, rows, lanes), f32),
        pltpu.VMEM((steps, 2, 6, rows, lanes), f32),
        pltpu.VMEM((steps, 2, 6, rows, lanes), f32),
        pltpu.VMEM((steps, 7, rows, lanes), f32),
        pltpu.VMEM((4, rows, lanes), f32),
        pltpu.VMEM((2, 6, rows, lanes), f32),
        pltpu.SemaphoreType.DMA((2, steps)),
        pltpu.SemaphoreType.DMA((2, steps, len(CHUNKS))),
    ]


def local(nx, ny, fields, material, permittivity, patch_cell, patch_owner):
    _, cx, cy, cz = fields.shape
    f32 = jnp.float32
    count = nx * ny
    patches = patch_cell.shape[0]
    vmem = pl.BlockSpec(memory_space=pltpu.VMEM)
    smem = pl.BlockSpec(memory_space=pltpu.SMEM)
    hbm = pl.BlockSpec(memory_space=pltpu.HBM)
    x_lines = [pltpu.VMEM((cx, cy, cz), f32)] * 4
    y_lines = [pltpu.VMEM((cy, cx, cz), f32)] * 4
    pinned = lambda value: pltpu.with_memory_space_constraint(value, pltpu.HBM)
    new_flat, far_field = pl.pallas_call(
        functools.partial(step_kernel, nx, ny, cx, cy, cz, 1.0 / math.sqrt(patches)),
        out_shape=(
            jax.ShapeDtypeStruct((6 * cx * cy, cz), f32),
            jax.ShapeDtypeStruct((12, ANG_DEV), f32),
        ),
        in_specs=[hbm, hbm, smem, smem, vmem, vmem],
        out_specs=(vmem, vmem),
        scratch_shapes=[
            pltpu.VMEM((cx, cy, cz), jnp.int32),
            pltpu.VMEM((6, cx + 2, cy, cz), f32),
            pltpu.VMEM((6, (cy + 2) * cx, cz), f32),
            pltpu.VMEM((2, 4, cx, cz), f32),
            pltpu.VMEM((4, cx, cz), f32),
            pltpu.VMEM((4, cx, cz), f32),
            pltpu.VMEM((cx * cy, cz), f32),
            *x_lines,
            pltpu.VMEM((6, cx, cy, cz), f32),
            pltpu.VMEM((cy, cx, cz), f32),
            *y_lines,
            pltpu.VMEM((6, cy, cx, cz), f32),
            pltpu.VMEM((2 * ANG_DEV, SLOTS * count), jnp.bfloat16),
            pltpu.VMEM((2 * ANG_DEV, SLOTS * count), jnp.bfloat16),
            *[pltpu.VMEM((count, 1, 8 * SLOTS), f32)] * 4,
            pltpu.SemaphoreType.DMA,
            pltpu.SemaphoreType.DMA,
            pltpu.SemaphoreType.DMA((3, 4)),
            pltpu.SemaphoreType.DMA((2, count)),
            pltpu.SemaphoreType.DMA((2, count)),
            *line_scratch(nx, cy, cz),
            *line_scratch(ny, cx, cz),
        ],
        compiler_params=pltpu.CompilerParams(
            collective_id=0, has_side_effects=True, vmem_limit_bytes=40 * 2**20),
        name="split_step",
    )(pinned(fields), pinned(material), pinned(permittivity), pinned(patch_cell), pinned(patch_cell[None, :]),
      pinned(patch_owner.reshape(1, patches)))
    new_flat, far_field = pl.pallas_call(
        store_kernel,
        out_shape=(
            jax.ShapeDtypeStruct((6 * cx * cy, cz), f32),
            jax.ShapeDtypeStruct((12, ANG_DEV), f32),
        ),
        in_specs=[vmem, vmem],
        out_specs=(hbm, hbm),
        scratch_shapes=[pltpu.SemaphoreType.DMA((2,))],
        compiler_params=pltpu.CompilerParams(vmem_limit_bytes=4 * 2**20),
        name="store",
    )(new_flat, far_field)
    return new_flat.reshape(fields.shape), far_field


def solution(mesh):
    return jax.shard_map(
        functools.partial(local, mesh.shape["gx"], mesh.shape["gy"]),
        mesh=mesh,
        in_specs=(
            P(None, "gx", "gy", None),
            P("gx", "gy", None),
            P(),
            P(("gx", "gy")),
            P(("gx", "gy"), None),
        ),
        out_specs=(P(None, "gx", "gy", None), P(None, ("gx", "gy"))),
        check_vma=False,
    )
```

```python
import functools
import math

import jax
import jax.numpy as jnp
from jax import lax
from jax.experimental import pallas as pl
from jax.experimental.pallas import tpu as pltpu
from jax.sharding import PartitionSpec as P

ANG_DEV = 128
COURANT = 64
KAPPA = 0.5
MESH = pl.DeviceIdType.MESH
X_MEMBERS = (1, 2, 4, 5)
Y_MEMBERS = (0, 2, 3, 5)
Z_MEMBERS = (0, 1, 3, 4)
TILE = 8
HALVES = ((0, 1, 2), (3, 4, 5))
SLOTS = 16


def lane_difference(value):
    lanes = value.shape[1]
    at = lax.broadcasted_iota(jnp.int32, value.shape, 1)
    below = jnp.where(at == 0, 0.0, pltpu.roll(value, 1, 1))
    above = jnp.where(at == lanes - 1, 0.0, pltpu.roll(value, lanes - 1, 1))
    return above - below


def updated(centre, dx, dy, half_curl, half_side):
    dz = {m: lane_difference(centre[m]) for m in Z_MEMBERS}
    curl_h = [dy[5] - dz[4], dz[3] - dx[5], dx[4] - dy[3]]
    curl_e = [dy[2] - dz[1], dz[0] - dx[2], dx[1] - dy[0]]
    return [centre[m] + half_curl * curl_h[m] for m in range(3)] + [
        centre[3 + m] - half_side * curl_e[m] for m in range(3)
    ]


def factor(length, coef_at, gain_ref, pivot_ref, left_ref, right_ref):
    zero = jnp.zeros(gain_ref.shape[1:], jnp.float32)

    def forward(i, carry):
        gain_prev, left_prev = carry
        coef = coef_at(i)
        pivot = 1.0 / (1.0 + 2.0 * coef - coef * gain_prev)
        gain = coef * pivot
        left = gain * left_prev
        gain_ref[i] = gain
        pivot_ref[i] = pivot
        left_ref[i] = left
        return gain, left

    lax.fori_loop(0, length, forward, (zero, jnp.ones_like(zero)), unroll=2)

    def backward(k, carry):
        left_next, right_next = carry
        i = length - 1 - k
        gain = gain_ref[i]
        left = left_ref[i] + gain * left_next
        right = gain * right_next
        left_ref[i] = left
        right_ref[i] = right
        return left, right

    lax.fori_loop(0, length, backward, (zero, jnp.ones_like(zero)), unroll=4)


def sweep_back(length, gain_ref, solved_ref, rows):
    def backward(k, carry):
        i = length - 1 - k
        gain = gain_ref[i, rows]
        now = [solved_ref[m, i, rows] + gain * carry[m] for m in range(6)]
        for m in range(6):
            solved_ref[m, i, rows] = now[m]
        return tuple(now)

    zero = jnp.zeros((TILE, gain_ref.shape[2]), jnp.float32)
    lax.fori_loop(0, length, backward, (zero,) * 6, unroll=4)


def tile_rows(tile):
    return pl.ds(tile * TILE, TILE)


class Line:
    def __init__(self, axis, count, refs):
        (self.mat_out, self.mat_in, self.rhs_out, self.rhs_in, self.plan, self.gains, self.ends,
         self.mat_sems, self.rhs_sems) = refs
        self.axis = axis
        self.count = count
        self.steps = count.bit_length() - 1
        self.chunks = self.rhs_out.shape[1]
        self.me = lax.axis_index(axis)

    def near(self, k):
        return 1 - (self.me // 2**k) % 2

    def partner(self, k):
        return {self.axis: self.me + (2 * self.near(k) - 1) * 2**k}

    def mat_copy(self, k):
        return pltpu.make_async_remote_copy(
            self.mat_out.at[k], self.mat_in.at[k], self.mat_sems.at[0, k], self.mat_sems.at[1, k],
            device_id=self.partner(k), device_id_type=MESH)

    def rhs_copy(self, k, chunk):
        source, target = self.rhs_out.at[k, chunk], self.rhs_in.at[k, chunk]
        if k == self.steps - 1:
            source, target = source.at[self.near(k)], target.at[0]
        return pltpu.make_async_remote_copy(
            source, target, self.rhs_sems.at[0, k, chunk], self.rhs_sems.at[1, k, chunk],
            device_id=self.partner(k), device_id_type=MESH)

    def mat_start(self, left_ref, right_ref):
        last = left_ref.shape[0] - 1
        for end, at in ((0, 0), (1, last)):
            self.mat_out[0, 2 * end] = left_ref[at]
            self.mat_out[0, 2 * end + 1] = right_ref[at]
        one, zero = jnp.ones(left_ref.shape[1:], jnp.float32), jnp.zeros(left_ref.shape[1:], jnp.float32)
        self.gains[0] = one
        self.gains[1] = zero
        self.gains[2] = zero
        self.gains[3] = one
        self.mat_copy(0).start()

    def mat_merge(self, k):
        self.mat_copy(k).wait_recv()
        n = self.near(k)
        f = 1 - n
        mine = lambda end, side: self.mat_out[k, 2 * end + side]
        other = lambda end, side: self.mat_in[k, 2 * end + side]
        m_nn, m_fn, m_nf, m_ff = mine(n, n), mine(f, n), mine(n, f), mine(f, f)
        o_nn, o_fn, o_nf, o_ff = other(f, f), other(n, f), other(f, n), other(n, n)
        inv = 1.0 / (1.0 - m_nn * o_nn)
        o_by_m = o_nn * m_nf * inv
        o_by_o = o_nf * inv
        m_by_m = m_nf * inv
        m_by_o = m_nn * o_nf * inv
        gain_in, gain_out = self.gains[n], self.gains[2 + n]
        for slot, value in enumerate((inv, o_nn * inv, m_nn * inv, m_fn, o_fn, gain_in, gain_out)):
            self.plan[k, slot] = value
        if k < self.steps - 1:
            self.mat_out[k + 1, 2 * f + f] = m_ff + m_fn * o_by_m
            self.mat_out[k + 1, 2 * f + n] = m_fn * o_by_o
            self.mat_out[k + 1, 2 * n + n] = o_ff + o_fn * m_by_o
            self.mat_out[k + 1, 2 * n + f] = o_fn * m_by_m
            self.mat_copy(k + 1).start()
            self.gains[f] = self.gains[f] + gain_in * o_by_m
            self.gains[2 + f] = self.gains[2 + f] + gain_out * o_by_m
            self.gains[n] = gain_in * o_by_o
            self.gains[2 + n] = gain_out * o_by_o

    def rhs_start(self, tile, half, firsts, lasts):
        chunk = tile * len(HALVES) + half
        for at in range(len(HALVES[half])):
            self.rhs_out[0, chunk, 0, at] = firsts[at]
            self.rhs_out[0, chunk, 1, at] = lasts[at]
        self.rhs_copy(0, chunk).start()

    def rhs_merge(self, k, tile, half):
        chunk = tile * len(HALVES) + half
        rows = tile_rows(tile)
        self.rhs_copy(k, chunk).wait_recv()
        n = self.near(k)
        f = 1 - n
        ending = k == self.steps - 1
        inv, o_nn, m_nn, m_fn, o_fn, gain_in, gain_out = [self.plan[k, slot, rows] for slot in range(7)]
        for at, m in enumerate(HALVES[half]):
            mine = self.rhs_out[k, chunk, n, at]
            other = self.rhs_in[k, chunk, 0, at] if ending else self.rhs_in[k, chunk, f, at]
            o_value = other * inv + o_nn * mine
            if not ending:
                m_value = mine * inv + m_nn * other
                self.rhs_out[k + 1, chunk, f, at] = self.rhs_out[k, chunk, f, at] + m_fn * o_value
                self.rhs_out[k + 1, chunk, n, at] = self.rhs_in[k, chunk, n, at] + o_fn * m_value
            into, out_of = gain_in * o_value, gain_out * o_value
            if k > 0:
                into, out_of = self.ends[0, m, rows] + into, self.ends[1, m, rows] + out_of
            self.ends[0, m, rows] = into
            self.ends[1, m, rows] = out_of
        if not ending:
            self.rhs_copy(k + 1, chunk).start()

    def drain(self):
        for k in range(self.steps):
            self.mat_copy(k).wait_send()
            for chunk in range(self.chunks):
                self.rhs_copy(k, chunk).wait_send()


def both_ways(axis, count, out_low, out_high, in_low, in_high, sems):
    me = lax.axis_index(axis)
    up = lambda: pltpu.make_async_remote_copy(
        out_high, in_low, sems.at[0], sems.at[1], device_id={axis: me + 1}, device_id_type=MESH)
    down = lambda: pltpu.make_async_remote_copy(
        out_low, in_high, sems.at[2], sems.at[3], device_id={axis: me - 1}, device_id_type=MESH)

    def start_up():
        @pl.when(me < count - 1)
        def _():
            up().start()

        @pl.when(me == 0)
        def _():
            in_low[...] = jnp.zeros(in_low.shape, jnp.float32)

    def start_down():
        @pl.when(me > 0)
        def _():
            down().start()

        @pl.when(me == count - 1)
        def _():
            in_high[...] = jnp.zeros(in_high.shape, jnp.float32)

    def wait():
        @pl.when(me > 0)
        def _():
            up().wait_recv()

        @pl.when(me < count - 1)
        def _():
            down().wait_recv()

    def drain():
        @pl.when(me < count - 1)
        def _():
            up().wait_send()

        @pl.when(me > 0)
        def _():
            down().wait_send()

    return start_up, start_down, wait, drain


def in_fours(count, act):
    head = (count - 1) % 4
    for k in range(1, 1 + head):
        act(k)

    def four(g, carry):
        for u in range(4):
            act(1 + head + 4 * g + u)
        return carry

    lax.fori_loop(0, (count - 1) // 4, four, 0)


def greet_all(count, ny, me, barrier):
    def hello(k):
        to = lax.rem(me + k, count)
        pl.semaphore_signal(
            barrier, inc=1, device_id=(lax.div(to, ny), lax.rem(to, ny)), device_id_type=MESH)

    in_fours(count, hello)


def cos_sin(angle):
    turns = jnp.floor(angle * (2.0 / math.pi) + 0.5)
    rest = ((angle - turns * 1.5703125) - turns * 4.837512969970703125e-4) - turns * 7.54978995489188216e-8
    square = rest * rest
    sine = ((-1.9515295891e-4 * square + 8.3321608736e-3) * square - 1.6666654611e-1) * square * rest + rest
    cosine = (
        (2.443315711809948e-5 * square - 1.388731625493765e-3) * square + 4.166664568298827e-2
    ) * square * square - 0.5 * square + 1.0
    quarter = turns.astype(jnp.int32) & 3
    swap = (quarter & 1) == 1
    plain_cos = jnp.where(swap, sine, cosine)
    plain_sin = jnp.where(swap, cosine, sine)
    minus_cos = (quarter == 1) | (quarter == 2)
    return jnp.where(minus_cos, -plain_cos, plain_cos), jnp.where(quarter >= 2, -plain_sin, plain_sin)


def split_bf16(value):
    high = value.astype(jnp.bfloat16)
    return high, (value - high.astype(jnp.float32)).astype(jnp.bfloat16)


def dot_rows(left, right):
    return lax.dot_general(left, right, (((1,), (1,)), ((), ())), preferred_element_type=jnp.float32)


def slot_ranks(count, owner):
    patches = owner.shape[1]
    hot = lax.broadcasted_iota(jnp.int32, (count, patches), 0) == owner
    before = lax.broadcasted_iota(jnp.int32, (patches, patches), 0) < lax.broadcasted_iota(
        jnp.int32, (patches, patches), 1)
    as_bf16 = lambda mask: jnp.where(mask, 1.0, 0.0).astype(jnp.bfloat16)
    ahead = lax.dot_general(as_bf16(hot), as_bf16(before), (((1,), (0,)), ((), ())),
                            preferred_element_type=jnp.float32)
    rank = jnp.sum(jnp.where(hot, ahead, 0.0), axis=0, keepdims=True)
    return as_bf16(hot), rank.astype(jnp.int32)


def by_owner(hot, rank, values):
    slots = lax.broadcasted_iota(jnp.int32, (SLOTS, rank.shape[1]), 0) == rank
    rows = [jnp.where(slots, value, 0.0) for value in values]
    rows += [jnp.zeros_like(rows[0])] * (8 - len(rows))
    high, low = split_bf16(jnp.concatenate(rows, axis=0))
    both = dot_rows(hot, jnp.concatenate([high, low], axis=0))
    return both[:, :8 * SLOTS] + both[:, 8 * SLOTS:]


def fields_on_rows(landed_ref):
    count, _, lanes = landed_ref.shape
    row = lax.broadcasted_iota(jnp.int32, (8, lanes), 0)
    block = lax.shift_right_logical(
        lax.broadcasted_iota(jnp.int32, (8, lanes), 1), jnp.full((8, lanes), SLOTS.bit_length() - 1, jnp.int32))
    groups = []
    for g in range(count // 8):
        value = jnp.concatenate([landed_ref[g * 8 + i] for i in range(8)], axis=0)
        for bit in (1, 2, 4):
            later = pltpu.roll(pltpu.roll(value, 8 - bit, 0), SLOTS * bit, 1)
            sooner = pltpu.roll(pltpu.roll(value, bit, 0), lanes - SLOTS * bit, 1)
            row_bit, block_bit = row & bit, block & bit
            value = jnp.where(row_bit == block_bit, value, jnp.where(row_bit == 0, later, sooner))
        groups.append(value)
    return jnp.concatenate(groups, axis=1)


def fill_weights(count, me, places, high_ref, low_ref):
    angles = high_ref.shape[0] // 2
    slots = places.shape[1]
    azimuth = jnp.full((16, 128), me.astype(jnp.float32) * (2.0 * math.pi / count))
    cos_phi, sin_phi = cos_sin(azimuth)
    pos = [jnp.broadcast_to(places[c:c + 1], (16, slots)) for c in range(3)]

    def group(g, carry):
        start = pl.multiple_of(g * 16, 16)
        index = (lax.broadcasted_iota(jnp.int32, (16, 128), 0) + start).astype(jnp.float32)
        cos_theta, sin_theta = cos_sin(math.pi * (index + 0.5) / angles)
        for part in range(0, slots, 128):
            at = slice(part, part + 128)
            phase = KAPPA * (pos[0][:, at] * sin_theta * cos_phi + pos[1][:, at] * sin_theta * sin_phi
                             + pos[2][:, at] * cos_theta)
            for s, value in enumerate(cos_sin(phase)):
                high, low = split_bf16(value)
                rows = pl.ds(pl.multiple_of(start + s * angles, 16), 16)
                high_ref[rows, at] = high
                low_ref[rows, at] = low
        return carry

    lax.fori_loop(0, angles // 16, group, 0)


def to_owners(count, ny, me, out_ref, landed_ref, sems):
    def copy(k):
        to = lax.rem(me + k, count)
        return pltpu.make_async_remote_copy(
            out_ref.at[to], landed_ref.at[me], sems.at[0, k], sems.at[1, k],
            device_id=(lax.div(to, ny), lax.rem(to, ny)), device_id_type=MESH)

    def start(rows):
        for i in range(count):
            out_ref[i] = rows[i:i + 1]
        landed_ref[me] = out_ref[me]
        in_fours(count, lambda k: copy(k).start())

    return start, lambda: in_fours(count, lambda k: copy(k).wait_recv()), lambda: in_fours(
        count, lambda k: copy(k).wait_send())


def step_kernel(nx, ny, cx, cy, cz, scale, fields_hbm, material_hbm, permit_ref,
                cell_row, owner_row, out_ref, far_ref, material_ref,
                grid_x, grid_y, y_out, y_low, y_high, mid_low, mid_high, coef_x,
                gain_x, pivot_x, left_x, right_x, solved_x,
                coef_y, gain_y, pivot_y, left_y, right_y, solved_y,
                weight_high, weight_low, place_out, place_in, value_out, value_in, packed, spots, spots_smem,
                load_sem, move_sems, halo_sems, place_sems, value_sems, *line_refs):
    half_step = COURANT / 2.0
    half_side = 0.5 * half_step
    count = nx * ny
    wide = cx + 2 * TILE
    tiles_x, tiles_y = cy // TILE, cx // TILE
    me = lax.axis_index("gx") * ny + lax.axis_index("gy")
    barrier = pltpu.get_barrier_semaphore()
    load = pltpu.make_async_copy(fields_hbm, grid_x.at[:, pl.ds(1, cx), pl.ds(TILE, cy)], load_sem)
    load.start()
    load_material = pltpu.make_async_copy(material_hbm, material_ref, move_sems.at[0])
    load_material.start()
    greet_all(count, ny, me, barrier)
    line_x = Line("gx", nx, line_refs[:9])
    line_y = Line("gy", ny, line_refs[9:])

    def x_halo(first, sems):
        plane = lambda i: grid_x.at[pl.ds(first, 2), i, pl.ds(TILE, cy)]
        return both_ways("gx", nx, plane(1), plane(cx), plane(0), plane(cx + 1), sems)

    mid_plane = lambda j: grid_y.at[:, pl.ds((j + 1) * wide + TILE, cx)]
    first_halos = [
        both_ways("gy", ny, y_out.at[0], y_out.at[1], y_low, y_high, halo_sems.at[0]),
        x_halo(1, halo_sems.at[1]),
        x_halo(4, halo_sems.at[2]),
    ]
    mid_halo = both_ways("gy", ny, mid_plane(0), mid_plane(cy - 1), mid_low, mid_high, halo_sems.at[3])

    def coefs(i, carry):
        which = material_ref[i]
        permit = jnp.zeros(which.shape, jnp.float32)
        for entry in range(permit_ref.shape[0]):
            permit = jnp.where(which == entry, permit_ref[entry], permit)
        coef_x[pl.ds(pl.multiple_of(i * cy, 8), cy), :] = (half_step * half_step) / permit
        return carry

    load_material.wait()
    lax.fori_loop(0, cx, coefs, 0, unroll=2)
    load.wait()
    for slot, member in enumerate(Y_MEMBERS):
        for end, row in ((0, TILE), (1, TILE + cy - 1)):
            y_out[end, slot] = jnp.concatenate(
                [grid_x[member, 1 + i, row:row + 1] for i in range(cx)], axis=0)
    pl.semaphore_wait(barrier, count - 1)
    for halo in first_halos:
        halo[0]()
        halo[1]()
    coef_plane = lambda i: coef_x[pl.ds(pl.multiple_of(i * cy, 8), cy), :]
    factor(cx, coef_plane, gain_x, pivot_x, left_x, right_x)
    line_x.mat_start(left_x, right_x)
    for j in range(cy):
        coef_y[j] = coef_x[pl.ds(j, cx, stride=cy), :]
    for m in range(6):
        for plane in (0, cy + 1):
            grid_y[m, pl.ds(plane * wide, wide), :] = jnp.zeros((wide, cz), jnp.float32)
    patches = cell_row.shape[1]
    cell = cell_row[...]
    line = lax.shift_right_logical(cell, jnp.full_like(cell, cz.bit_length() - 1))
    at_x = jnp.zeros_like(cell)
    for i in range(1, cx):
        at_x = at_x + jnp.where(line >= i * cy, 1, 0)
    at_y, at_z = line - at_x * cy, cell - line * cz
    lanes = lax.broadcasted_iota(jnp.int32, cell.shape, 1)
    spots[0:1] = at_y * cx + at_x
    spots[1:2] = (lanes - at_z) & (cz - 1)
    find = pltpu.make_async_copy(spots, spots_smem, move_sems.at[1])
    find.start()
    places = [at_x + lax.axis_index("gx") * cx, at_y + lax.axis_index("gy") * cy, at_z]
    hot, rank = slot_ranks(count, owner_row[...])
    place_send = to_owners(count, ny, me, place_out, place_in, place_sems)
    value_send = to_owners(count, ny, me, value_out, value_in, value_sems)
    place_send[0](by_owner(hot, rank, [place.astype(jnp.float32) for place in places]))
    factor(cy, lambda j: coef_y[j], gain_y, pivot_y, left_y, right_y)
    line_y.mat_start(left_y, right_y)
    for halo in first_halos:
        halo[2]()

    def solve_x(tile):
        row = (tile + 1) * TILE
        for at, side, need in ((TILE - 1, y_low, tile == 0), (TILE + cy, y_high, tile == tiles_x - 1)):
            for slot, member in enumerate(Y_MEMBERS if need else ()):
                for i in range(cx):
                    grid_x[member, i + 1, at:at + 1] = side[slot, i:i + 1]

        def forward(i, carry):
            near = lambda m, plane, shift: grid_x[m, i + 1 + plane, row + shift:row + shift + TILE]
            centre = [near(m, 0, 0) for m in range(6)]
            dx = {m: near(m, 1, 0) - near(m, -1, 0) for m in X_MEMBERS}
            dy = {m: near(m, 0, 1) - near(m, 0, -1) for m in Y_MEMBERS}
            coef = coef_x[pl.ds(pl.multiple_of(i * cy + tile * TILE, 8), TILE), :]
            right = updated(centre, dx, dy, coef * (0.5 / half_step), half_side)
            gain, pivot = gain_x[i, tile_rows(tile)], pivot_x[i, tile_rows(tile)]
            now = [right[m] * pivot + gain * carry[m] for m in range(6)]
            for m in range(6):
                solved_x[m, i, tile_rows(tile)] = now[m]
            return tuple(now)

        lax.fori_loop(0, cx, forward, (jnp.zeros((TILE, cz), jnp.float32),) * 6, unroll=2)
        sweep_back(cx, gain_x, solved_x, tile_rows(tile))
        for half, members in enumerate(HALVES):
            line_x.rhs_start(tile, half, [solved_x[m, 0, tile_rows(tile)] for m in members],
                             [solved_x[m, cx - 1, tile_rows(tile)] for m in members])

    def finish_x(tile):
        rows = tile_rows(tile)
        planes = lambda i: pl.ds((tile * TILE + 1) * wide + TILE + i, TILE, stride=wide)
        ends = [[line_x.ends[end, m, rows] for m in range(6)] for end in range(2)]
        for m in range(6):
            grid_y[m, planes(-1), :] = ends[0][m]
            grid_y[m, planes(cx), :] = ends[1][m]
        for i in range(cx):
            left, right = left_x[i, rows], right_x[i, rows]
            for m in range(6):
                grid_y[m, planes(i), :] = solved_x[m, i, rows] + left * ends[0][m] + right * ends[1][m]

    def forward_y(j, carry):
        near = lambda m, plane, shift: grid_y[m, pl.ds((j + 1 + plane) * wide + TILE + shift, cx), :]
        centre = [near(m, 0, 0) for m in range(6)]
        dx = {m: near(m, 0, 1) - near(m, 0, -1) for m in X_MEMBERS}
        dy = {m: near(m, 1, 0) - near(m, -1, 0) for m in Y_MEMBERS}
        right = updated(centre, dx, dy, coef_y[j] * (0.5 / half_step), half_side)
        gain, pivot = gain_y[j], pivot_y[j]
        now = [right[m] * pivot + gain * carry[m] for m in range(6)]
        for m in range(6):
            solved_y[m, j] = now[m]
        return tuple(now)

    order = [0, tiles_x - 1] + list(range(1, tiles_x - 1))
    for place, tile in enumerate(order):
        solve_x(tile)
        if place == 0:
            line_x.mat_merge(0)
    early = min(2, line_x.steps)
    if early > 1:
        line_x.mat_merge(1)
    place_send[1]()
    fill_weights(count, me, fields_on_rows(place_in), weight_high, weight_low)
    for k in range(line_x.steps - 1):
        if k >= early:
            line_x.mat_merge(k)
        for tile in order:
            for half in range(len(HALVES)):
                line_x.rhs_merge(k, tile, half)
        if k < line_y.steps:
            line_y.mat_merge(k)
    if line_x.steps > early:
        line_x.mat_merge(line_x.steps - 1)
    for k in range(line_x.steps - 1, line_y.steps):
        line_y.mat_merge(k)
    carry = (jnp.zeros((cx, cz), jnp.float32),) * 6
    for tile in order:
        for half in range(len(HALVES)):
            line_x.rhs_merge(line_x.steps - 1, tile, half)
        finish_x(tile)
        if tile == 0:
            mid_halo[1]()
            carry = lax.fori_loop(0, TILE - 2, forward_y, carry, unroll=2)
        if tile == tiles_x - 1:
            mid_halo[0]()
    lax.fori_loop(TILE - 2, cy, forward_y, carry, unroll=2)
    for tile in range(tiles_y):
        sweep_back(cy, gain_y, solved_y, tile_rows(tile))
    mid_halo[2]()

    def ghosts(tile):
        rows = tile_rows(tile)
        found = []
        for ref, at, sign in ((mid_low, 0, 1.0), (mid_high, cy - 1, -1.0)):
            side = sign * half_side / coef_y[at, rows]
            found.append({
                0: ref[5, rows] * (-sign * 0.5 / half_step),
                2: ref[3, rows] * (sign * 0.5 / half_step),
                3: ref[2, rows] * side,
                5: ref[0, rows] * -side,
            })
        return found

    added = [ghosts(tile) for tile in range(tiles_y)]
    for tile in range(tiles_y):
        rows = tile_rows(tile)
        low, high = added[tile]

        def outer(m, at):
            value = solved_y[m, at, rows]
            return value + left_y[at, rows] * low[m] + right_y[at, rows] * high[m] if m in low else value

        for half, members in enumerate(HALVES):
            line_y.rhs_start(tile, half, [outer(m, 0) for m in members], [outer(m, cy - 1) for m in members])
    for k in range(line_y.steps):
        for tile in range(tiles_y):
            for half in range(len(HALVES)):
                line_y.rhs_merge(k, tile, half)
            if k == line_y.steps - 1:
                rows = tile_rows(tile)
                ends = [[line_y.ends[end, m, rows] + added[tile][end][m] if m in added[tile][end]
                         else line_y.ends[end, m, rows] for m in range(6)] for end in range(2)]
                for j in range(cy):
                    left, right = left_y[j, rows], right_y[j, rows]
                    for m in range(6):
                        value = solved_y[m, j, rows] + left * ends[0][m] + right * ends[1][m]
                        out_ref[pl.ds((m * cx + tile * TILE) * cy + j, TILE, stride=cy), :] = value
                        packed[pl.ds((j * cx + tile * TILE) * 8 + m, TILE, stride=8), :] = value

    lane = lax.broadcasted_iota(jnp.int32, (8, cz), 1)
    find.wait()
    found = []
    for first in range(0, patches, cz):
        def fetch(q, kept):
            for u in range(16):
                at = q * 16 + u
                rows = packed[pl.ds(spots_smem[0, first + at] * 8, 8), :]
                kept = jnp.where(lane == at, pltpu.roll(rows, spots_smem[1, first + at], 1), kept)
            return kept

        found.append(lax.fori_loop(0, cz // 16, fetch, jnp.zeros((8, cz), jnp.float32)))
    values = jnp.concatenate(found, axis=1)
    value_send[0](by_owner(hot, rank, [values[m:m + 1] for m in range(6)]))
    for halo in [*first_halos, mid_halo]:
        halo[3]()
    line_x.drain()
    line_y.drain()
    place_send[2]()
    value_send[1]()
    high, low = split_bf16(fields_on_rows(value_in))
    both = jnp.concatenate([high, low], axis=0)
    product = dot_rows(both, weight_high[...]) + dot_rows(both, weight_low[...])
    product = (product[:8] + product[8:]) * scale
    angles = far_ref.shape[1]
    for s in range(2):
        far_ref[pl.ds(s * 6, 6), :] = product[:6, s * angles:(s + 1) * angles]
    value_send[2]()


def store_kernel(new_ref, far_ref, new_hbm, far_hbm, sems):
    copies = [pltpu.make_async_copy(new_ref, new_hbm, sems.at[0]), pltpu.make_async_copy(far_ref, far_hbm, sems.at[1])]
    for one in copies:
        one.start()
    for one in copies:
        one.wait()


def line_scratch(count, rows, lanes):
    steps = count.bit_length() - 1
    chunks = rows // TILE * len(HALVES)
    f32 = jnp.float32
    return [
        pltpu.VMEM((steps, 4, rows, lanes), f32),
        pltpu.VMEM((steps, 4, rows, lanes), f32),
        pltpu.VMEM((steps, chunks, 2, 3, TILE, lanes), f32),
        pltpu.VMEM((steps, chunks, 2, 3, TILE, lanes), f32),
        pltpu.VMEM((steps, 7, rows, lanes), f32),
        pltpu.VMEM((4, rows, lanes), f32),
        pltpu.VMEM((2, 6, rows, lanes), f32),
        pltpu.SemaphoreType.DMA((2, steps)),
        pltpu.SemaphoreType.DMA((2, steps, chunks)),
    ]


def local(nx, ny, fields, material, permittivity, patch_cell, patch_owner):
    _, cx, cy, cz = fields.shape
    f32 = jnp.float32
    count = nx * ny
    patches = patch_cell.shape[0]
    vmem = pl.BlockSpec(memory_space=pltpu.VMEM)
    smem = pl.BlockSpec(memory_space=pltpu.SMEM)
    hbm = pl.BlockSpec(memory_space=pltpu.HBM)
    x_lines = [pltpu.VMEM((cx, cy, cz), f32)] * 4
    y_lines = [pltpu.VMEM((cy, cx, cz), f32)] * 4
    pinned = lambda value: pltpu.with_memory_space_constraint(value, pltpu.HBM)
    new_flat, far_field = pl.pallas_call(
        functools.partial(step_kernel, nx, ny, cx, cy, cz, 1.0 / math.sqrt(patches)),
        out_shape=(
            jax.ShapeDtypeStruct((6 * cx * cy, cz), f32),
            jax.ShapeDtypeStruct((12, ANG_DEV), f32),
        ),
        in_specs=[hbm, hbm, smem, vmem, vmem],
        out_specs=(vmem, vmem),
        scratch_shapes=[
            pltpu.VMEM((cx, cy, cz), jnp.int32),
            pltpu.VMEM((6, cx + 2, cy + 2 * TILE, cz), f32),
            pltpu.VMEM((6, (cy + 2) * (cx + 2 * TILE), cz), f32),
            pltpu.VMEM((2, 4, cx, cz), f32),
            pltpu.VMEM((4, cx, cz), f32),
            pltpu.VMEM((4, cx, cz), f32),
            pltpu.VMEM((6, cx, cz), f32),
            pltpu.VMEM((6, cx, cz), f32),
            pltpu.VMEM((cx * cy, cz), f32),
            *x_lines,
            pltpu.VMEM((6, cx, cy, cz), f32),
            pltpu.VMEM((cy, cx, cz), f32),
            *y_lines,
            pltpu.VMEM((6, cy, cx, cz), f32),
            pltpu.VMEM((2 * ANG_DEV, SLOTS * count), jnp.bfloat16),
            pltpu.VMEM((2 * ANG_DEV, SLOTS * count), jnp.bfloat16),
            *[pltpu.VMEM((count, 1, 8 * SLOTS), f32)] * 4,
            pltpu.VMEM((cx * cy * 8, cz), f32),
            pltpu.VMEM((2, patches), jnp.int32),
            pltpu.SMEM((2, patches), jnp.int32),
            pltpu.SemaphoreType.DMA,
            pltpu.SemaphoreType.DMA((2,)),
            pltpu.SemaphoreType.DMA((4, 4)),
            pltpu.SemaphoreType.DMA((2, count)),
            pltpu.SemaphoreType.DMA((2, count)),
            *line_scratch(nx, cy, cz),
            *line_scratch(ny, cx, cz),
        ],
        compiler_params=pltpu.CompilerParams(
            collective_id=0, has_side_effects=True, vmem_limit_bytes=40 * 2**20),
        name="split_step",
    )(pinned(fields), pinned(material), pinned(permittivity), pinned(patch_cell[None, :]),
      pinned(patch_owner.reshape(1, patches)))
    new_flat, far_field = pl.pallas_call(
        store_kernel,
        out_shape=(
            jax.ShapeDtypeStruct((6 * cx * cy, cz), f32),
            jax.ShapeDtypeStruct((12, ANG_DEV), f32),
        ),
        in_specs=[vmem, vmem],
        out_specs=(hbm, hbm),
        scratch_shapes=[pltpu.SemaphoreType.DMA((2,))],
        compiler_params=pltpu.CompilerParams(vmem_limit_bytes=4 * 2**20),
        name="store",
    )(new_flat, far_field)
    return new_flat.reshape(fields.shape), far_field


def solution(mesh):
    return jax.shard_map(
        functools.partial(local, mesh.shape["gx"], mesh.shape["gy"]),
        mesh=mesh,
        in_specs=(
            P(None, "gx", "gy", None),
            P("gx", "gy", None),
            P(),
            P(("gx", "gy")),
            P(("gx", "gy"), None),
        ),
        out_specs=(P(None, "gx", "gy", None), P(None, ("gx", "gy"))),
        check_vma=False,
    )
```

```python
import functools
import math

import jax
import jax.numpy as jnp
from jax import lax
from jax.experimental import pallas as pl
from jax.experimental.pallas import tpu as pltpu
from jax.sharding import PartitionSpec as P

ANG_DEV = 128
COURANT = 64
KAPPA = 0.5
MESH = pl.DeviceIdType.MESH
X_MEMBERS = (1, 2, 4, 5)
Y_MEMBERS = (0, 2, 3, 5)
Z_MEMBERS = (0, 1, 3, 4)
TILE = 8
HALVES = ((0, 1, 2), (3, 4, 5))
SLOTS = 16


def lane_difference(value):
    lanes = value.shape[1]
    at = lax.broadcasted_iota(jnp.int32, value.shape, 1)
    below = jnp.where(at == 0, 0.0, pltpu.roll(value, 1, 1))
    above = jnp.where(at == lanes - 1, 0.0, pltpu.roll(value, lanes - 1, 1))
    return above - below


def updated(centre, dx, dy, half_curl, half_side):
    dz = {m: lane_difference(centre[m]) for m in Z_MEMBERS}
    curl_h = [dy[5] - dz[4], dz[3] - dx[5], dx[4] - dy[3]]
    curl_e = [dy[2] - dz[1], dz[0] - dx[2], dx[1] - dy[0]]
    return [centre[m] + half_curl * curl_h[m] for m in range(3)] + [
        centre[3 + m] - half_side * curl_e[m] for m in range(3)
    ]


def factor(length, coef_at, gain_ref, pivot_ref, left_ref, right_ref):
    zero = jnp.zeros(gain_ref.shape[1:], jnp.float32)

    def forward(i, carry):
        gain_prev, left_prev = carry
        coef = coef_at(i)
        pivot = 1.0 / (1.0 + 2.0 * coef - coef * gain_prev)
        gain = coef * pivot
        left = gain * left_prev
        gain_ref[i] = gain
        pivot_ref[i] = pivot
        left_ref[i] = left
        return gain, left

    lax.fori_loop(0, length, forward, (zero, jnp.ones_like(zero)), unroll=2)

    def backward(k, carry):
        left_next, right_next = carry
        i = length - 1 - k
        gain = gain_ref[i]
        left = left_ref[i] + gain * left_next
        right = gain * right_next
        left_ref[i] = left
        right_ref[i] = right
        return left, right

    lax.fori_loop(0, length, backward, (zero, jnp.ones_like(zero)), unroll=4)


def sweep_back(length, gain_ref, solved_ref, rows):
    def backward(k, carry):
        i = length - 1 - k
        gain = gain_ref[i, rows]
        now = [solved_ref[m, i, rows] + gain * carry[m] for m in range(6)]
        for m in range(6):
            solved_ref[m, i, rows] = now[m]
        return tuple(now)

    zero = jnp.zeros((TILE, gain_ref.shape[2]), jnp.float32)
    lax.fori_loop(0, length, backward, (zero,) * 6, unroll=4)


def padded_rows(rows):
    return (rows // TILE + 2 | 1) * TILE


def tile_rows(tile):
    return pl.ds(tile * TILE, TILE)


class Line:
    def __init__(self, axis, count, refs):
        (self.mat_out, self.mat_in, self.rhs_out, self.rhs_in, self.plan, self.gains, self.ends,
         self.sent, self.mat_sems, self.rhs_sems) = refs
        self.axis = axis
        self.count = count
        self.steps = count.bit_length() - 1
        self.chunks = self.rhs_out.shape[1]
        self.me = lax.axis_index(axis)

    def near(self, k):
        return 1 - (self.me // 2**k) % 2

    def partner(self, k):
        return {self.axis: self.me + (2 * self.near(k) - 1) * 2**k}

    def mat_copy(self, k):
        return pltpu.make_async_remote_copy(
            self.mat_out.at[k], self.mat_in.at[k], self.sent.at[0], self.mat_sems.at[k],
            device_id=self.partner(k), device_id_type=MESH)

    def rhs_copy(self, k, chunk):
        source, target = self.rhs_out.at[k, chunk], self.rhs_in.at[k, chunk]
        if k == self.steps - 1:
            source, target = source.at[self.near(k)], target.at[0]
        return pltpu.make_async_remote_copy(
            source, target, self.sent.at[1 if k < self.steps - 1 else 2], self.rhs_sems.at[k, chunk],
            device_id=self.partner(k), device_id_type=MESH)

    def mat_start(self, left_ref, right_ref):
        last = left_ref.shape[0] - 1
        for end, at in ((0, 0), (1, last)):
            self.mat_out[0, 2 * end] = left_ref[at]
            self.mat_out[0, 2 * end + 1] = right_ref[at]
        one, zero = jnp.ones(left_ref.shape[1:], jnp.float32), jnp.zeros(left_ref.shape[1:], jnp.float32)
        self.gains[0] = one
        self.gains[1] = zero
        self.gains[2] = zero
        self.gains[3] = one
        self.mat_copy(0).start()

    def mat_merge(self, k):
        self.mat_copy(k).wait_recv()
        n = self.near(k)
        f = 1 - n
        mine = lambda end, side: self.mat_out[k, 2 * end + side]
        other = lambda end, side: self.mat_in[k, 2 * end + side]
        m_nn, m_fn, m_nf, m_ff = mine(n, n), mine(f, n), mine(n, f), mine(f, f)
        o_nn, o_fn, o_nf, o_ff = other(f, f), other(n, f), other(f, n), other(n, n)
        inv = 1.0 / (1.0 - m_nn * o_nn)
        o_by_m = o_nn * m_nf * inv
        o_by_o = o_nf * inv
        m_by_m = m_nf * inv
        m_by_o = m_nn * o_nf * inv
        gain_in, gain_out = self.gains[n], self.gains[2 + n]
        for slot, value in enumerate((inv, o_nn * inv, m_nn * inv, m_fn, o_fn, gain_in, gain_out)):
            self.plan[k, slot] = value
        if k < self.steps - 1:
            self.mat_out[k + 1, 2 * f + f] = m_ff + m_fn * o_by_m
            self.mat_out[k + 1, 2 * f + n] = m_fn * o_by_o
            self.mat_out[k + 1, 2 * n + n] = o_ff + o_fn * m_by_o
            self.mat_out[k + 1, 2 * n + f] = o_fn * m_by_m
            self.mat_copy(k + 1).start()
            self.gains[f] = self.gains[f] + gain_in * o_by_m
            self.gains[2 + f] = self.gains[2 + f] + gain_out * o_by_m
            self.gains[n] = gain_in * o_by_o
            self.gains[2 + n] = gain_out * o_by_o

    def rhs_start(self, tile, half, firsts, lasts):
        chunk = tile * len(HALVES) + half
        for at in range(len(HALVES[half])):
            self.rhs_out[0, chunk, 0, at] = firsts[at]
            self.rhs_out[0, chunk, 1, at] = lasts[at]
        self.rhs_copy(0, chunk).start()

    def rhs_merge(self, k, tile, half):
        chunk = tile * len(HALVES) + half
        rows = tile_rows(tile)
        self.rhs_copy(k, chunk).wait_recv()
        n = self.near(k)
        f = 1 - n
        ending = k == self.steps - 1
        inv, o_nn, m_nn, m_fn, o_fn, gain_in, gain_out = [self.plan[k, slot, rows] for slot in range(7)]
        for at, m in enumerate(HALVES[half]):
            mine = self.rhs_out[k, chunk, n, at]
            other = self.rhs_in[k, chunk, 0, at] if ending else self.rhs_in[k, chunk, f, at]
            o_value = other * inv + o_nn * mine
            if not ending:
                m_value = mine * inv + m_nn * other
                self.rhs_out[k + 1, chunk, f, at] = self.rhs_out[k, chunk, f, at] + m_fn * o_value
                self.rhs_out[k + 1, chunk, n, at] = self.rhs_in[k, chunk, n, at] + o_fn * m_value
            into, out_of = gain_in * o_value, gain_out * o_value
            if k > 0:
                into, out_of = self.ends[0, m, rows] + into, self.ends[1, m, rows] + out_of
            self.ends[0, m, rows] = into
            self.ends[1, m, rows] = out_of
        if not ending:
            self.rhs_copy(k + 1, chunk).start()

    def drain(self):
        early = pl.ds(0, self.steps - 1)
        last = self.steps - 1
        for slot, source, target in (
            (0, self.mat_out, self.mat_in),
            (1, self.rhs_out.at[early], self.rhs_in.at[early]),
            (2, self.rhs_out.at[last, :, 0], self.rhs_in.at[last, :, 0]),
        ):
            pltpu.make_async_remote_copy(
                source, target, self.sent.at[slot], self.mat_sems.at[0],
                device_id=self.partner(0), device_id_type=MESH).wait_send()


def both_ways(axis, count, out_low, out_high, in_low, in_high, sems):
    me = lax.axis_index(axis)
    up = lambda: pltpu.make_async_remote_copy(
        out_high, in_low, sems.at[0], sems.at[1], device_id={axis: me + 1}, device_id_type=MESH)
    down = lambda: pltpu.make_async_remote_copy(
        out_low, in_high, sems.at[2], sems.at[3], device_id={axis: me - 1}, device_id_type=MESH)

    def start_up():
        @pl.when(me < count - 1)
        def _():
            up().start()

        @pl.when(me == 0)
        def _():
            in_low[...] = jnp.zeros(in_low.shape, jnp.float32)

    def start_down():
        @pl.when(me > 0)
        def _():
            down().start()

        @pl.when(me == count - 1)
        def _():
            in_high[...] = jnp.zeros(in_high.shape, jnp.float32)

    def wait():
        @pl.when(me > 0)
        def _():
            up().wait_recv()

        @pl.when(me < count - 1)
        def _():
            down().wait_recv()

    def drain():
        @pl.when(me < count - 1)
        def _():
            up().wait_send()

        @pl.when(me > 0)
        def _():
            down().wait_send()

    return start_up, start_down, wait, drain


def in_fours(count, act):
    head = (count - 1) % 4
    for k in range(1, 1 + head):
        act(k)

    def four(g, carry):
        for u in range(4):
            act(1 + head + 4 * g + u)
        return carry

    lax.fori_loop(0, (count - 1) // 4, four, 0)


def greet_all(count, ny, me, barrier):
    def hello(k):
        to = lax.rem(me + k, count)
        pl.semaphore_signal(
            barrier, inc=1, device_id=(lax.div(to, ny), lax.rem(to, ny)), device_id_type=MESH)

    in_fours(count, hello)


def cos_sin(angle):
    turns = jnp.floor(angle * (2.0 / math.pi) + 0.5)
    rest = ((angle - turns * 1.5703125) - turns * 4.837512969970703125e-4) - turns * 7.54978995489188216e-8
    square = rest * rest
    sine = ((-1.9515295891e-4 * square + 8.3321608736e-3) * square - 1.6666654611e-1) * square * rest + rest
    cosine = (
        (2.443315711809948e-5 * square - 1.388731625493765e-3) * square + 4.166664568298827e-2
    ) * square * square - 0.5 * square + 1.0
    quarter = turns.astype(jnp.int32) & 3
    swap = (quarter & 1) == 1
    plain_cos = jnp.where(swap, sine, cosine)
    plain_sin = jnp.where(swap, cosine, sine)
    minus_cos = (quarter == 1) | (quarter == 2)
    return jnp.where(minus_cos, -plain_cos, plain_cos), jnp.where(quarter >= 2, -plain_sin, plain_sin)


def split_bf16(value):
    high = value.astype(jnp.bfloat16)
    return high, (value - high.astype(jnp.float32)).astype(jnp.bfloat16)


def dot_rows(left, right):
    return lax.dot_general(left, right, (((1,), (1,)), ((), ())), preferred_element_type=jnp.float32)


def slot_ranks(count, owner):
    patches = owner.shape[1]
    hot = lax.broadcasted_iota(jnp.int32, (count, patches), 0) == owner
    before = lax.broadcasted_iota(jnp.int32, (patches, patches), 0) < lax.broadcasted_iota(
        jnp.int32, (patches, patches), 1)
    as_bf16 = lambda mask: jnp.where(mask, 1.0, 0.0).astype(jnp.bfloat16)
    ahead = lax.dot_general(as_bf16(hot), as_bf16(before), (((1,), (0,)), ((), ())),
                            preferred_element_type=jnp.float32)
    rank = jnp.sum(jnp.where(hot, ahead, 0.0), axis=0, keepdims=True)
    return as_bf16(hot), rank.astype(jnp.int32)


def by_owner(hot, rank, values):
    slots = lax.broadcasted_iota(jnp.int32, (SLOTS, rank.shape[1]), 0) == rank
    rows = [jnp.where(slots, value, 0.0) for value in values]
    rows += [jnp.zeros_like(rows[0])] * (8 - len(rows))
    high, low = split_bf16(jnp.concatenate(rows, axis=0))
    both = dot_rows(hot, jnp.concatenate([high, low], axis=0))
    return both[:, :8 * SLOTS] + both[:, 8 * SLOTS:]


def fields_on_rows(landed_ref):
    count, _, lanes = landed_ref.shape
    row = lax.broadcasted_iota(jnp.int32, (8, lanes), 0)
    block = lax.shift_right_logical(
        lax.broadcasted_iota(jnp.int32, (8, lanes), 1), jnp.full((8, lanes), SLOTS.bit_length() - 1, jnp.int32))
    groups = []
    for g in range(count // 8):
        value = jnp.concatenate([landed_ref[g * 8 + i] for i in range(8)], axis=0)
        for bit in (1, 2, 4):
            later = pltpu.roll(pltpu.roll(value, 8 - bit, 0), SLOTS * bit, 1)
            sooner = pltpu.roll(pltpu.roll(value, bit, 0), lanes - SLOTS * bit, 1)
            row_bit, block_bit = row & bit, block & bit
            value = jnp.where(row_bit == block_bit, value, jnp.where(row_bit == 0, later, sooner))
        groups.append(value)
    return jnp.concatenate(groups, axis=1)


def fill_weights(count, me, places, high_ref, low_ref):
    angles = high_ref.shape[0] // 2
    slots = places.shape[1]
    azimuth = jnp.full((16, 128), me.astype(jnp.float32) * (2.0 * math.pi / count))
    cos_phi, sin_phi = cos_sin(azimuth)
    pos = [jnp.broadcast_to(places[c:c + 1], (16, slots)) for c in range(3)]

    def group(g, carry):
        start = pl.multiple_of(g * 16, 16)
        index = (lax.broadcasted_iota(jnp.int32, (16, 128), 0) + start).astype(jnp.float32)
        cos_theta, sin_theta = cos_sin(math.pi * (index + 0.5) / angles)
        for part in range(0, slots, 128):
            at = slice(part, part + 128)
            phase = KAPPA * (pos[0][:, at] * sin_theta * cos_phi + pos[1][:, at] * sin_theta * sin_phi
                             + pos[2][:, at] * cos_theta)
            for s, value in enumerate(cos_sin(phase)):
                high, low = split_bf16(value)
                rows = pl.ds(pl.multiple_of(start + s * angles, 16), 16)
                high_ref[rows, at] = high
                low_ref[rows, at] = low
        return carry

    lax.fori_loop(0, angles // 16, group, 0)


def to_owners(count, ny, me, out_ref, landed_ref, sems):
    def copy(k):
        to = lax.rem(me + k, count)
        return pltpu.make_async_remote_copy(
            out_ref.at[to], landed_ref.at[me], sems.at[0], sems.at[1],
            device_id=(lax.div(to, ny), lax.rem(to, ny)), device_id_type=MESH)

    def start(rows):
        for i in range(count):
            out_ref[i] = rows[i:i + 1]
        landed_ref[me] = out_ref[me]
        in_fours(count, lambda k: copy(k).start())

    others = pl.ds(0, count - 1)
    whole = pltpu.make_async_remote_copy(
        out_ref.at[others], landed_ref.at[others], sems.at[0], sems.at[1],
        device_id=(me // ny, me % ny), device_id_type=MESH)
    return start, whole.wait_recv, whole.wait_send


def step_kernel(nx, ny, cx, cy, cz, scale, fields_hbm, material_hbm, permit_ref,
                cell_row, owner_row, out_ref, far_ref, material_ref,
                grid_x, grid_y, y_out, y_low, y_high, mid_low, mid_high, coef_x,
                gain_x, pivot_x, left_x, right_x, solved_x,
                coef_y, gain_y, pivot_y, left_y, right_y, solved_y,
                weight_high, weight_low, place_out, place_in, value_out, value_in, packed, spots, spots_smem,
                load_sem, move_sems, halo_sems, place_sems, value_sems, *line_refs):
    half_step = COURANT / 2.0
    half_side = 0.5 * half_step
    count = nx * ny
    wide = padded_rows(cx)
    tiles_x, tiles_y = cy // TILE, cx // TILE
    me = lax.axis_index("gx") * ny + lax.axis_index("gy")
    barrier = pltpu.get_barrier_semaphore()
    load = pltpu.make_async_copy(fields_hbm, grid_x.at[:, pl.ds(1, cx), pl.ds(TILE, cy)], load_sem)
    load.start()
    load_material = pltpu.make_async_copy(material_hbm, material_ref, move_sems.at[0])
    load_material.start()
    greet_all(count, ny, me, barrier)
    line_x = Line("gx", nx, line_refs[:10])
    line_y = Line("gy", ny, line_refs[10:])

    def x_halo(first, sems):
        plane = lambda i: grid_x.at[pl.ds(first, 2), i, pl.ds(TILE, cy)]
        return both_ways("gx", nx, plane(1), plane(cx), plane(0), plane(cx + 1), sems)

    mid_plane = lambda j: grid_y.at[:, pl.ds((j + 1) * wide + TILE, cx)]
    first_halos = [
        both_ways("gy", ny, y_out.at[0], y_out.at[1], y_low, y_high, halo_sems.at[0]),
        x_halo(1, halo_sems.at[1]),
        x_halo(4, halo_sems.at[2]),
    ]
    mid_halo = both_ways("gy", ny, mid_plane(0), mid_plane(cy - 1), mid_low, mid_high, halo_sems.at[3])

    def coefs(i, carry):
        which = material_ref[i]
        permit = jnp.zeros(which.shape, jnp.float32)
        for entry in range(permit_ref.shape[0]):
            permit = jnp.where(which == entry, permit_ref[entry], permit)
        coef_x[pl.ds(pl.multiple_of(i * cy, 8), cy), :] = (half_step * half_step) / permit
        return carry

    load_material.wait()
    lax.fori_loop(0, cx, coefs, 0, unroll=2)
    load.wait()
    for slot, member in enumerate(Y_MEMBERS):
        for end, row in ((0, TILE), (1, TILE + cy - 1)):
            y_out[end, slot] = jnp.concatenate(
                [grid_x[member, 1 + i, row:row + 1] for i in range(cx)], axis=0)
    pl.semaphore_wait(barrier, count - 1)
    for halo in first_halos:
        halo[0]()
        halo[1]()
    coef_plane = lambda i: coef_x[pl.ds(pl.multiple_of(i * cy, 8), cy), :]
    factor(cx, coef_plane, gain_x, pivot_x, left_x, right_x)
    line_x.mat_start(left_x, right_x)
    for j in range(cy):
        coef_y[j] = coef_x[pl.ds(j, cx, stride=cy), :]
    for m in range(6):
        for plane in (0, cy + 1):
            grid_y[m, pl.ds(plane * wide, wide), :] = jnp.zeros((wide, cz), jnp.float32)
    patches = cell_row.shape[1]
    cell = cell_row[...]
    line = lax.shift_right_logical(cell, jnp.full_like(cell, cz.bit_length() - 1))
    at_x = jnp.zeros_like(cell)
    for i in range(1, cx):
        at_x = at_x + jnp.where(line >= i * cy, 1, 0)
    at_y, at_z = line - at_x * cy, cell - line * cz
    lanes = lax.broadcasted_iota(jnp.int32, cell.shape, 1)
    spots[0:1] = (at_y * cx + at_x) * 8
    spots[1:2] = (lanes - at_z) & (cz - 1)
    find = pltpu.make_async_copy(spots, spots_smem, move_sems.at[1])
    find.start()
    places = [at_x + lax.axis_index("gx") * cx, at_y + lax.axis_index("gy") * cy, at_z]
    hot, rank = slot_ranks(count, owner_row[...])
    place_send = to_owners(count, ny, me, place_out, place_in, place_sems)
    value_send = to_owners(count, ny, me, value_out, value_in, value_sems)
    place_send[0](by_owner(hot, rank, [place.astype(jnp.float32) for place in places]))
    factor(cy, lambda j: coef_y[j], gain_y, pivot_y, left_y, right_y)
    line_y.mat_start(left_y, right_y)
    for halo in first_halos:
        halo[2]()

    def solve_x(tile):
        row = (tile + 1) * TILE
        for at, side, need in ((TILE - 1, y_low, tile == 0), (TILE + cy, y_high, tile == tiles_x - 1)):
            for slot, member in enumerate(Y_MEMBERS if need else ()):
                for i in range(cx):
                    grid_x[member, i + 1, at:at + 1] = side[slot, i:i + 1]

        def forward(i, carry):
            near = lambda m, plane, shift: grid_x[m, i + 1 + plane, row + shift:row + shift + TILE]
            centre = [near(m, 0, 0) for m in range(6)]
            dx = {m: near(m, 1, 0) - near(m, -1, 0) for m in X_MEMBERS}
            dy = {m: near(m, 0, 1) - near(m, 0, -1) for m in Y_MEMBERS}
            coef = coef_x[pl.ds(pl.multiple_of(i * cy + tile * TILE, 8), TILE), :]
            right = updated(centre, dx, dy, coef * (0.5 / half_step), half_side)
            gain, pivot = gain_x[i, tile_rows(tile)], pivot_x[i, tile_rows(tile)]
            now = [right[m] * pivot + gain * carry[m] for m in range(6)]
            for m in range(6):
                solved_x[m, i, tile_rows(tile)] = now[m]
            return tuple(now)

        lax.fori_loop(0, cx, forward, (jnp.zeros((TILE, cz), jnp.float32),) * 6, unroll=4)
        sweep_back(cx, gain_x, solved_x, tile_rows(tile))
        for half, members in enumerate(HALVES):
            line_x.rhs_start(tile, half, [solved_x[m, 0, tile_rows(tile)] for m in members],
                             [solved_x[m, cx - 1, tile_rows(tile)] for m in members])

    def finish_x(tile):
        rows = tile_rows(tile)
        planes = lambda i: pl.ds((tile * TILE + 1) * wide + TILE + i, TILE, stride=wide)
        ends = [[line_x.ends[end, m, rows] for m in range(6)] for end in range(2)]
        for m in range(6):
            grid_y[m, planes(-1), :] = ends[0][m]
            grid_y[m, planes(cx), :] = ends[1][m]
        for i in range(cx):
            left, right = left_x[i, rows], right_x[i, rows]
            for m in range(6):
                grid_y[m, planes(i), :] = solved_x[m, i, rows] + left * ends[0][m] + right * ends[1][m]

    def forward_y(j, carry):
        near = lambda m, plane, shift: grid_y[m, pl.ds((j + 1 + plane) * wide + TILE + shift, cx), :]
        centre = [near(m, 0, 0) for m in range(6)]
        dx = {m: near(m, 0, 1) - near(m, 0, -1) for m in X_MEMBERS}
        dy = {m: near(m, 1, 0) - near(m, -1, 0) for m in Y_MEMBERS}
        right = updated(centre, dx, dy, coef_y[j] * (0.5 / half_step), half_side)
        gain, pivot = gain_y[j], pivot_y[j]
        now = [right[m] * pivot + gain * carry[m] for m in range(6)]
        for m in range(6):
            solved_y[m, j] = now[m]
        return tuple(now)

    order = [0, tiles_x - 1] + list(range(1, tiles_x - 1))
    for place, tile in enumerate(order):
        solve_x(tile)
        if place == 0:
            line_x.mat_merge(0)
    early = min(2, line_x.steps)
    if early > 1:
        line_x.mat_merge(1)
    place_send[1]()
    fill_weights(count, me, fields_on_rows(place_in), weight_high, weight_low)
    for k in range(line_x.steps - 1):
        if k >= early:
            line_x.mat_merge(k)
        for tile in order:
            for half in range(len(HALVES)):
                line_x.rhs_merge(k, tile, half)
        if k < line_y.steps:
            line_y.mat_merge(k)
    if line_x.steps > early:
        line_x.mat_merge(line_x.steps - 1)
    for k in range(line_x.steps - 1, line_y.steps):
        line_y.mat_merge(k)
    carry = (jnp.zeros((cx, cz), jnp.float32),) * 6
    for tile in order:
        for half in range(len(HALVES)):
            line_x.rhs_merge(line_x.steps - 1, tile, half)
        finish_x(tile)
        if tile == 0:
            mid_halo[1]()
            carry = lax.fori_loop(0, TILE - 2, forward_y, carry, unroll=2)
        if tile == tiles_x - 1:
            mid_halo[0]()
    lax.fori_loop(TILE - 2, cy, forward_y, carry, unroll=2)
    for tile in range(tiles_y):
        sweep_back(cy, gain_y, solved_y, tile_rows(tile))
    mid_halo[2]()

    def ghosts(tile):
        rows = tile_rows(tile)
        found = []
        for ref, at, sign in ((mid_low, 0, 1.0), (mid_high, cy - 1, -1.0)):
            side = sign * half_side / coef_y[at, rows]
            found.append({
                0: ref[5, rows] * (-sign * 0.5 / half_step),
                2: ref[3, rows] * (sign * 0.5 / half_step),
                3: ref[2, rows] * side,
                5: ref[0, rows] * -side,
            })
        return found

    added = [ghosts(tile) for tile in range(tiles_y)]
    for tile in range(tiles_y):
        rows = tile_rows(tile)
        low, high = added[tile]

        def outer(m, at):
            value = solved_y[m, at, rows]
            return value + left_y[at, rows] * low[m] + right_y[at, rows] * high[m] if m in low else value

        for half, members in enumerate(HALVES):
            line_y.rhs_start(tile, half, [outer(m, 0) for m in members], [outer(m, cy - 1) for m in members])
    for k in range(line_y.steps):
        for tile in range(tiles_y):
            for half in range(len(HALVES)):
                line_y.rhs_merge(k, tile, half)
            if k == line_y.steps - 1:
                rows = tile_rows(tile)
                ends = [[line_y.ends[end, m, rows] + added[tile][end][m] if m in added[tile][end]
                         else line_y.ends[end, m, rows] for m in range(6)] for end in range(2)]
                for j in range(cy):
                    left, right = left_y[j, rows], right_y[j, rows]
                    for m in range(6):
                        value = solved_y[m, j, rows] + left * ends[0][m] + right * ends[1][m]
                        out_ref[pl.ds((m * cx + tile * TILE) * cy + j, TILE, stride=cy), :] = value
                        packed[pl.ds((j * cx + tile * TILE) * 8 + m, TILE, stride=8), :] = value

    lane = lax.broadcasted_iota(jnp.int32, (8, cz), 1)
    find.wait()
    found = []
    for first in range(0, patches, cz):
        kept = jnp.zeros((8, cz), jnp.float32)
        for at in range(cz):
            rows = packed[pl.ds(spots_smem[0, first + at], 8), :]
            kept = jnp.where(lane == at, pltpu.roll(rows, spots_smem[1, first + at], 1), kept)
        found.append(kept)
    values = jnp.concatenate(found, axis=1)
    value_send[0](by_owner(hot, rank, [values[m:m + 1] for m in range(6)]))
    for halo in [*first_halos, mid_halo]:
        halo[3]()
    line_x.drain()
    line_y.drain()
    place_send[2]()
    value_send[1]()
    high, low = split_bf16(fields_on_rows(value_in))
    both = jnp.concatenate([high, low], axis=0)
    product = dot_rows(both, weight_high[...]) + dot_rows(both, weight_low[...])
    product = (product[:8] + product[8:]) * scale
    angles = far_ref.shape[1]
    for s in range(2):
        far_ref[pl.ds(s * 6, 6), :] = product[:6, s * angles:(s + 1) * angles]
    value_send[2]()


def store_kernel(new_ref, far_ref, new_hbm, far_hbm, sems):
    copies = [pltpu.make_async_copy(new_ref, new_hbm, sems.at[0]), pltpu.make_async_copy(far_ref, far_hbm, sems.at[1])]
    for one in copies:
        one.start()
    for one in copies:
        one.wait()


def line_scratch(count, rows, lanes):
    steps = count.bit_length() - 1
    chunks = rows // TILE * len(HALVES)
    f32 = jnp.float32
    return [
        pltpu.VMEM((steps, 4, rows, lanes), f32),
        pltpu.VMEM((steps, 4, rows, lanes), f32),
        pltpu.VMEM((steps, chunks, 2, 3, TILE, lanes), f32),
        pltpu.VMEM((steps, chunks, 2, 3, TILE, lanes), f32),
        pltpu.VMEM((steps, 7, rows, lanes), f32),
        pltpu.VMEM((4, rows, lanes), f32),
        pltpu.VMEM((2, 6, rows, lanes), f32),
        pltpu.SemaphoreType.DMA((3,)),
        pltpu.SemaphoreType.DMA((steps,)),
        pltpu.SemaphoreType.DMA((steps, chunks)),
    ]


def local(nx, ny, fields, material, permittivity, patch_cell, patch_owner):
    _, cx, cy, cz = fields.shape
    f32 = jnp.float32
    count = nx * ny
    patches = patch_cell.shape[0]
    vmem = pl.BlockSpec(memory_space=pltpu.VMEM)
    smem = pl.BlockSpec(memory_space=pltpu.SMEM)
    hbm = pl.BlockSpec(memory_space=pltpu.HBM)
    x_lines = [pltpu.VMEM((cx, cy, cz), f32)] * 4
    y_lines = [pltpu.VMEM((cy, cx, cz), f32)] * 4
    pinned = lambda value: pltpu.with_memory_space_constraint(value, pltpu.HBM)
    new_flat, far_field = pl.pallas_call(
        functools.partial(step_kernel, nx, ny, cx, cy, cz, 1.0 / math.sqrt(patches)),
        out_shape=(
            jax.ShapeDtypeStruct((6 * cx * cy, cz), f32),
            jax.ShapeDtypeStruct((12, ANG_DEV), f32),
        ),
        in_specs=[hbm, hbm, smem, vmem, vmem],
        out_specs=(vmem, vmem),
        scratch_shapes=[
            pltpu.VMEM((cx, cy, cz), jnp.int32),
            pltpu.VMEM((6, cx + 2, cy + 2 * TILE, cz), f32),
            pltpu.VMEM((6, (cy + 2) * padded_rows(cx), cz), f32),
            pltpu.VMEM((2, 4, cx, cz), f32),
            pltpu.VMEM((4, cx, cz), f32),
            pltpu.VMEM((4, cx, cz), f32),
            pltpu.VMEM((6, cx, cz), f32),
            pltpu.VMEM((6, cx, cz), f32),
            pltpu.VMEM((cx * cy, cz), f32),
            *x_lines,
            pltpu.VMEM((6, cx, cy, cz), f32),
            pltpu.VMEM((cy, cx, cz), f32),
            *y_lines,
            pltpu.VMEM((6, cy, cx, cz), f32),
            pltpu.VMEM((2 * ANG_DEV, SLOTS * count), jnp.bfloat16),
            pltpu.VMEM((2 * ANG_DEV, SLOTS * count), jnp.bfloat16),
            *[pltpu.VMEM((count, 1, 8 * SLOTS), f32)] * 4,
            pltpu.VMEM((cx * cy * 8, cz), f32),
            pltpu.VMEM((2, patches), jnp.int32),
            pltpu.SMEM((2, patches), jnp.int32),
            pltpu.SemaphoreType.DMA,
            pltpu.SemaphoreType.DMA((2,)),
            pltpu.SemaphoreType.DMA((4, 4)),
            pltpu.SemaphoreType.DMA((2,)),
            pltpu.SemaphoreType.DMA((2,)),
            *line_scratch(nx, cy, cz),
            *line_scratch(ny, cx, cz),
        ],
        compiler_params=pltpu.CompilerParams(
            collective_id=0, has_side_effects=True, vmem_limit_bytes=40 * 2**20),
        name="split_step",
    )(pinned(fields), pinned(material), pinned(permittivity), pinned(patch_cell[None, :]),
      pinned(patch_owner.reshape(1, patches)))
    new_flat, far_field = pl.pallas_call(
        store_kernel,
        out_shape=(
            jax.ShapeDtypeStruct((6 * cx * cy, cz), f32),
            jax.ShapeDtypeStruct((12, ANG_DEV), f32),
        ),
        in_specs=[vmem, vmem],
        out_specs=(hbm, hbm),
        scratch_shapes=[pltpu.SemaphoreType.DMA((2,))],
        compiler_params=pltpu.CompilerParams(vmem_limit_bytes=4 * 2**20),
        name="store",
    )(new_flat, far_field)
    return new_flat.reshape(fields.shape), far_field


def solution(mesh):
    return jax.shard_map(
        functools.partial(local, mesh.shape["gx"], mesh.shape["gy"]),
        mesh=mesh,
        in_specs=(
            P(None, "gx", "gy", None),
            P("gx", "gy", None),
            P(),
            P(("gx", "gy")),
            P(("gx", "gy"), None),
        ),
        out_specs=(P(None, "gx", "gy", None), P(None, ("gx", "gy"))),
        check_vma=False,
    )
```

```python
import functools
import math

import jax
import jax.numpy as jnp
from jax import lax
from jax.experimental import pallas as pl
from jax.experimental.pallas import tpu as pltpu
from jax.sharding import PartitionSpec as P

ANG_DEV = 128
COURANT = 64
KAPPA = 0.5
MESH = pl.DeviceIdType.MESH
X_MEMBERS = (1, 2, 4, 5)
Y_MEMBERS = (0, 2, 3, 5)
Z_MEMBERS = (0, 1, 3, 4)
TILE = 8
HALVES = ((0, 1, 2), (3, 4, 5))
SLOTS = 16


def lane_difference(value):
    lanes = value.shape[1]
    at = lax.broadcasted_iota(jnp.int32, value.shape, 1)
    below = jnp.where(at == 0, 0.0, pltpu.roll(value, 1, 1))
    above = jnp.where(at == lanes - 1, 0.0, pltpu.roll(value, lanes - 1, 1))
    return above - below


def updated(centre, dx, dy, half_curl, half_side):
    dz = {m: lane_difference(centre[m]) for m in Z_MEMBERS}
    curl_h = [dy[5] - dz[4], dz[3] - dx[5], dx[4] - dy[3]]
    curl_e = [dy[2] - dz[1], dz[0] - dx[2], dx[1] - dy[0]]
    return [centre[m] + half_curl * curl_h[m] for m in range(3)] + [
        centre[3 + m] - half_side * curl_e[m] for m in range(3)
    ]


def factor(length, coef_at, gain_ref, pivot_ref, left_ref, right_ref):
    zero = jnp.zeros(gain_ref.shape[1:], jnp.float32)

    def forward(i, carry):
        gain_prev, left_prev = carry
        coef = coef_at(i)
        pivot = 1.0 / (1.0 + 2.0 * coef - coef * gain_prev)
        gain = coef * pivot
        left = gain * left_prev
        gain_ref[i] = gain
        pivot_ref[i] = pivot
        left_ref[i] = left
        return gain, left

    lax.fori_loop(0, length, forward, (zero, jnp.ones_like(zero)), unroll=2)

    def backward(k, carry):
        left_next, right_next = carry
        i = length - 1 - k
        gain = gain_ref[i]
        left = left_ref[i] + gain * left_next
        right = gain * right_next
        left_ref[i] = left
        right_ref[i] = right
        return left, right

    lax.fori_loop(0, length, backward, (zero, jnp.ones_like(zero)), unroll=4)


def sweep_back(length, gain_ref, solved_ref, rows):
    def backward(k, carry):
        i = length - 1 - k
        gain = gain_ref[i, rows]
        now = [solved_ref[m, i, rows] + gain * carry[m] for m in range(6)]
        for m in range(6):
            solved_ref[m, i, rows] = now[m]
        return tuple(now)

    zero = jnp.zeros((TILE, gain_ref.shape[2]), jnp.float32)
    lax.fori_loop(0, length, backward, (zero,) * 6, unroll=4)


def padded_rows(rows):
    return (rows // TILE + 2 | 1) * TILE


def tile_rows(tile):
    return pl.ds(tile * TILE, TILE)


class Line:
    def __init__(self, axis, count, refs):
        (self.mat_out, self.mat_in, self.rhs_out, self.rhs_in, self.plan, self.gains, self.ends,
         self.sent, self.mat_sems, self.rhs_sems) = refs
        self.axis = axis
        self.count = count
        self.steps = count.bit_length() - 1
        self.chunks = self.rhs_out.shape[1]
        self.me = lax.axis_index(axis)

    def near(self, k):
        return 1 - (self.me // 2**k) % 2

    def partner(self, k):
        return {self.axis: self.me + (2 * self.near(k) - 1) * 2**k}

    def mat_copy(self, k):
        return pltpu.make_async_remote_copy(
            self.mat_out.at[k], self.mat_in.at[k], self.sent.at[0], self.mat_sems.at[k],
            device_id=self.partner(k), device_id_type=MESH)

    def rhs_copy(self, k, chunk):
        source, target = self.rhs_out.at[k, chunk], self.rhs_in.at[k, chunk]
        if k == self.steps - 1:
            source, target = source.at[self.near(k)], target.at[0]
        return pltpu.make_async_remote_copy(
            source, target, self.sent.at[1 if k < self.steps - 1 else 2], self.rhs_sems.at[k, chunk],
            device_id=self.partner(k), device_id_type=MESH)

    def mat_start(self, left_ref, right_ref):
        last = left_ref.shape[0] - 1
        for end, at in ((0, 0), (1, last)):
            self.mat_out[0, 2 * end] = left_ref[at]
            self.mat_out[0, 2 * end + 1] = right_ref[at]
        one, zero = jnp.ones(left_ref.shape[1:], jnp.float32), jnp.zeros(left_ref.shape[1:], jnp.float32)
        self.gains[0] = one
        self.gains[1] = zero
        self.gains[2] = zero
        self.gains[3] = one
        self.mat_copy(0).start()

    def mat_merge(self, k):
        self.mat_copy(k).wait_recv()
        n = self.near(k)
        f = 1 - n
        mine = lambda end, side: self.mat_out[k, 2 * end + side]
        other = lambda end, side: self.mat_in[k, 2 * end + side]
        m_nn, m_fn, m_nf, m_ff = mine(n, n), mine(f, n), mine(n, f), mine(f, f)
        o_nn, o_fn, o_nf, o_ff = other(f, f), other(n, f), other(f, n), other(n, n)
        inv = 1.0 / (1.0 - m_nn * o_nn)
        o_by_m = o_nn * m_nf * inv
        o_by_o = o_nf * inv
        m_by_m = m_nf * inv
        m_by_o = m_nn * o_nf * inv
        gain_in, gain_out = self.gains[n], self.gains[2 + n]
        for slot, value in enumerate((inv, o_nn * inv, m_nn * inv, m_fn, o_fn, gain_in, gain_out)):
            self.plan[k, slot] = value
        if k < self.steps - 1:
            self.mat_out[k + 1, 2 * f + f] = m_ff + m_fn * o_by_m
            self.mat_out[k + 1, 2 * f + n] = m_fn * o_by_o
            self.mat_out[k + 1, 2 * n + n] = o_ff + o_fn * m_by_o
            self.mat_out[k + 1, 2 * n + f] = o_fn * m_by_m
            self.mat_copy(k + 1).start()
            self.gains[f] = self.gains[f] + gain_in * o_by_m
            self.gains[2 + f] = self.gains[2 + f] + gain_out * o_by_m
            self.gains[n] = gain_in * o_by_o
            self.gains[2 + n] = gain_out * o_by_o

    def rhs_start(self, tile, half, firsts, lasts):
        chunk = tile * len(HALVES) + half
        for at in range(len(HALVES[half])):
            self.rhs_out[0, chunk, 0, at] = firsts[at]
            self.rhs_out[0, chunk, 1, at] = lasts[at]
        self.rhs_copy(0, chunk).start()

    def rhs_merge(self, k, tile, half):
        chunk = tile * len(HALVES) + half
        rows = tile_rows(tile)
        self.rhs_copy(k, chunk).wait_recv()
        n = self.near(k)
        f = 1 - n
        ending = k == self.steps - 1
        inv, o_nn, m_nn, m_fn, o_fn, gain_in, gain_out = [self.plan[k, slot, rows] for slot in range(7)]
        for at, m in enumerate(HALVES[half]):
            mine = self.rhs_out[k, chunk, n, at]
            other = self.rhs_in[k, chunk, 0, at] if ending else self.rhs_in[k, chunk, f, at]
            o_value = other * inv + o_nn * mine
            if not ending:
                m_value = mine * inv + m_nn * other
                self.rhs_out[k + 1, chunk, f, at] = self.rhs_out[k, chunk, f, at] + m_fn * o_value
                self.rhs_out[k + 1, chunk, n, at] = self.rhs_in[k, chunk, n, at] + o_fn * m_value
            into, out_of = gain_in * o_value, gain_out * o_value
            if k > 0:
                into, out_of = self.ends[0, m, rows] + into, self.ends[1, m, rows] + out_of
            self.ends[0, m, rows] = into
            self.ends[1, m, rows] = out_of
        if not ending:
            self.rhs_copy(k + 1, chunk).start()

    def drain(self):
        early = pl.ds(0, self.steps - 1)
        last = self.steps - 1
        for slot, source, target in (
            (0, self.mat_out, self.mat_in),
            (1, self.rhs_out.at[early], self.rhs_in.at[early]),
            (2, self.rhs_out.at[last, :, 0], self.rhs_in.at[last, :, 0]),
        ):
            pltpu.make_async_remote_copy(
                source, target, self.sent.at[slot], self.mat_sems.at[0],
                device_id=self.partner(0), device_id_type=MESH).wait_send()


def both_ways(axis, count, out_low, out_high, in_low, in_high, sems):
    me = lax.axis_index(axis)
    up = lambda: pltpu.make_async_remote_copy(
        out_high, in_low, sems.at[0], sems.at[1], device_id={axis: me + 1}, device_id_type=MESH)
    down = lambda: pltpu.make_async_remote_copy(
        out_low, in_high, sems.at[2], sems.at[3], device_id={axis: me - 1}, device_id_type=MESH)

    def start_up():
        @pl.when(me < count - 1)
        def _():
            up().start()

        @pl.when(me == 0)
        def _():
            in_low[...] = jnp.zeros(in_low.shape, jnp.float32)

    def start_down():
        @pl.when(me > 0)
        def _():
            down().start()

        @pl.when(me == count - 1)
        def _():
            in_high[...] = jnp.zeros(in_high.shape, jnp.float32)

    def wait():
        @pl.when(me > 0)
        def _():
            up().wait_recv()

        @pl.when(me < count - 1)
        def _():
            down().wait_recv()

    def drain():
        @pl.when(me < count - 1)
        def _():
            up().wait_send()

        @pl.when(me > 0)
        def _():
            down().wait_send()

    return start_up, start_down, wait, drain


def in_fours(count, act):
    head = (count - 1) % 4
    for k in range(1, 1 + head):
        act(k)

    def four(g, carry):
        for u in range(4):
            act(1 + head + 4 * g + u)
        return carry

    lax.fori_loop(0, (count - 1) // 4, four, 0)


def greet_all(count, ny, me, barrier):
    def hello(k):
        to = lax.rem(me + k, count)
        pl.semaphore_signal(
            barrier, inc=1, device_id=(lax.div(to, ny), lax.rem(to, ny)), device_id_type=MESH)

    def pair(i):
        hello(i)
        hello(count - i)

    in_fours(count // 2, pair)
    hello(count // 2)


def cos_sin(angle):
    turns = jnp.floor(angle * (2.0 / math.pi) + 0.5)
    rest = ((angle - turns * 1.5703125) - turns * 4.837512969970703125e-4) - turns * 7.54978995489188216e-8
    square = rest * rest
    sine = ((-1.9515295891e-4 * square + 8.3321608736e-3) * square - 1.6666654611e-1) * square * rest + rest
    cosine = (
        (2.443315711809948e-5 * square - 1.388731625493765e-3) * square + 4.166664568298827e-2
    ) * square * square - 0.5 * square + 1.0
    quarter = turns.astype(jnp.int32) & 3
    swap = (quarter & 1) == 1
    plain_cos = jnp.where(swap, sine, cosine)
    plain_sin = jnp.where(swap, cosine, sine)
    minus_cos = (quarter == 1) | (quarter == 2)
    return jnp.where(minus_cos, -plain_cos, plain_cos), jnp.where(quarter >= 2, -plain_sin, plain_sin)


def split_bf16(value):
    high = value.astype(jnp.bfloat16)
    return high, (value - high.astype(jnp.float32)).astype(jnp.bfloat16)


def dot_rows(left, right):
    return lax.dot_general(left, right, (((1,), (1,)), ((), ())), preferred_element_type=jnp.float32)


def slot_ranks(count, owner):
    patches = owner.shape[1]
    hot = lax.broadcasted_iota(jnp.int32, (count, patches), 0) == owner
    before = lax.broadcasted_iota(jnp.int32, (patches, patches), 0) < lax.broadcasted_iota(
        jnp.int32, (patches, patches), 1)
    as_bf16 = lambda mask: jnp.where(mask, 1.0, 0.0).astype(jnp.bfloat16)
    ahead = lax.dot_general(as_bf16(hot), as_bf16(before), (((1,), (0,)), ((), ())),
                            preferred_element_type=jnp.float32)
    rank = jnp.sum(jnp.where(hot, ahead, 0.0), axis=0, keepdims=True)
    return as_bf16(hot), rank.astype(jnp.int32)


def by_owner(hot, rank, values):
    slots = lax.broadcasted_iota(jnp.int32, (SLOTS, rank.shape[1]), 0) == rank
    rows = [jnp.where(slots, value, 0.0) for value in values]
    rows += [jnp.zeros_like(rows[0])] * (8 - len(rows))
    high, low = split_bf16(jnp.concatenate(rows, axis=0))
    both = dot_rows(hot, jnp.concatenate([high, low], axis=0))
    return both[:, :8 * SLOTS] + both[:, 8 * SLOTS:]


def fields_on_rows(landed_ref):
    count, _, lanes = landed_ref.shape
    row = lax.broadcasted_iota(jnp.int32, (8, lanes), 0)
    block = lax.shift_right_logical(
        lax.broadcasted_iota(jnp.int32, (8, lanes), 1), jnp.full((8, lanes), SLOTS.bit_length() - 1, jnp.int32))
    groups = []
    for g in range(count // 8):
        value = jnp.concatenate([landed_ref[g * 8 + i] for i in range(8)], axis=0)
        for bit in (1, 2, 4):
            later = pltpu.roll(pltpu.roll(value, 8 - bit, 0), SLOTS * bit, 1)
            sooner = pltpu.roll(pltpu.roll(value, bit, 0), lanes - SLOTS * bit, 1)
            row_bit, block_bit = row & bit, block & bit
            value = jnp.where(row_bit == block_bit, value, jnp.where(row_bit == 0, later, sooner))
        groups.append(value)
    return jnp.concatenate(groups, axis=1)


def fill_weights(count, me, places, high_ref, low_ref):
    angles = high_ref.shape[0] // 2
    slots = places.shape[1]
    azimuth = jnp.full((16, 128), me.astype(jnp.float32) * (2.0 * math.pi / count))
    cos_phi, sin_phi = cos_sin(azimuth)
    pos = [jnp.broadcast_to(places[c:c + 1], (16, slots)) for c in range(3)]

    def group(g, carry):
        start = pl.multiple_of(g * 16, 16)
        index = (lax.broadcasted_iota(jnp.int32, (16, 128), 0) + start).astype(jnp.float32)
        cos_theta, sin_theta = cos_sin(math.pi * (index + 0.5) / angles)
        for part in range(0, slots, 128):
            at = slice(part, part + 128)
            phase = KAPPA * (pos[0][:, at] * sin_theta * cos_phi + pos[1][:, at] * sin_theta * sin_phi
                             + pos[2][:, at] * cos_theta)
            for s, value in enumerate(cos_sin(phase)):
                high, low = split_bf16(value)
                rows = pl.ds(pl.multiple_of(start + s * angles, 16), 16)
                high_ref[rows, at] = high
                low_ref[rows, at] = low
        return carry

    lax.fori_loop(0, angles // 16, group, 0)


def to_owners(count, ny, me, out_ref, landed_ref, sems):
    def copy(k):
        to = lax.rem(me + k, count)
        return pltpu.make_async_remote_copy(
            out_ref.at[to], landed_ref.at[me], sems.at[0], sems.at[1],
            device_id=(lax.div(to, ny), lax.rem(to, ny)), device_id_type=MESH)

    def start(rows):
        for i in range(count):
            out_ref[i] = rows[i:i + 1]
        landed_ref[me] = out_ref[me]
        in_fours(count, lambda k: copy(k).start())

    others = pl.ds(0, count - 1)
    whole = pltpu.make_async_remote_copy(
        out_ref.at[others], landed_ref.at[others], sems.at[0], sems.at[1],
        device_id=(me // ny, me % ny), device_id_type=MESH)
    return start, whole.wait_recv, whole.wait_send


def step_kernel(nx, ny, cx, cy, cz, scale, fields_hbm, material_hbm, permit_ref,
                cell_row, owner_row, out_ref, far_ref, material_ref,
                grid_x, grid_y, y_out, y_low, y_high, mid_low, mid_high, coef_x,
                gain_x, pivot_x, left_x, right_x, solved_x,
                coef_y, gain_y, pivot_y, left_y, right_y, solved_y,
                weight_high, weight_low, place_out, place_in, value_out, value_in, packed, spots, spots_smem,
                load_sem, move_sems, halo_sems, place_sems, value_sems, *line_refs):
    half_step = COURANT / 2.0
    half_side = 0.5 * half_step
    count = nx * ny
    wide = padded_rows(cx)
    tiles_x, tiles_y = cy // TILE, cx // TILE
    me = lax.axis_index("gx") * ny + lax.axis_index("gy")
    barrier = pltpu.get_barrier_semaphore()
    inner = grid_x.at[:, pl.ds(1, cx), pl.ds(TILE, cy)]
    load = pltpu.make_async_copy(fields_hbm, inner, load_sem)
    for m in range(6):
        pltpu.make_async_copy(fields_hbm.at[m], inner.at[m], load_sem).start()
    load_material = pltpu.make_async_copy(material_hbm, material_ref, move_sems.at[0])
    load_material.start()
    greet_all(count, ny, me, barrier)
    line_x = Line("gx", nx, line_refs[:10])
    line_y = Line("gy", ny, line_refs[10:])

    def x_halo(first, sems):
        plane = lambda i: grid_x.at[pl.ds(first, 2), i, pl.ds(TILE, cy)]
        return both_ways("gx", nx, plane(1), plane(cx), plane(0), plane(cx + 1), sems)

    mid_plane = lambda j: grid_y.at[:, pl.ds((j + 1) * wide + TILE, cx)]
    first_halos = [
        both_ways("gy", ny, y_out.at[0], y_out.at[1], y_low, y_high, halo_sems.at[0]),
        x_halo(1, halo_sems.at[1]),
        x_halo(4, halo_sems.at[2]),
    ]
    mid_halo = both_ways("gy", ny, mid_plane(0), mid_plane(cy - 1), mid_low, mid_high, halo_sems.at[3])

    def coefs(i, carry):
        which = material_ref[i]
        permit = jnp.zeros(which.shape, jnp.float32)
        for entry in range(permit_ref.shape[0]):
            permit = jnp.where(which == entry, permit_ref[entry], permit)
        coef_x[pl.ds(pl.multiple_of(i * cy, 8), cy), :] = (half_step * half_step) / permit
        return carry

    load.wait()
    for slot, member in enumerate(Y_MEMBERS):
        for end, row in ((0, TILE), (1, TILE + cy - 1)):
            y_out[end, slot] = jnp.concatenate(
                [grid_x[member, 1 + i, row:row + 1] for i in range(cx)], axis=0)
    pl.semaphore_wait(barrier, count - 1)
    for halo in first_halos:
        halo[0]()
        halo[1]()
    load_material.wait()
    lax.fori_loop(0, cx, coefs, 0, unroll=2)
    coef_plane = lambda i: coef_x[pl.ds(pl.multiple_of(i * cy, 8), cy), :]
    factor(cx, coef_plane, gain_x, pivot_x, left_x, right_x)
    line_x.mat_start(left_x, right_x)
    for j in range(cy):
        coef_y[j] = coef_x[pl.ds(j, cx, stride=cy), :]
    for m in range(6):
        for plane in (0, cy + 1):
            grid_y[m, pl.ds(plane * wide, wide), :] = jnp.zeros((wide, cz), jnp.float32)
    patches = cell_row.shape[1]
    cell = cell_row[...]
    line = lax.shift_right_logical(cell, jnp.full_like(cell, cz.bit_length() - 1))
    at_x = jnp.zeros_like(cell)
    for i in range(1, cx):
        at_x = at_x + jnp.where(line >= i * cy, 1, 0)
    at_y, at_z = line - at_x * cy, cell - line * cz
    lanes = lax.broadcasted_iota(jnp.int32, cell.shape, 1)
    spots[0:1] = (at_y * cx + at_x) * 8
    spots[1:2] = (lanes - at_z) & (cz - 1)
    find = pltpu.make_async_copy(spots, spots_smem, move_sems.at[1])
    find.start()
    places = [at_x + lax.axis_index("gx") * cx, at_y + lax.axis_index("gy") * cy, at_z]
    hot, rank = slot_ranks(count, owner_row[...])
    place_send = to_owners(count, ny, me, place_out, place_in, place_sems)
    value_send = to_owners(count, ny, me, value_out, value_in, value_sems)
    place_send[0](by_owner(hot, rank, [place.astype(jnp.float32) for place in places]))
    factor(cy, lambda j: coef_y[j], gain_y, pivot_y, left_y, right_y)
    line_y.mat_start(left_y, right_y)
    for halo in first_halos:
        halo[2]()

    def solve_x(tile):
        row = (tile + 1) * TILE
        for at, side, need in ((TILE - 1, y_low, tile == 0), (TILE + cy, y_high, tile == tiles_x - 1)):
            for slot, member in enumerate(Y_MEMBERS if need else ()):
                for i in range(cx):
                    grid_x[member, i + 1, at:at + 1] = side[slot, i:i + 1]

        def forward(i, carry):
            near = lambda m, plane, shift: grid_x[m, i + 1 + plane, row + shift:row + shift + TILE]
            centre = [near(m, 0, 0) for m in range(6)]
            dx = {m: near(m, 1, 0) - near(m, -1, 0) for m in X_MEMBERS}
            dy = {m: near(m, 0, 1) - near(m, 0, -1) for m in Y_MEMBERS}
            coef = coef_x[pl.ds(pl.multiple_of(i * cy + tile * TILE, 8), TILE), :]
            right = updated(centre, dx, dy, coef * (0.5 / half_step), half_side)
            gain, pivot = gain_x[i, tile_rows(tile)], pivot_x[i, tile_rows(tile)]
            now = [right[m] * pivot + gain * carry[m] for m in range(6)]
            for m in range(6):
                solved_x[m, i, tile_rows(tile)] = now[m]
            return tuple(now)

        lax.fori_loop(0, cx, forward, (jnp.zeros((TILE, cz), jnp.float32),) * 6, unroll=8)
        sweep_back(cx, gain_x, solved_x, tile_rows(tile))
        for half, members in enumerate(HALVES):
            line_x.rhs_start(tile, half, [solved_x[m, 0, tile_rows(tile)] for m in members],
                             [solved_x[m, cx - 1, tile_rows(tile)] for m in members])

    def finish_x(tile):
        rows = tile_rows(tile)
        planes = lambda i: pl.ds((tile * TILE + 1) * wide + TILE + i, TILE, stride=wide)
        ends = [[line_x.ends[end, m, rows] for m in range(6)] for end in range(2)]
        for m in range(6):
            grid_y[m, planes(-1), :] = ends[0][m]
            grid_y[m, planes(cx), :] = ends[1][m]
        for i in range(cx):
            left, right = left_x[i, rows], right_x[i, rows]
            for m in range(6):
                grid_y[m, planes(i), :] = solved_x[m, i, rows] + left * ends[0][m] + right * ends[1][m]

    def forward_y(j, carry):
        near = lambda m, plane, shift: grid_y[m, pl.ds((j + 1 + plane) * wide + TILE + shift, cx), :]
        centre = [near(m, 0, 0) for m in range(6)]
        dx = {m: near(m, 0, 1) - near(m, 0, -1) for m in X_MEMBERS}
        dy = {m: near(m, 1, 0) - near(m, -1, 0) for m in Y_MEMBERS}
        right = updated(centre, dx, dy, coef_y[j] * (0.5 / half_step), half_side)
        gain, pivot = gain_y[j], pivot_y[j]
        now = [right[m] * pivot + gain * carry[m] for m in range(6)]
        for m in range(6):
            solved_y[m, j] = now[m]
        return tuple(now)

    order = [0, tiles_x - 1] + list(range(1, tiles_x - 1))
    for place, tile in enumerate(order):
        solve_x(tile)
        if place == 1:
            line_x.mat_merge(0)
    place_send[1]()
    fill_weights(count, me, fields_on_rows(place_in), weight_high, weight_low)
    chunks = [(tile, half) for tile in order for half in range(len(HALVES))]
    for k in range(line_x.steps - 1):
        for place, chunk in enumerate(chunks):
            line_x.rhs_merge(k, *chunk)
            if place == 1 and k + 1 < line_x.steps - 1:
                line_x.mat_merge(k + 1)
        if k < line_y.steps:
            line_y.mat_merge(k)
    if line_x.steps > 1:
        line_x.mat_merge(line_x.steps - 1)
    for k in range(line_x.steps - 1, line_y.steps):
        line_y.mat_merge(k)
    carry = (jnp.zeros((cx, cz), jnp.float32),) * 6
    for tile in order:
        for half in range(len(HALVES)):
            line_x.rhs_merge(line_x.steps - 1, tile, half)
        finish_x(tile)
        if tile == 0:
            mid_halo[1]()
            carry = lax.fori_loop(0, TILE - 2, forward_y, carry, unroll=6)
        if tile == tiles_x - 1:
            mid_halo[0]()
    lax.fori_loop(TILE - 2, cy, forward_y, carry, unroll=6)
    for tile in range(tiles_y):
        sweep_back(cy, gain_y, solved_y, tile_rows(tile))
    mid_halo[2]()

    def ghosts(tile):
        rows = tile_rows(tile)
        found = []
        for ref, at, sign in ((mid_low, 0, 1.0), (mid_high, cy - 1, -1.0)):
            side = sign * half_side / coef_y[at, rows]
            found.append({
                0: ref[5, rows] * (-sign * 0.5 / half_step),
                2: ref[3, rows] * (sign * 0.5 / half_step),
                3: ref[2, rows] * side,
                5: ref[0, rows] * -side,
            })
        return found

    added = [ghosts(tile) for tile in range(tiles_y)]
    for tile in range(tiles_y):
        rows = tile_rows(tile)
        low, high = added[tile]

        def outer(m, at):
            value = solved_y[m, at, rows]
            return value + left_y[at, rows] * low[m] + right_y[at, rows] * high[m] if m in low else value

        for half, members in enumerate(HALVES):
            line_y.rhs_start(tile, half, [outer(m, 0) for m in members], [outer(m, cy - 1) for m in members])
    for k in range(line_y.steps):
        for tile in range(tiles_y):
            for half in range(len(HALVES)):
                line_y.rhs_merge(k, tile, half)
            if k == line_y.steps - 1:
                rows = tile_rows(tile)
                ends = [[line_y.ends[end, m, rows] + added[tile][end][m] if m in added[tile][end]
                         else line_y.ends[end, m, rows] for m in range(6)] for end in range(2)]
                for j in range(cy):
                    left, right = left_y[j, rows], right_y[j, rows]
                    for m in range(6):
                        value = solved_y[m, j, rows] + left * ends[0][m] + right * ends[1][m]
                        out_ref[pl.ds((m * cx + tile * TILE) * cy + j, TILE, stride=cy), :] = value
                        packed[pl.ds((j * cx + tile * TILE) * 8 + m, TILE, stride=8), :] = value

    lane = lax.broadcasted_iota(jnp.int32, (8, cz), 1)
    find.wait()
    found = []
    for first in range(0, patches, cz):
        kept = jnp.zeros((8, cz), jnp.float32)
        for at in range(cz):
            rows = packed[pl.ds(spots_smem[0, first + at], 8), :]
            kept = jnp.where(lane == at, pltpu.roll(rows, spots_smem[1, first + at], 1), kept)
        found.append(kept)
    values = jnp.concatenate(found, axis=1)
    value_send[0](by_owner(hot, rank, [values[m:m + 1] for m in range(6)]))
    for halo in [*first_halos, mid_halo]:
        halo[3]()
    line_x.drain()
    line_y.drain()
    place_send[2]()
    value_send[1]()
    high, low = split_bf16(fields_on_rows(value_in))
    both = jnp.concatenate([high, low], axis=0)
    product = dot_rows(both, weight_high[...]) + dot_rows(both, weight_low[...])
    product = (product[:8] + product[8:]) * scale
    angles = far_ref.shape[1]
    for s in range(2):
        far_ref[pl.ds(s * 6, 6), :] = product[:6, s * angles:(s + 1) * angles]
    value_send[2]()


def store_kernel(new_ref, far_ref, new_hbm, far_hbm, sems):
    rows = new_ref.shape[0] // 6
    for m in range(6):
        part = pl.ds(m * rows, rows)
        pltpu.make_async_copy(new_ref.at[part], new_hbm.at[part], sems.at[0]).start()
    far = pltpu.make_async_copy(far_ref, far_hbm, sems.at[1])
    far.start()
    pltpu.make_async_copy(new_ref, new_hbm, sems.at[0]).wait()
    far.wait()


def line_scratch(count, rows, lanes):
    steps = count.bit_length() - 1
    chunks = rows // TILE * len(HALVES)
    f32 = jnp.float32
    return [
        pltpu.VMEM((steps, 4, rows, lanes), f32),
        pltpu.VMEM((steps, 4, rows, lanes), f32),
        pltpu.VMEM((steps, chunks, 2, len(HALVES[0]), TILE, lanes), f32),
        pltpu.VMEM((steps, chunks, 2, len(HALVES[0]), TILE, lanes), f32),
        pltpu.VMEM((steps, 7, rows, lanes), f32),
        pltpu.VMEM((4, rows, lanes), f32),
        pltpu.VMEM((2, 6, rows, lanes), f32),
        pltpu.SemaphoreType.DMA((3,)),
        pltpu.SemaphoreType.DMA((steps,)),
        pltpu.SemaphoreType.DMA((steps, chunks)),
    ]


def local(nx, ny, fields, material, permittivity, patch_cell, patch_owner):
    _, cx, cy, cz = fields.shape
    f32 = jnp.float32
    count = nx * ny
    patches = patch_cell.shape[0]
    vmem = pl.BlockSpec(memory_space=pltpu.VMEM)
    smem = pl.BlockSpec(memory_space=pltpu.SMEM)
    hbm = pl.BlockSpec(memory_space=pltpu.HBM)
    x_lines = [pltpu.VMEM((cx, cy, cz), f32)] * 4
    y_lines = [pltpu.VMEM((cy, cx, cz), f32)] * 4
    pinned = lambda value: pltpu.with_memory_space_constraint(value, pltpu.HBM)
    new_flat, far_field = pl.pallas_call(
        functools.partial(step_kernel, nx, ny, cx, cy, cz, 1.0 / math.sqrt(patches)),
        out_shape=(
            jax.ShapeDtypeStruct((6 * cx * cy, cz), f32),
            jax.ShapeDtypeStruct((12, ANG_DEV), f32),
        ),
        in_specs=[hbm, hbm, smem, vmem, vmem],
        out_specs=(vmem, vmem),
        scratch_shapes=[
            pltpu.VMEM((cx, cy, cz), jnp.int32),
            pltpu.VMEM((6, cx + 2, cy + 2 * TILE, cz), f32),
            pltpu.VMEM((6, (cy + 2) * padded_rows(cx), cz), f32),
            pltpu.VMEM((2, 4, cx, cz), f32),
            pltpu.VMEM((4, cx, cz), f32),
            pltpu.VMEM((4, cx, cz), f32),
            pltpu.VMEM((6, cx, cz), f32),
            pltpu.VMEM((6, cx, cz), f32),
            pltpu.VMEM((cx * cy, cz), f32),
            *x_lines,
            pltpu.VMEM((6, cx, cy, cz), f32),
            pltpu.VMEM((cy, cx, cz), f32),
            *y_lines,
            pltpu.VMEM((6, cy, cx, cz), f32),
            pltpu.VMEM((2 * ANG_DEV, SLOTS * count), jnp.bfloat16),
            pltpu.VMEM((2 * ANG_DEV, SLOTS * count), jnp.bfloat16),
            *[pltpu.VMEM((count, 1, 8 * SLOTS), f32)] * 4,
            pltpu.VMEM((cx * cy * 8, cz), f32),
            pltpu.VMEM((2, patches), jnp.int32),
            pltpu.SMEM((2, patches), jnp.int32),
            pltpu.SemaphoreType.DMA,
            pltpu.SemaphoreType.DMA((2,)),
            pltpu.SemaphoreType.DMA((4, 4)),
            pltpu.SemaphoreType.DMA((2,)),
            pltpu.SemaphoreType.DMA((2,)),
            *line_scratch(nx, cy, cz),
            *line_scratch(ny, cx, cz),
        ],
        compiler_params=pltpu.CompilerParams(
            collective_id=0, has_side_effects=True, vmem_limit_bytes=40 * 2**20),
        name="split_step",
    )(pinned(fields), pinned(material), pinned(permittivity), pinned(patch_cell[None, :]),
      pinned(patch_owner.reshape(1, patches)))
    new_flat, far_field = pl.pallas_call(
        store_kernel,
        out_shape=(
            jax.ShapeDtypeStruct((6 * cx * cy, cz), f32),
            jax.ShapeDtypeStruct((12, ANG_DEV), f32),
        ),
        in_specs=[vmem, vmem],
        out_specs=(hbm, hbm),
        scratch_shapes=[pltpu.SemaphoreType.DMA((2,))],
        compiler_params=pltpu.CompilerParams(vmem_limit_bytes=4 * 2**20),
        name="store",
    )(new_flat, far_field)
    return new_flat.reshape(fields.shape), far_field


def solution(mesh):
    return jax.shard_map(
        functools.partial(local, mesh.shape["gx"], mesh.shape["gy"]),
        mesh=mesh,
        in_specs=(
            P(None, "gx", "gy", None),
            P("gx", "gy", None),
            P(),
            P(("gx", "gy")),
            P(("gx", "gy"), None),
        ),
        out_specs=(P(None, "gx", "gy", None), P(None, ("gx", "gy"))),
        check_vma=False,
    )
```

```python
import functools
import math

import jax
import jax.numpy as jnp
from jax import lax
from jax.experimental import pallas as pl
from jax.experimental.pallas import tpu as pltpu
from jax.sharding import PartitionSpec as P

ANG_DEV = 128
COURANT = 64
KAPPA = 0.5
MESH = pl.DeviceIdType.MESH
X_MEMBERS = (1, 2, 4, 5)
Y_MEMBERS = (0, 2, 3, 5)
Z_MEMBERS = (0, 1, 3, 4)
TILE = 8
HALVES = ((0, 1, 2), (3, 4, 5))
SLOTS = 16


def lane_difference(value):
    lanes = value.shape[1]
    at = lax.broadcasted_iota(jnp.int32, value.shape, 1)
    below = jnp.where(at == 0, 0.0, pltpu.roll(value, 1, 1))
    above = jnp.where(at == lanes - 1, 0.0, pltpu.roll(value, lanes - 1, 1))
    return above - below


def updated(centre, dx, dy, half_curl, half_side):
    dz = {m: lane_difference(centre[m]) for m in Z_MEMBERS}
    curl_h = [dy[5] - dz[4], dz[3] - dx[5], dx[4] - dy[3]]
    curl_e = [dy[2] - dz[1], dz[0] - dx[2], dx[1] - dy[0]]
    return [centre[m] + half_curl * curl_h[m] for m in range(3)] + [
        centre[3 + m] - half_side * curl_e[m] for m in range(3)
    ]


def factor(length, coef_at, gain_ref, pivot_ref, left_ref, right_ref):
    zero = jnp.zeros(gain_ref.shape[1:], jnp.float32)

    def forward(i, carry):
        gain_prev, left_prev = carry
        coef = coef_at(i)
        pivot = 1.0 / (1.0 + 2.0 * coef - coef * gain_prev)
        gain = coef * pivot
        left = gain * left_prev
        gain_ref[i] = gain
        pivot_ref[i] = pivot
        left_ref[i] = left
        return gain, left

    lax.fori_loop(0, length, forward, (zero, jnp.ones_like(zero)), unroll=2)

    def backward(k, carry):
        left_next, right_next = carry
        i = length - 1 - k
        gain = gain_ref[i]
        left = left_ref[i] + gain * left_next
        right = gain * right_next
        left_ref[i] = left
        right_ref[i] = right
        return left, right

    lax.fori_loop(0, length, backward, (zero, jnp.ones_like(zero)), unroll=4)


def sweep_back(length, gain_ref, solved_ref, rows):
    def backward(k, carry):
        i = length - 1 - k
        gain = gain_ref[i, rows]
        now = [solved_ref[m, i, rows] + gain * carry[m] for m in range(6)]
        for m in range(6):
            solved_ref[m, i, rows] = now[m]
        return tuple(now)

    zero = jnp.zeros((TILE, gain_ref.shape[2]), jnp.float32)
    lax.fori_loop(0, length, backward, (zero,) * 6, unroll=4)


def padded_rows(rows):
    return (rows // TILE + 2 | 1) * TILE


def tile_rows(tile):
    return pl.ds(tile * TILE, TILE)


class Line:
    def __init__(self, axis, count, refs):
        (self.mat_out, self.mat_in, self.rhs_out, self.rhs_in, self.plan, self.gains, self.ends,
         self.sent, self.mat_sems, self.rhs_sems) = refs
        self.axis = axis
        self.count = count
        self.steps = count.bit_length() - 1
        self.chunks = self.rhs_out.shape[1]
        self.me = lax.axis_index(axis)

    def near(self, k):
        return 1 - (self.me // 2**k) % 2

    def partner(self, k):
        return {self.axis: self.me + (2 * self.near(k) - 1) * 2**k}

    def mat_copy(self, k):
        return pltpu.make_async_remote_copy(
            self.mat_out.at[k], self.mat_in.at[k], self.sent.at[0], self.mat_sems.at[k],
            device_id=self.partner(k), device_id_type=MESH)

    def rhs_copy(self, k, chunk):
        source, target = self.rhs_out.at[k, chunk], self.rhs_in.at[k, chunk]
        if k == self.steps - 1:
            source, target = source.at[self.near(k)], target.at[0]
        return pltpu.make_async_remote_copy(
            source, target, self.sent.at[1 if k < self.steps - 1 else 2], self.rhs_sems.at[k, chunk],
            device_id=self.partner(k), device_id_type=MESH)

    def mat_start(self, left_ref, right_ref):
        last = left_ref.shape[0] - 1
        for end, at in ((0, 0), (1, last)):
            self.mat_out[0, 2 * end] = left_ref[at]
            self.mat_out[0, 2 * end + 1] = right_ref[at]
        one, zero = jnp.ones(left_ref.shape[1:], jnp.float32), jnp.zeros(left_ref.shape[1:], jnp.float32)
        self.gains[0] = one
        self.gains[1] = zero
        self.gains[2] = zero
        self.gains[3] = one
        self.mat_copy(0).start()

    def mat_merge(self, k):
        self.mat_copy(k).wait_recv()
        n = self.near(k)
        f = 1 - n
        mine = lambda end, side: self.mat_out[k, 2 * end + side]
        other = lambda end, side: self.mat_in[k, 2 * end + side]
        m_nn, m_fn, m_nf, m_ff = mine(n, n), mine(f, n), mine(n, f), mine(f, f)
        o_nn, o_fn, o_nf, o_ff = other(f, f), other(n, f), other(f, n), other(n, n)
        inv = 1.0 / (1.0 - m_nn * o_nn)
        o_by_m = o_nn * m_nf * inv
        o_by_o = o_nf * inv
        m_by_m = m_nf * inv
        m_by_o = m_nn * o_nf * inv
        gain_in, gain_out = self.gains[n], self.gains[2 + n]
        for slot, value in enumerate((inv, o_nn * inv, m_nn * inv, m_fn, o_fn, gain_in, gain_out)):
            self.plan[k, slot] = value
        if k < self.steps - 1:
            self.mat_out[k + 1, 2 * f + f] = m_ff + m_fn * o_by_m
            self.mat_out[k + 1, 2 * f + n] = m_fn * o_by_o
            self.mat_out[k + 1, 2 * n + n] = o_ff + o_fn * m_by_o
            self.mat_out[k + 1, 2 * n + f] = o_fn * m_by_m
            self.mat_copy(k + 1).start()
            self.gains[f] = self.gains[f] + gain_in * o_by_m
            self.gains[2 + f] = self.gains[2 + f] + gain_out * o_by_m
            self.gains[n] = gain_in * o_by_o
            self.gains[2 + n] = gain_out * o_by_o

    def rhs_start(self, tile, half, firsts, lasts):
        chunk = tile * len(HALVES) + half
        for at in range(len(HALVES[half])):
            self.rhs_out[0, chunk, 0, at] = firsts[at]
            self.rhs_out[0, chunk, 1, at] = lasts[at]
        self.rhs_copy(0, chunk).start()

    def rhs_merge(self, k, tile, half):
        chunk = tile * len(HALVES) + half
        rows = tile_rows(tile)
        self.rhs_copy(k, chunk).wait_recv()
        n = self.near(k)
        f = 1 - n
        ending = k == self.steps - 1
        inv, o_nn, m_nn, m_fn, o_fn, gain_in, gain_out = [self.plan[k, slot, rows] for slot in range(7)]
        for at, m in enumerate(HALVES[half]):
            mine = self.rhs_out[k, chunk, n, at]
            other = self.rhs_in[k, chunk, 0, at] if ending else self.rhs_in[k, chunk, f, at]
            o_value = other * inv + o_nn * mine
            if not ending:
                m_value = mine * inv + m_nn * other
                self.rhs_out[k + 1, chunk, f, at] = self.rhs_out[k, chunk, f, at] + m_fn * o_value
                self.rhs_out[k + 1, chunk, n, at] = self.rhs_in[k, chunk, n, at] + o_fn * m_value
            into, out_of = gain_in * o_value, gain_out * o_value
            if k > 0:
                into, out_of = self.ends[0, m, rows] + into, self.ends[1, m, rows] + out_of
            self.ends[0, m, rows] = into
            self.ends[1, m, rows] = out_of
        if not ending:
            self.rhs_copy(k + 1, chunk).start()

    def known_ends(self, tile, m):
        k, rows = self.steps - 1, tile_rows(tile)
        scaled = self.plan[k, 1, rows] * self.near_value(tile, m)
        ends = [self.plan[k, 5 + end, rows] * scaled for end in range(2)]
        return [self.ends[end, m, rows] + ends[end] for end in range(2)] if k > 0 else ends

    def place_of(self, tile, m):
        half = next(h for h, members in enumerate(HALVES) if m in members)
        return tile * len(HALVES) + half, HALVES[half].index(m)

    def near_value(self, tile, m):
        k = self.steps - 1
        chunk, at = self.place_of(tile, m)
        return self.rhs_out[k, chunk, self.near(k), at]

    def far_values(self, tile):
        k = self.steps - 1
        for half in range(len(HALVES)):
            self.rhs_copy(k, tile * len(HALVES) + half).wait_recv()
        found = []
        for m in range(6):
            chunk, at = self.place_of(tile, m)
            found.append(self.rhs_in[k, chunk, 0, at])
        return found

    def drain(self):
        early = pl.ds(0, self.steps - 1)
        last = self.steps - 1
        for slot, source, target in (
            (0, self.mat_out, self.mat_in),
            (1, self.rhs_out.at[early], self.rhs_in.at[early]),
            (2, self.rhs_out.at[last, :, 0], self.rhs_in.at[last, :, 0]),
        ):
            pltpu.make_async_remote_copy(
                source, target, self.sent.at[slot], self.mat_sems.at[0],
                device_id=self.partner(0), device_id_type=MESH).wait_send()


def both_ways(axis, count, out_low, out_high, in_low, in_high, sems):
    me = lax.axis_index(axis)
    up = lambda: pltpu.make_async_remote_copy(
        out_high, in_low, sems.at[0], sems.at[1], device_id={axis: me + 1}, device_id_type=MESH)
    down = lambda: pltpu.make_async_remote_copy(
        out_low, in_high, sems.at[2], sems.at[3], device_id={axis: me - 1}, device_id_type=MESH)

    def start_up():
        @pl.when(me < count - 1)
        def _():
            up().start()

        @pl.when(me == 0)
        def _():
            in_low[...] = jnp.zeros(in_low.shape, jnp.float32)

    def start_down():
        @pl.when(me > 0)
        def _():
            down().start()

        @pl.when(me == count - 1)
        def _():
            in_high[...] = jnp.zeros(in_high.shape, jnp.float32)

    def wait():
        @pl.when(me > 0)
        def _():
            up().wait_recv()

        @pl.when(me < count - 1)
        def _():
            down().wait_recv()

    def drain():
        @pl.when(me < count - 1)
        def _():
            up().wait_send()

        @pl.when(me > 0)
        def _():
            down().wait_send()

    return start_up, start_down, wait, drain


def in_fours(count, act):
    head = (count - 1) % 4
    for k in range(1, 1 + head):
        act(k)

    def four(g, carry):
        for u in range(4):
            act(1 + head + 4 * g + u)
        return carry

    lax.fori_loop(0, (count - 1) // 4, four, 0)


def greet_all(count, ny, me, barrier):
    def hello(k):
        to = lax.rem(me + k, count)
        pl.semaphore_signal(
            barrier, inc=1, device_id=(lax.div(to, ny), lax.rem(to, ny)), device_id_type=MESH)

    def pair(i):
        hello(i)
        hello(count - i)

    in_fours(count // 2, pair)
    hello(count // 2)


def cos_sin(angle):
    turns = jnp.floor(angle * (2.0 / math.pi) + 0.5)
    rest = ((angle - turns * 1.5703125) - turns * 4.837512969970703125e-4) - turns * 7.54978995489188216e-8
    square = rest * rest
    sine = ((-1.9515295891e-4 * square + 8.3321608736e-3) * square - 1.6666654611e-1) * square * rest + rest
    cosine = (
        (2.443315711809948e-5 * square - 1.388731625493765e-3) * square + 4.166664568298827e-2
    ) * square * square - 0.5 * square + 1.0
    quarter = turns.astype(jnp.int32) & 3
    swap = (quarter & 1) == 1
    plain_cos = jnp.where(swap, sine, cosine)
    plain_sin = jnp.where(swap, cosine, sine)
    minus_cos = (quarter == 1) | (quarter == 2)
    return jnp.where(minus_cos, -plain_cos, plain_cos), jnp.where(quarter >= 2, -plain_sin, plain_sin)


def split_bf16(value):
    high = value.astype(jnp.bfloat16)
    return high, (value - high.astype(jnp.float32)).astype(jnp.bfloat16)


def dot_rows(left, right):
    return lax.dot_general(left, right, (((1,), (1,)), ((), ())), preferred_element_type=jnp.float32)


def slot_ranks(count, owner):
    patches = owner.shape[1]
    hot = lax.broadcasted_iota(jnp.int32, (count, patches), 0) == owner
    before = lax.broadcasted_iota(jnp.int32, (patches, patches), 0) < lax.broadcasted_iota(
        jnp.int32, (patches, patches), 1)
    as_bf16 = lambda mask: jnp.where(mask, 1.0, 0.0).astype(jnp.bfloat16)
    ahead = lax.dot_general(as_bf16(hot), as_bf16(before), (((1,), (0,)), ((), ())),
                            preferred_element_type=jnp.float32)
    rank = jnp.sum(jnp.where(hot, ahead, 0.0), axis=0, keepdims=True)
    return as_bf16(hot), rank.astype(jnp.int32)


def by_owner(hot, rank, values):
    slots = lax.broadcasted_iota(jnp.int32, (SLOTS, rank.shape[1]), 0) == rank
    rows = [jnp.where(slots, value, 0.0) for value in values]
    rows += [jnp.zeros_like(rows[0])] * (8 - len(rows))
    high, low = split_bf16(jnp.concatenate(rows, axis=0))
    both = dot_rows(hot, jnp.concatenate([high, low], axis=0))
    return both[:, :8 * SLOTS] + both[:, 8 * SLOTS:]


def fields_on_rows(landed_ref, ny):
    count, kinds, lanes = landed_ref.shape

    def of(device):
        if kinds == 1:
            return landed_ref[device]
        partner = device + ny // 2 if device % ny < ny // 2 else device - ny // 2
        return landed_ref[device, 0:1] + landed_ref[partner, 1:2]

    row = lax.broadcasted_iota(jnp.int32, (8, lanes), 0)
    block = lax.shift_right_logical(
        lax.broadcasted_iota(jnp.int32, (8, lanes), 1), jnp.full((8, lanes), SLOTS.bit_length() - 1, jnp.int32))
    groups = []
    for g in range(count // 8):
        value = jnp.concatenate([of(g * 8 + i) for i in range(8)], axis=0)
        for bit in (1, 2, 4):
            later = pltpu.roll(pltpu.roll(value, 8 - bit, 0), SLOTS * bit, 1)
            sooner = pltpu.roll(pltpu.roll(value, bit, 0), lanes - SLOTS * bit, 1)
            row_bit, block_bit = row & bit, block & bit
            value = jnp.where(row_bit == block_bit, value, jnp.where(row_bit == 0, later, sooner))
        groups.append(value)
    return jnp.concatenate(groups, axis=1)


def fill_weights(count, me, places, high_ref, low_ref):
    angles = high_ref.shape[0] // 2
    slots = places.shape[1]
    azimuth = jnp.full((16, 128), me.astype(jnp.float32) * (2.0 * math.pi / count))
    cos_phi, sin_phi = cos_sin(azimuth)
    pos = [jnp.broadcast_to(places[c:c + 1], (16, slots)) for c in range(3)]

    def group(g, carry):
        start = pl.multiple_of(g * 16, 16)
        index = (lax.broadcasted_iota(jnp.int32, (16, 128), 0) + start).astype(jnp.float32)
        cos_theta, sin_theta = cos_sin(math.pi * (index + 0.5) / angles)
        for part in range(0, slots, 128):
            at = slice(part, part + 128)
            phase = KAPPA * (pos[0][:, at] * sin_theta * cos_phi + pos[1][:, at] * sin_theta * sin_phi
                             + pos[2][:, at] * cos_theta)
            for s, value in enumerate(cos_sin(phase)):
                high, low = split_bf16(value)
                rows = pl.ds(pl.multiple_of(start + s * angles, 16), 16)
                high_ref[rows, at] = high
                low_ref[rows, at] = low
        return carry

    lax.fori_loop(0, angles // 16, group, 0)


def to_owners(count, ny, me, out_ref, landed_ref, sems):
    def copy(k):
        to = lax.rem(me + k, count)
        return pltpu.make_async_remote_copy(
            out_ref.at[to], landed_ref.at[me], sems.at[0], sems.at[1],
            device_id=(lax.div(to, ny), lax.rem(to, ny)), device_id_type=MESH)

    def start(*kinds):
        for i in range(count):
            for kind, rows in enumerate(kinds):
                out_ref[i, kind:kind + 1] = rows[i:i + 1]
        landed_ref[me] = out_ref[me]
        in_fours(count, lambda k: copy(k).start())

    others = pl.ds(0, count - 1)
    whole = pltpu.make_async_remote_copy(
        out_ref.at[others], landed_ref.at[others], sems.at[0], sems.at[1],
        device_id=(me // ny, me % ny), device_id_type=MESH)
    return start, whole.wait_recv, whole.wait_send


def step_kernel(nx, ny, cx, cy, cz, scale, fields_hbm, material_hbm, permit_ref,
                cell_row, owner_row, out_ref, far_ref, material_ref,
                grid_x, grid_y, y_out, y_low, y_high, mid_low, mid_high, coef_x,
                gain_x, pivot_x, left_x, right_x, solved_x,
                coef_y, gain_y, pivot_y, left_y, right_y, solved_y,
                weight_high, weight_low, place_out, place_in, value_out, value_in, packed, near_packed, spots, spots_smem,
                other_spots_smem, facts, other_facts, factors, other_factors, last_factor,
                load_sem, move_sems, halo_sems, place_sems, value_sems, fact_sems, *line_refs):
    half_step = COURANT / 2.0
    half_side = 0.5 * half_step
    count = nx * ny
    wide = padded_rows(cx)
    tiles_x, tiles_y = cy // TILE, cx // TILE
    me = lax.axis_index("gx") * ny + lax.axis_index("gy")
    barrier = pltpu.get_barrier_semaphore()
    inner = grid_x.at[:, pl.ds(1, cx), pl.ds(TILE, cy)]
    load = pltpu.make_async_copy(fields_hbm, inner, load_sem)
    for m in range(6):
        pltpu.make_async_copy(fields_hbm.at[m], inner.at[m], load_sem).start()
    load_material = pltpu.make_async_copy(material_hbm, material_ref, move_sems.at[0])
    load_material.start()
    greet_all(count, ny, me, barrier)
    line_x = Line("gx", nx, line_refs[:10])
    line_y = Line("gy", ny, line_refs[10:])

    def x_halo(first, sems):
        plane = lambda i: grid_x.at[pl.ds(first, 2), i, pl.ds(TILE, cy)]
        return both_ways("gx", nx, plane(1), plane(cx), plane(0), plane(cx + 1), sems)

    mid_plane = lambda j: grid_y.at[:, pl.ds((j + 1) * wide + TILE, cx)]
    first_halos = [
        both_ways("gy", ny, y_out.at[0], y_out.at[1], y_low, y_high, halo_sems.at[0]),
        x_halo(1, halo_sems.at[1]),
        x_halo(4, halo_sems.at[2]),
    ]
    mid_halo = both_ways("gy", ny, mid_plane(0), mid_plane(cy - 1), mid_low, mid_high, halo_sems.at[3])

    def coefs(i, carry):
        which = material_ref[i]
        permit = jnp.zeros(which.shape, jnp.float32)
        for entry in range(permit_ref.shape[0]):
            permit = jnp.where(which == entry, permit_ref[entry], permit)
        coef_x[pl.ds(pl.multiple_of(i * cy, 8), cy), :] = (half_step * half_step) / permit
        return carry

    load.wait()
    for slot, member in enumerate(Y_MEMBERS):
        for end, row in ((0, TILE), (1, TILE + cy - 1)):
            y_out[end, slot] = jnp.concatenate(
                [grid_x[member, 1 + i, row:row + 1] for i in range(cx)], axis=0)
    pl.semaphore_wait(barrier, count - 1)
    for halo in first_halos:
        halo[0]()
        halo[1]()
    load_material.wait()
    lax.fori_loop(0, cx, coefs, 0, unroll=2)
    coef_plane = lambda i: coef_x[pl.ds(pl.multiple_of(i * cy, 8), cy), :]
    factor(cx, coef_plane, gain_x, pivot_x, left_x, right_x)
    line_x.mat_start(left_x, right_x)
    for j in range(cy):
        coef_y[j] = coef_x[pl.ds(j, cx, stride=cy), :]
    for m in range(6):
        for plane in (0, cy + 1):
            grid_y[m, pl.ds(plane * wide, wide), :] = jnp.zeros((wide, cz), jnp.float32)
    patches = cell_row.shape[1]
    cell = cell_row[...]
    line = lax.shift_right_logical(cell, jnp.full_like(cell, cz.bit_length() - 1))
    at_x = jnp.zeros_like(cell)
    for i in range(1, cx):
        at_x = at_x + jnp.where(line >= i * cy, 1, 0)
    at_y, at_z = line - at_x * cy, cell - line * cz
    lanes = lax.broadcasted_iota(jnp.int32, cell.shape, 1)
    spots[0:1] = (at_y * cx + at_x) * 8
    spots[1:2] = (lanes - at_z) & (cz - 1)
    find = pltpu.make_async_copy(spots, spots_smem, move_sems.at[1])
    find.start()
    places = [at_x + lax.axis_index("gx") * cx, at_y + lax.axis_index("gy") * cy, at_z]
    hot, rank = slot_ranks(count, owner_row[...])
    place_send = to_owners(count, ny, me, place_out, place_in, place_sems)
    value_send = to_owners(count, ny, me, value_out, value_in, value_sems)
    place_send[0](by_owner(hot, rank, [place.astype(jnp.float32) for place in places]))
    facts[0:1] = at_x * 8
    facts[1:2] = (lanes - at_z) & (cz - 1)
    facts[2:3] = owner_row[...]
    facts[3:4] = rank
    last = line_y.steps - 1
    tell = [
        pltpu.make_async_remote_copy(
            source, target, fact_sems.at[2 * i], fact_sems.at[2 * i + 1],
            device_id=line_y.partner(last), device_id_type=MESH)
        for i, (source, target) in enumerate(((facts, other_facts), (factors, other_factors)))
    ]
    tell[0].start()

    def gathered(ref, where_ref):
        lane = lax.broadcasted_iota(jnp.int32, (8, cz), 1)
        found = []
        for first in range(0, patches, cz):
            kept = jnp.zeros((8, cz), jnp.float32)
            for at in range(cz):
                rows = ref[pl.ds(where_ref[0, first + at], 8), :]
                kept = jnp.where(lane == at, pltpu.roll(rows, where_ref[1, first + at], 1), kept)
            found.append(kept)
        return jnp.concatenate(found, axis=1)

    factor(cy, lambda j: coef_y[j], gain_y, pivot_y, left_y, right_y)
    line_y.mat_start(left_y, right_y)
    for halo in first_halos:
        halo[2]()

    def solve_x(tile):
        row = (tile + 1) * TILE
        for at, side, need in ((TILE - 1, y_low, tile == 0), (TILE + cy, y_high, tile == tiles_x - 1)):
            for slot, member in enumerate(Y_MEMBERS if need else ()):
                for i in range(cx):
                    grid_x[member, i + 1, at:at + 1] = side[slot, i:i + 1]

        def forward(i, carry):
            near = lambda m, plane, shift: grid_x[m, i + 1 + plane, row + shift:row + shift + TILE]
            centre = [near(m, 0, 0) for m in range(6)]
            dx = {m: near(m, 1, 0) - near(m, -1, 0) for m in X_MEMBERS}
            dy = {m: near(m, 0, 1) - near(m, 0, -1) for m in Y_MEMBERS}
            coef = coef_x[pl.ds(pl.multiple_of(i * cy + tile * TILE, 8), TILE), :]
            right = updated(centre, dx, dy, coef * (0.5 / half_step), half_side)
            gain, pivot = gain_x[i, tile_rows(tile)], pivot_x[i, tile_rows(tile)]
            now = [right[m] * pivot + gain * carry[m] for m in range(6)]
            for m in range(6):
                solved_x[m, i, tile_rows(tile)] = now[m]
            return tuple(now)

        lax.fori_loop(0, cx, forward, (jnp.zeros((TILE, cz), jnp.float32),) * 6, unroll=8)
        sweep_back(cx, gain_x, solved_x, tile_rows(tile))
        for half, members in enumerate(HALVES):
            line_x.rhs_start(tile, half, [solved_x[m, 0, tile_rows(tile)] for m in members],
                             [solved_x[m, cx - 1, tile_rows(tile)] for m in members])

    def finish_x(tile):
        rows = tile_rows(tile)
        planes = lambda i: pl.ds((tile * TILE + 1) * wide + TILE + i, TILE, stride=wide)
        ends = [[line_x.ends[end, m, rows] for m in range(6)] for end in range(2)]
        for m in range(6):
            grid_y[m, planes(-1), :] = ends[0][m]
            grid_y[m, planes(cx), :] = ends[1][m]
        for i in range(cx):
            left, right = left_x[i, rows], right_x[i, rows]
            for m in range(6):
                grid_y[m, planes(i), :] = solved_x[m, i, rows] + left * ends[0][m] + right * ends[1][m]

    def forward_y(j, carry):
        near = lambda m, plane, shift: grid_y[m, pl.ds((j + 1 + plane) * wide + TILE + shift, cx), :]
        centre = [near(m, 0, 0) for m in range(6)]
        dx = {m: near(m, 0, 1) - near(m, 0, -1) for m in X_MEMBERS}
        dy = {m: near(m, 1, 0) - near(m, -1, 0) for m in Y_MEMBERS}
        right = updated(centre, dx, dy, coef_y[j] * (0.5 / half_step), half_side)
        gain, pivot = gain_y[j], pivot_y[j]
        now = [right[m] * pivot + gain * carry[m] for m in range(6)]
        for m in range(6):
            solved_y[m, j] = now[m]
        return tuple(now)

    order = [0, tiles_x - 1] + list(range(1, tiles_x - 1))
    for place, tile in enumerate(order):
        solve_x(tile)
        if place == 1:
            line_x.mat_merge(0)
    place_send[1]()
    fill_weights(count, me, fields_on_rows(place_in, ny), weight_high, weight_low)
    chunks = [(tile, half) for tile in order for half in range(len(HALVES))]
    for k in range(line_x.steps - 1):
        for place, chunk in enumerate(chunks):
            line_x.rhs_merge(k, *chunk)
            if place == 1 and k + 1 < line_x.steps - 1:
                line_x.mat_merge(k + 1)
        if k < line_y.steps:
            line_y.mat_merge(k)
    if line_x.steps > 1:
        line_x.mat_merge(line_x.steps - 1)
    for k in range(line_x.steps - 1, line_y.steps):
        line_y.mat_merge(k)
    inv, gain_in, gain_out = line_y.plan[last, 0], line_y.plan[last, 5], line_y.plan[last, 6]
    for j in range(cy):
        value = (left_y[j] * gain_in + right_y[j] * gain_out) * inv
        last_factor[j] = value
        for tile in range(tiles_y):
            packed[pl.ds((j * cx + tile * TILE) * 8 + 6, TILE, stride=8), :] = value[tile * TILE:(tile + 1) * TILE]
    find.wait()
    factors[...] = gathered(packed, spots_smem)[6:7]
    tell[1].start()
    tell[0].wait_recv()
    find_other = pltpu.make_async_copy(other_facts, other_spots_smem, move_sems.at[1])
    find_other.start()
    carry = (jnp.zeros((cx, cz), jnp.float32),) * 6
    for tile in order:
        for half in range(len(HALVES)):
            line_x.rhs_merge(line_x.steps - 1, tile, half)
        finish_x(tile)
        if tile == 0:
            mid_halo[1]()
            carry = lax.fori_loop(0, TILE - 2, forward_y, carry, unroll=6)
        if tile == tiles_x - 1:
            mid_halo[0]()
    lax.fori_loop(TILE - 2, cy, forward_y, carry, unroll=6)
    for tile in range(tiles_y):
        sweep_back(cy, gain_y, solved_y, tile_rows(tile))
    mid_halo[2]()

    def ghosts(tile):
        rows = tile_rows(tile)
        found = []
        for ref, at, sign in ((mid_low, 0, 1.0), (mid_high, cy - 1, -1.0)):
            side = sign * half_side / coef_y[at, rows]
            found.append({
                0: ref[5, rows] * (-sign * 0.5 / half_step),
                2: ref[3, rows] * (sign * 0.5 / half_step),
                3: ref[2, rows] * side,
                5: ref[0, rows] * -side,
            })
        return found

    added = [ghosts(tile) for tile in range(tiles_y)]
    for tile in range(tiles_y):
        rows = tile_rows(tile)
        low, high = added[tile]

        def outer(m, at):
            value = solved_y[m, at, rows]
            return value + left_y[at, rows] * low[m] + right_y[at, rows] * high[m] if m in low else value

        for half, members in enumerate(HALVES):
            line_y.rhs_start(tile, half, [outer(m, 0) for m in members], [outer(m, cy - 1) for m in members])
    for k in range(line_y.steps - 1):
        for tile in range(tiles_y):
            for half in range(len(HALVES)):
                line_y.rhs_merge(k, tile, half)
    for tile in range(tiles_y):
        rows = tile_rows(tile)
        ends = [line_y.known_ends(tile, m) for m in range(6)]
        for m in range(6):
            near_packed[pl.ds(tile * TILE * 8 + m, TILE, stride=8), :] = line_y.near_value(tile, m)
            if m in added[tile][0]:
                ends[m] = [ends[m][end] + added[tile][end][m] for end in range(2)]
        for j in range(cy):
            left, right = left_y[j, rows], right_y[j, rows]
            for m in range(6):
                value = solved_y[m, j, rows] + left * ends[m][0] + right * ends[m][1]
                solved_y[m, j, rows] = value
                packed[pl.ds((j * cx + tile * TILE) * 8 + m, TILE, stride=8), :] = value

    tell[1].wait_recv()
    find_other.wait()
    values = gathered(packed, spots_smem)
    theirs = gathered(near_packed, other_spots_smem) * other_factors[...]
    other_hot = (lax.broadcasted_iota(jnp.int32, (count, patches), 0) == other_facts[2:3])
    other_hot = jnp.where(other_hot, 1.0, 0.0).astype(jnp.bfloat16)
    value_send[0](by_owner(hot, rank, [values[m:m + 1] for m in range(6)]),
                  by_owner(other_hot, other_facts[3:4], [theirs[m:m + 1] for m in range(6)]))
    for tile in range(tiles_y):
        rows = tile_rows(tile)
        received = line_y.far_values(tile)
        for j in range(cy):
            factor_row = last_factor[j, rows]
            for m in range(6):
                out_ref[pl.ds((m * cx + tile * TILE) * cy + j, TILE, stride=cy), :] = (
                    solved_y[m, j, rows] + factor_row * received[m])
    for one in tell:
        one.wait_send()
    for halo in [*first_halos, mid_halo]:
        halo[3]()
    line_x.drain()
    line_y.drain()
    place_send[2]()
    value_send[1]()
    high, low = split_bf16(fields_on_rows(value_in, ny))
    both = jnp.concatenate([high, low], axis=0)
    product = dot_rows(both, weight_high[...]) + dot_rows(both, weight_low[...])
    product = (product[:8] + product[8:]) * scale
    angles = far_ref.shape[1]
    for s in range(2):
        far_ref[pl.ds(s * 6, 6), :] = product[:6, s * angles:(s + 1) * angles]
    value_send[2]()


def store_kernel(new_ref, far_ref, new_hbm, far_hbm, sems):
    rows = new_ref.shape[0] // 6
    for m in range(6):
        part = pl.ds(m * rows, rows)
        pltpu.make_async_copy(new_ref.at[part], new_hbm.at[part], sems.at[0]).start()
    far = pltpu.make_async_copy(far_ref, far_hbm, sems.at[1])
    far.start()
    pltpu.make_async_copy(new_ref, new_hbm, sems.at[0]).wait()
    far.wait()


def line_scratch(count, rows, lanes):
    steps = count.bit_length() - 1
    chunks = rows // TILE * len(HALVES)
    f32 = jnp.float32
    return [
        pltpu.VMEM((steps, 4, rows, lanes), f32),
        pltpu.VMEM((steps, 4, rows, lanes), f32),
        pltpu.VMEM((steps, chunks, 2, len(HALVES[0]), TILE, lanes), f32),
        pltpu.VMEM((steps, chunks, 2, len(HALVES[0]), TILE, lanes), f32),
        pltpu.VMEM((steps, 7, rows, lanes), f32),
        pltpu.VMEM((4, rows, lanes), f32),
        pltpu.VMEM((2, 6, rows, lanes), f32),
        pltpu.SemaphoreType.DMA((3,)),
        pltpu.SemaphoreType.DMA((steps,)),
        pltpu.SemaphoreType.DMA((steps, chunks)),
    ]


def local(nx, ny, fields, material, permittivity, patch_cell, patch_owner):
    _, cx, cy, cz = fields.shape
    f32 = jnp.float32
    count = nx * ny
    patches = patch_cell.shape[0]
    vmem = pl.BlockSpec(memory_space=pltpu.VMEM)
    smem = pl.BlockSpec(memory_space=pltpu.SMEM)
    hbm = pl.BlockSpec(memory_space=pltpu.HBM)
    x_lines = [pltpu.VMEM((cx, cy, cz), f32)] * 4
    y_lines = [pltpu.VMEM((cy, cx, cz), f32)] * 4
    pinned = lambda value: pltpu.with_memory_space_constraint(value, pltpu.HBM)
    new_flat, far_field = pl.pallas_call(
        functools.partial(step_kernel, nx, ny, cx, cy, cz, 1.0 / math.sqrt(patches)),
        out_shape=(
            jax.ShapeDtypeStruct((6 * cx * cy, cz), f32),
            jax.ShapeDtypeStruct((12, ANG_DEV), f32),
        ),
        in_specs=[hbm, hbm, smem, vmem, vmem],
        out_specs=(vmem, vmem),
        scratch_shapes=[
            pltpu.VMEM((cx, cy, cz), jnp.int32),
            pltpu.VMEM((6, cx + 2, cy + 2 * TILE, cz), f32),
            pltpu.VMEM((6, (cy + 2) * padded_rows(cx), cz), f32),
            pltpu.VMEM((2, 4, cx, cz), f32),
            pltpu.VMEM((4, cx, cz), f32),
            pltpu.VMEM((4, cx, cz), f32),
            pltpu.VMEM((6, cx, cz), f32),
            pltpu.VMEM((6, cx, cz), f32),
            pltpu.VMEM((cx * cy, cz), f32),
            *x_lines,
            pltpu.VMEM((6, cx, cy, cz), f32),
            pltpu.VMEM((cy, cx, cz), f32),
            *y_lines,
            pltpu.VMEM((6, cy, cx, cz), f32),
            pltpu.VMEM((2 * ANG_DEV, SLOTS * count), jnp.bfloat16),
            pltpu.VMEM((2 * ANG_DEV, SLOTS * count), jnp.bfloat16),
            *[pltpu.VMEM((count, 1, 8 * SLOTS), f32)] * 2,
            *[pltpu.VMEM((count, 2, 8 * SLOTS), f32)] * 2,
            pltpu.VMEM((cx * cy * 8, cz), f32),
            pltpu.VMEM((cx * 8, cz), f32),
            pltpu.VMEM((2, patches), jnp.int32),
            pltpu.SMEM((2, patches), jnp.int32),
            pltpu.SMEM((4, patches), jnp.int32),
            pltpu.VMEM((4, patches), jnp.int32),
            pltpu.VMEM((4, patches), jnp.int32),
            pltpu.VMEM((1, patches), f32),
            pltpu.VMEM((1, patches), f32),
            pltpu.VMEM((cy, cx, cz), f32),
            pltpu.SemaphoreType.DMA,
            pltpu.SemaphoreType.DMA((2,)),
            pltpu.SemaphoreType.DMA((4, 4)),
            pltpu.SemaphoreType.DMA((2,)),
            pltpu.SemaphoreType.DMA((2,)),
            pltpu.SemaphoreType.DMA((4,)),
            *line_scratch(nx, cy, cz),
            *line_scratch(ny, cx, cz),
        ],
        compiler_params=pltpu.CompilerParams(
            collective_id=0, has_side_effects=True, vmem_limit_bytes=40 * 2**20),
        name="split_step",
    )(pinned(fields), pinned(material), pinned(permittivity), pinned(patch_cell[None, :]),
      pinned(patch_owner.reshape(1, patches)))
    new_flat, far_field = pl.pallas_call(
        store_kernel,
        out_shape=(
            jax.ShapeDtypeStruct((6 * cx * cy, cz), f32),
            jax.ShapeDtypeStruct((12, ANG_DEV), f32),
        ),
        in_specs=[vmem, vmem],
        out_specs=(hbm, hbm),
        scratch_shapes=[pltpu.SemaphoreType.DMA((2,))],
        compiler_params=pltpu.CompilerParams(vmem_limit_bytes=4 * 2**20),
        name="store",
    )(new_flat, far_field)
    return new_flat.reshape(fields.shape), far_field


def solution(mesh):
    return jax.shard_map(
        functools.partial(local, mesh.shape["gx"], mesh.shape["gy"]),
        mesh=mesh,
        in_specs=(
            P(None, "gx", "gy", None),
            P("gx", "gy", None),
            P(),
            P(("gx", "gy")),
            P(("gx", "gy"), None),
        ),
        out_specs=(P(None, "gx", "gy", None), P(None, ("gx", "gy"))),
        check_vma=False,
    )
```

```python
import functools
import math

import jax
import jax.numpy as jnp
from jax import lax
from jax.experimental import pallas as pl
from jax.experimental.pallas import tpu as pltpu
from jax.sharding import PartitionSpec as P

ANG_DEV = 128
COURANT = 64
KAPPA = 0.5
MESH = pl.DeviceIdType.MESH
X_MEMBERS = (1, 2, 4, 5)
Y_MEMBERS = (0, 2, 3, 5)
Z_MEMBERS = (0, 1, 3, 4)
TILE = 8
HALVES = ((0, 1, 2), (3, 4, 5))
SLOTS = 16


def lane_difference(value):
    lanes = value.shape[1]
    at = lax.broadcasted_iota(jnp.int32, value.shape, 1)
    below = jnp.where(at == 0, 0.0, pltpu.roll(value, 1, 1))
    above = jnp.where(at == lanes - 1, 0.0, pltpu.roll(value, lanes - 1, 1))
    return above - below


def updated(centre, dx, dy, half_curl, half_side):
    dz = {m: lane_difference(centre[m]) for m in Z_MEMBERS}
    curl_h = [dy[5] - dz[4], dz[3] - dx[5], dx[4] - dy[3]]
    curl_e = [dy[2] - dz[1], dz[0] - dx[2], dx[1] - dy[0]]
    return [centre[m] + half_curl * curl_h[m] for m in range(3)] + [
        centre[3 + m] - half_side * curl_e[m] for m in range(3)
    ]


def factor(length, coef_at, gain_ref, pivot_ref, left_ref, right_ref):
    zero = jnp.zeros(gain_ref.shape[1:], jnp.float32)

    def forward(i, carry):
        gain_prev, left_prev = carry
        coef = coef_at(i)
        pivot = 1.0 / (1.0 + 2.0 * coef - coef * gain_prev)
        gain = coef * pivot
        left = gain * left_prev
        gain_ref[i] = gain
        pivot_ref[i] = pivot
        left_ref[i] = left
        return gain, left

    lax.fori_loop(0, length, forward, (zero, jnp.ones_like(zero)), unroll=2)

    def backward(k, carry):
        left_next, right_next = carry
        i = length - 1 - k
        gain = gain_ref[i]
        left = left_ref[i] + gain * left_next
        right = gain * right_next
        left_ref[i] = left
        right_ref[i] = right
        return left, right

    lax.fori_loop(0, length, backward, (zero, jnp.ones_like(zero)), unroll=4)


def sweep_back(length, gain_ref, solved_ref, rows, unroll):
    def backward(k, carry):
        i = length - 1 - k
        gain = gain_ref[i, rows]
        now = [solved_ref[m, i, rows] + gain * carry[m] for m in range(6)]
        for m in range(6):
            solved_ref[m, i, rows] = now[m]
        return tuple(now)

    zero = jnp.zeros((rows.size, gain_ref.shape[2]), jnp.float32)
    lax.fori_loop(0, length, backward, (zero,) * 6, unroll=unroll)


def padded_rows(rows):
    return (rows // TILE + 2 | 1) * TILE


def tile_rows(tile):
    return pl.ds(tile * TILE, TILE)


class Line:
    def __init__(self, axis, count, refs):
        (self.mat_out, self.mat_in, self.rhs_out, self.rhs_in, self.plan, self.gains, self.ends,
         self.sent, self.mat_sems, self.rhs_sems) = refs
        self.axis = axis
        self.count = count
        self.steps = count.bit_length() - 1
        self.chunks = self.rhs_out.shape[1]
        self.me = lax.axis_index(axis)

    def near(self, k):
        return 1 - (self.me // 2**k) % 2

    def partner(self, k):
        return {self.axis: self.me + (2 * self.near(k) - 1) * 2**k}

    def mat_copy(self, k):
        source, target, sent = self.mat_out.at[k], self.mat_in.at[k], 0
        if k == self.steps - 1:
            source, target, sent = source.at[3 * self.near(k)], target.at[0], 3
        return pltpu.make_async_remote_copy(
            source, target, self.sent.at[sent], self.mat_sems.at[k],
            device_id=self.partner(k), device_id_type=MESH)

    def rhs_copy(self, k, chunk):
        source, target = self.rhs_out.at[k, chunk], self.rhs_in.at[k, chunk]
        if k == self.steps - 1:
            source, target = source.at[self.near(k)], target.at[0]
        return pltpu.make_async_remote_copy(
            source, target, self.sent.at[1 if k < self.steps - 1 else 2], self.rhs_sems.at[k, chunk],
            device_id=self.partner(k), device_id_type=MESH)

    def mat_start(self, left_ref, right_ref):
        last = left_ref.shape[0] - 1
        for end, at in ((0, 0), (1, last)):
            self.mat_out[0, 2 * end] = left_ref[at]
            self.mat_out[0, 2 * end + 1] = right_ref[at]
        one, zero = jnp.ones(left_ref.shape[1:], jnp.float32), jnp.zeros(left_ref.shape[1:], jnp.float32)
        self.gains[0] = one
        self.gains[1] = zero
        self.gains[2] = zero
        self.gains[3] = one
        self.mat_copy(0).start()

    def mat_merge(self, k):
        self.mat_copy(k).wait_recv()
        n = self.near(k)
        f = 1 - n
        mine = lambda end, side: self.mat_out[k, 2 * end + side]
        other = lambda end, side: self.mat_in[k, 2 * end + side]
        gain_in, gain_out = self.gains[n], self.gains[2 + n]
        if k == self.steps - 1:
            m_nn, o_nn = mine(n, n), self.mat_in[k, 0]
            inv = 1.0 / (1.0 - m_nn * o_nn)
            for slot, value in ((0, inv), (1, o_nn * inv), (5, gain_in), (6, gain_out)):
                self.plan[k, slot] = value
            return
        m_nn, m_fn, m_nf, m_ff = mine(n, n), mine(f, n), mine(n, f), mine(f, f)
        o_nn, o_fn, o_nf, o_ff = other(f, f), other(n, f), other(f, n), other(n, n)
        inv = 1.0 / (1.0 - m_nn * o_nn)
        o_by_m = o_nn * m_nf * inv
        o_by_o = o_nf * inv
        m_by_m = m_nf * inv
        m_by_o = m_nn * o_nf * inv
        for slot, value in enumerate((inv, o_nn * inv, m_nn * inv, m_fn, o_fn, gain_in, gain_out)):
            self.plan[k, slot] = value
        self.mat_out[k + 1, 2 * f + f] = m_ff + m_fn * o_by_m
        self.mat_out[k + 1, 2 * f + n] = m_fn * o_by_o
        self.mat_out[k + 1, 2 * n + n] = o_ff + o_fn * m_by_o
        self.mat_out[k + 1, 2 * n + f] = o_fn * m_by_m
        self.mat_copy(k + 1).start()
        self.gains[f] = self.gains[f] + gain_in * o_by_m
        self.gains[2 + f] = self.gains[2 + f] + gain_out * o_by_m
        self.gains[n] = gain_in * o_by_o
        self.gains[2 + n] = gain_out * o_by_o

    def rhs_start(self, tile, half, firsts, lasts):
        chunk = tile * len(HALVES) + half
        for at in range(len(HALVES[half])):
            self.rhs_out[0, chunk, 0, at] = firsts[at]
            self.rhs_out[0, chunk, 1, at] = lasts[at]
        self.rhs_copy(0, chunk).start()

    def rhs_merge(self, k, tile, half):
        chunk = tile * len(HALVES) + half
        rows = tile_rows(tile)
        self.rhs_copy(k, chunk).wait_recv()
        n = self.near(k)
        f = 1 - n
        ending = k == self.steps - 1
        inv, o_nn, gain_in, gain_out = [self.plan[k, slot, rows] for slot in (0, 1, 5, 6)]
        m_nn, m_fn, o_fn = [None if ending else self.plan[k, slot, rows] for slot in (2, 3, 4)]
        for at, m in enumerate(HALVES[half]):
            mine = self.rhs_out[k, chunk, n, at]
            other = self.rhs_in[k, chunk, 0, at] if ending else self.rhs_in[k, chunk, f, at]
            o_value = other * inv + o_nn * mine
            if not ending:
                m_value = mine * inv + m_nn * other
                self.rhs_out[k + 1, chunk, f, at] = self.rhs_out[k, chunk, f, at] + m_fn * o_value
                self.rhs_out[k + 1, chunk, n, at] = self.rhs_in[k, chunk, n, at] + o_fn * m_value
            into, out_of = gain_in * o_value, gain_out * o_value
            if k > 0:
                into, out_of = self.ends[0, m, rows] + into, self.ends[1, m, rows] + out_of
            self.ends[0, m, rows] = into
            self.ends[1, m, rows] = out_of
        if not ending:
            self.rhs_copy(k + 1, chunk).start()

    def known_ends(self, tile, m):
        k, rows = self.steps - 1, tile_rows(tile)
        scaled = self.plan[k, 1, rows] * self.near_value(tile, m)
        ends = [self.plan[k, 5 + end, rows] * scaled for end in range(2)]
        return [self.ends[end, m, rows] + ends[end] for end in range(2)] if k > 0 else ends

    def place_of(self, tile, m):
        half = next(h for h, members in enumerate(HALVES) if m in members)
        return tile * len(HALVES) + half, HALVES[half].index(m)

    def near_value(self, tile, m):
        k = self.steps - 1
        chunk, at = self.place_of(tile, m)
        return self.rhs_out[k, chunk, self.near(k), at]

    def drain(self):
        early = pl.ds(0, self.steps - 1)
        last = self.steps - 1
        for slot, source, target in (
            (0, self.mat_out.at[early], self.mat_in.at[early]),
            (3, self.mat_out.at[last, 0], self.mat_in.at[last, 0]),
            (1, self.rhs_out.at[early], self.rhs_in.at[early]),
            (2, self.rhs_out.at[last, :, 0], self.rhs_in.at[last, :, 0]),
        ):
            pltpu.make_async_remote_copy(
                source, target, self.sent.at[slot], self.mat_sems.at[0],
                device_id=self.partner(0), device_id_type=MESH).wait_send()


def both_ways(axis, count, out_low, out_high, in_low, in_high, sems):
    me = lax.axis_index(axis)
    up = lambda: pltpu.make_async_remote_copy(
        out_high, in_low, sems.at[0], sems.at[1], device_id={axis: me + 1}, device_id_type=MESH)
    down = lambda: pltpu.make_async_remote_copy(
        out_low, in_high, sems.at[2], sems.at[3], device_id={axis: me - 1}, device_id_type=MESH)

    def start_up():
        @pl.when(me < count - 1)
        def _():
            up().start()

        @pl.when(me == 0)
        def _():
            in_low[...] = jnp.zeros(in_low.shape, jnp.float32)

    def start_down():
        @pl.when(me > 0)
        def _():
            down().start()

        @pl.when(me == count - 1)
        def _():
            in_high[...] = jnp.zeros(in_high.shape, jnp.float32)

    def wait():
        @pl.when(me > 0)
        def _():
            up().wait_recv()

        @pl.when(me < count - 1)
        def _():
            down().wait_recv()

    def drain():
        @pl.when(me < count - 1)
        def _():
            up().wait_send()

        @pl.when(me > 0)
        def _():
            down().wait_send()

    return start_up, start_down, wait, drain


def in_fours(count, act):
    head = (count - 1) % 4
    for k in range(1, 1 + head):
        act(k)

    def four(g, carry):
        for u in range(4):
            act(1 + head + 4 * g + u)
        return carry

    lax.fori_loop(0, (count - 1) // 4, four, 0)


def greet_all(count, ny, me, barrier):
    def hello(k):
        to = lax.rem(me + k, count)
        pl.semaphore_signal(
            barrier, inc=1, device_id=(lax.div(to, ny), lax.rem(to, ny)), device_id_type=MESH)

    def pair(i):
        hello(i)
        hello(count - i)

    in_fours(count // 2, pair)
    hello(count // 2)


def cos_sin(angle):
    turns = jnp.floor(angle * (2.0 / math.pi) + 0.5)
    rest = ((angle - turns * 1.5703125) - turns * 4.837512969970703125e-4) - turns * 7.54978995489188216e-8
    square = rest * rest
    sine = ((-1.9515295891e-4 * square + 8.3321608736e-3) * square - 1.6666654611e-1) * square * rest + rest
    cosine = (
        (2.443315711809948e-5 * square - 1.388731625493765e-3) * square + 4.166664568298827e-2
    ) * square * square - 0.5 * square + 1.0
    quarter = turns.astype(jnp.int32) & 3
    swap = (quarter & 1) == 1
    plain_cos = jnp.where(swap, sine, cosine)
    plain_sin = jnp.where(swap, cosine, sine)
    minus_cos = (quarter == 1) | (quarter == 2)
    return jnp.where(minus_cos, -plain_cos, plain_cos), jnp.where(quarter >= 2, -plain_sin, plain_sin)


def split_bf16(value):
    high = value.astype(jnp.bfloat16)
    return high, (value - high.astype(jnp.float32)).astype(jnp.bfloat16)


def dot_rows(left, right):
    return lax.dot_general(left, right, (((1,), (1,)), ((), ())), preferred_element_type=jnp.float32)


def at_columns(table_ref, at_x, at_z):
    lanes = table_ref.shape[1]
    groups = []
    for first in range(0, at_x.shape[1], lanes):
        here = slice(first, first + lanes)
        where_x = jnp.broadcast_to(at_x[:, here], (8, lanes))
        where_z = jnp.broadcast_to(at_z[:, here], (8, lanes))
        kept = jnp.zeros((8, lanes), jnp.float32)
        for x in range(table_ref.shape[0] // 8):
            found = jnp.take_along_axis(table_ref[x * 8:(x + 1) * 8], where_z, axis=1, mode="promise_in_bounds")
            kept = jnp.where(where_x == x, found, kept)
        groups.append(kept)
    return jnp.concatenate(groups, axis=1)


def slot_ranks(count, owner):
    patches = owner.shape[1]
    hot = lax.broadcasted_iota(jnp.int32, (count, patches), 0) == owner
    before = lax.broadcasted_iota(jnp.int32, (patches, patches), 0) < lax.broadcasted_iota(
        jnp.int32, (patches, patches), 1)
    as_bf16 = lambda mask: jnp.where(mask, 1.0, 0.0).astype(jnp.bfloat16)
    ahead = lax.dot_general(as_bf16(hot), as_bf16(before), (((1,), (0,)), ((), ())),
                            preferred_element_type=jnp.float32)
    rank = jnp.sum(jnp.where(hot, ahead, 0.0), axis=0, keepdims=True)
    return as_bf16(hot), rank.astype(jnp.int32)


def by_owner(hot, rank, values):
    slots = lax.broadcasted_iota(jnp.int32, (SLOTS, rank.shape[1]), 0) == rank
    rows = [jnp.where(slots, value, 0.0) for value in values]
    rows += [jnp.zeros_like(rows[0])] * (8 - len(rows))
    high, low = split_bf16(jnp.concatenate(rows, axis=0))
    both = dot_rows(hot, jnp.concatenate([high, low], axis=0))
    return both[:, :8 * SLOTS] + both[:, 8 * SLOTS:]


def fields_on_rows(landed_ref, ny):
    count, kinds, lanes = landed_ref.shape

    def of(device):
        if kinds == 1:
            return landed_ref[device]
        partner = device + ny // 2 if device % ny < ny // 2 else device - ny // 2
        return landed_ref[device, 0:1] + landed_ref[partner, 1:2]

    row = lax.broadcasted_iota(jnp.int32, (8, lanes), 0)
    block = lax.shift_right_logical(
        lax.broadcasted_iota(jnp.int32, (8, lanes), 1), jnp.full((8, lanes), SLOTS.bit_length() - 1, jnp.int32))
    groups = []
    for g in range(count // 8):
        value = jnp.concatenate([of(g * 8 + i) for i in range(8)], axis=0)
        for bit in (1, 2, 4):
            later = pltpu.roll(pltpu.roll(value, 8 - bit, 0), SLOTS * bit, 1)
            sooner = pltpu.roll(pltpu.roll(value, bit, 0), lanes - SLOTS * bit, 1)
            row_bit, block_bit = row & bit, block & bit
            value = jnp.where(row_bit == block_bit, value, jnp.where(row_bit == 0, later, sooner))
        groups.append(value)
    return jnp.concatenate(groups, axis=1)


def fill_weights(count, me, places, high_ref, low_ref):
    angles = high_ref.shape[0] // 2
    slots = places.shape[1]
    azimuth = jnp.full((16, 128), me.astype(jnp.float32) * (2.0 * math.pi / count))
    cos_phi, sin_phi = cos_sin(azimuth)
    pos = [jnp.broadcast_to(places[c:c + 1], (16, slots)) for c in range(3)]

    def group(g, carry):
        start = pl.multiple_of(g * 16, 16)
        index = (lax.broadcasted_iota(jnp.int32, (16, 128), 0) + start).astype(jnp.float32)
        cos_theta, sin_theta = cos_sin(math.pi * (index + 0.5) / angles)
        for part in range(0, slots, 128):
            at = slice(part, part + 128)
            phase = KAPPA * (pos[0][:, at] * sin_theta * cos_phi + pos[1][:, at] * sin_theta * sin_phi
                             + pos[2][:, at] * cos_theta)
            for s, value in enumerate(cos_sin(phase)):
                high, low = split_bf16(value)
                rows = pl.ds(pl.multiple_of(start + s * angles, 16), 16)
                high_ref[rows, at] = high
                low_ref[rows, at] = low
        return carry

    lax.fori_loop(0, angles // 16, group, 0)


def to_owners(count, ny, me, out_ref, landed_ref, sems):
    def copy(k):
        to = lax.rem(me + k, count)
        return pltpu.make_async_remote_copy(
            out_ref.at[to], landed_ref.at[me], sems.at[0], sems.at[1],
            device_id=(lax.div(to, ny), lax.rem(to, ny)), device_id_type=MESH)

    def start(*kinds):
        for i in range(count):
            for kind, rows in enumerate(kinds):
                out_ref[i, kind:kind + 1] = rows[i:i + 1]
        landed_ref[me] = out_ref[me]
        in_fours(count, lambda k: copy(k).start())

    others = pl.ds(0, count - 1)
    whole = pltpu.make_async_remote_copy(
        out_ref.at[others], landed_ref.at[others], sems.at[0], sems.at[1],
        device_id=(me // ny, me % ny), device_id_type=MESH)
    return start, whole.wait_recv, whole.wait_send


def step_kernel(nx, ny, cx, cy, cz, scale, fields_hbm, material_hbm, permit_ref,
                cell_row, owner_row, out_ref, far_ref, material_ref,
                grid_x, grid_y, y_out, y_low, y_high, mid_low, mid_high, coef_x,
                gain_x, pivot_x, left_x, right_x, solved_x,
                coef_y, gain_y, pivot_y, left_y, right_y, solved_y,
                weight_high, weight_low, place_out, place_in, value_out, value_in, packed, near_packed, low_packed, high_packed, spots, spots_smem,
                facts, other_facts, factors, other_factors,
                load_sem, move_sems, halo_sems, place_sems, value_sems, fact_sems, *line_refs):
    half_step = COURANT / 2.0
    half_side = 0.5 * half_step
    count = nx * ny
    wide = padded_rows(cx)
    tiles_x, tiles_y = cy // TILE, cx // TILE
    me = lax.axis_index("gx") * ny + lax.axis_index("gy")
    barrier = pltpu.get_barrier_semaphore()
    inner = grid_x.at[:, pl.ds(1, cx), pl.ds(TILE, cy)]
    load = pltpu.make_async_copy(fields_hbm, inner, load_sem)
    for m in range(6):
        pltpu.make_async_copy(fields_hbm.at[m], inner.at[m], load_sem).start()
    load_material = pltpu.make_async_copy(material_hbm, material_ref, move_sems.at[0])
    load_material.start()
    greet_all(count, ny, me, barrier)
    line_x = Line("gx", nx, line_refs[:10])
    line_y = Line("gy", ny, line_refs[10:])

    def x_halo(first, sems):
        plane = lambda i: grid_x.at[pl.ds(first, 2), i, pl.ds(TILE, cy)]
        return both_ways("gx", nx, plane(1), plane(cx), plane(0), plane(cx + 1), sems)

    mid_plane = lambda j: grid_y.at[:, pl.ds((j + 1) * wide + TILE, cx)]
    first_halos = [
        both_ways("gy", ny, y_out.at[0], y_out.at[1], y_low, y_high, halo_sems.at[0]),
        x_halo(1, halo_sems.at[1]),
        x_halo(4, halo_sems.at[2]),
    ]
    mid_halo = both_ways("gy", ny, mid_plane(0), mid_plane(cy - 1), mid_low, mid_high, halo_sems.at[3])

    def coefs(i, carry):
        which = material_ref[i]
        permit = jnp.zeros(which.shape, jnp.float32)
        for entry in range(permit_ref.shape[0]):
            permit = jnp.where(which == entry, permit_ref[entry], permit)
        coef_x[pl.ds(pl.multiple_of(i * cy, 8), cy), :] = (half_step * half_step) / permit
        return carry

    load.wait()
    for slot, member in enumerate(Y_MEMBERS):
        for end, row in ((0, TILE), (1, TILE + cy - 1)):
            y_out[end, slot] = jnp.concatenate(
                [grid_x[member, 1 + i, row:row + 1] for i in range(cx)], axis=0)
    pl.semaphore_wait(barrier, count - 1)
    for halo in first_halos:
        halo[0]()
        halo[1]()
    load_material.wait()
    lax.fori_loop(0, cx, coefs, 0, unroll=2)
    coef_plane = lambda i: coef_x[pl.ds(pl.multiple_of(i * cy, 8), cy), :]
    factor(cx, coef_plane, gain_x, pivot_x, left_x, right_x)
    line_x.mat_start(left_x, right_x)
    for j in range(cy):
        coef_y[j] = coef_x[pl.ds(j, cx, stride=cy), :]
    for m in range(6):
        for plane in (0, cy + 1):
            grid_y[m, pl.ds(plane * wide, wide), :] = jnp.zeros((wide, cz), jnp.float32)
    patches = cell_row.shape[1]
    cell = cell_row[...]
    line = lax.shift_right_logical(cell, jnp.full_like(cell, cz.bit_length() - 1))
    at_x = jnp.zeros_like(cell)
    for i in range(1, cx):
        at_x = at_x + jnp.where(line >= i * cy, 1, 0)
    at_y, at_z = line - at_x * cy, cell - line * cz
    lanes = lax.broadcasted_iota(jnp.int32, cell.shape, 1)
    spots[0:1] = (at_y * cx + at_x) * 8
    spots[1:2] = (lanes - at_z) & (cz - 1)
    find = pltpu.make_async_copy(spots, spots_smem, move_sems.at[1])
    find.start()
    places = [at_x + lax.axis_index("gx") * cx, at_y + lax.axis_index("gy") * cy, at_z]
    hot, rank = slot_ranks(count, owner_row[...])
    place_send = to_owners(count, ny, me, place_out, place_in, place_sems)
    value_send = to_owners(count, ny, me, value_out, value_in, value_sems)
    place_send[0](by_owner(hot, rank, [place.astype(jnp.float32) for place in places]))
    facts[0:1] = at_x
    facts[1:2] = at_z
    facts[2:3] = owner_row[...]
    facts[3:4] = rank
    last = line_y.steps - 1
    tell = [
        pltpu.make_async_remote_copy(
            source, target, fact_sems.at[2 * i], fact_sems.at[2 * i + 1],
            device_id=line_y.partner(last), device_id_type=MESH)
        for i, (source, target) in enumerate(((facts, other_facts), (factors, other_factors)))
    ]
    tell[0].start()

    def gathered(ref, where_ref):
        lane = lax.broadcasted_iota(jnp.int32, (8, cz), 1)
        found = []
        for first in range(0, patches, cz):
            kept = jnp.zeros((8, cz), jnp.float32)
            for at in range(cz):
                rows = ref[pl.ds(where_ref[0, first + at], 8), :]
                kept = jnp.where(lane == at, pltpu.roll(rows, where_ref[1, first + at], 1), kept)
            found.append(kept)
        return jnp.concatenate(found, axis=1)

    factor(cy, lambda j: coef_y[j], gain_y, pivot_y, left_y, right_y)
    line_y.mat_start(left_y, right_y)
    for halo in first_halos:
        halo[2]()

    def solve_x(tile):
        row = (tile + 1) * TILE
        for at, side, need in ((TILE - 1, y_low, tile == 0), (TILE + cy, y_high, tile == tiles_x - 1)):
            for slot, member in enumerate(Y_MEMBERS if need else ()):
                for i in range(cx):
                    grid_x[member, i + 1, at:at + 1] = side[slot, i:i + 1]

        def forward(i, carry):
            near = lambda m, plane, shift: grid_x[m, i + 1 + plane, row + shift:row + shift + TILE]
            centre = [near(m, 0, 0) for m in range(6)]
            dx = {m: near(m, 1, 0) - near(m, -1, 0) for m in X_MEMBERS}
            dy = {m: near(m, 0, 1) - near(m, 0, -1) for m in Y_MEMBERS}
            coef = coef_x[pl.ds(pl.multiple_of(i * cy + tile * TILE, 8), TILE), :]
            right = updated(centre, dx, dy, coef * (0.5 / half_step), half_side)
            gain, pivot = gain_x[i, tile_rows(tile)], pivot_x[i, tile_rows(tile)]
            now = [right[m] * pivot + gain * carry[m] for m in range(6)]
            for m in range(6):
                solved_x[m, i, tile_rows(tile)] = now[m]
            return tuple(now)

        lax.fori_loop(0, cx, forward, (jnp.zeros((TILE, cz), jnp.float32),) * 6, unroll=8)
        sweep_back(cx, gain_x, solved_x, tile_rows(tile), 16)
        for half, members in enumerate(HALVES):
            line_x.rhs_start(tile, half, [solved_x[m, 0, tile_rows(tile)] for m in members],
                             [solved_x[m, cx - 1, tile_rows(tile)] for m in members])

    def finish_x(tile):
        rows = tile_rows(tile)
        planes = lambda i: pl.ds((tile * TILE + 1) * wide + TILE + i, TILE, stride=wide)
        ends = [[line_x.ends[end, m, rows] for m in range(6)] for end in range(2)]
        for m in range(6):
            grid_y[m, planes(-1), :] = ends[0][m]
            grid_y[m, planes(cx), :] = ends[1][m]
        for i in range(cx):
            left, right = left_x[i, rows], right_x[i, rows]
            for m in range(6):
                grid_y[m, planes(i), :] = solved_x[m, i, rows] + left * ends[0][m] + right * ends[1][m]

    def scaled_side(j):
        near = lambda m, plane, shift: grid_y[m, pl.ds((j + 1 + plane) * wide + TILE + shift, cx), :]
        centre = [near(m, 0, 0) for m in range(6)]
        dx = {m: near(m, 0, 1) - near(m, 0, -1) for m in X_MEMBERS}
        dy = {m: near(m, 1, 0) - near(m, -1, 0) for m in Y_MEMBERS}
        right = updated(centre, dx, dy, coef_y[j] * (0.5 / half_step), half_side)
        pivot = pivot_y[j]
        return [right[m] * pivot for m in range(6)]

    def advance(j, scaled, carry):
        gain = gain_y[j]
        now = [scaled[m] + gain * carry[m] for m in range(6)]
        for m in range(6):
            solved_y[m, j] = now[m]
        return tuple(now)

    def forward_y(j, carry):
        return advance(j, scaled_side(j), carry)

    def prepare_y(j, carry):
        for m, value in enumerate(scaled_side(j)):
            solved_y[m, j] = value
        return carry

    def resume_y(j, carry):
        return advance(j, [solved_y[m, j] for m in range(6)], carry)

    edge = TILE - 2
    order = [0, tiles_x - 1] + list(range(1, tiles_x - 1))
    for place, tile in enumerate(order):
        solve_x(tile)
        if place == 1:
            line_x.mat_merge(0)
    place_send[1]()
    fill_weights(count, me, fields_on_rows(place_in, ny), weight_high, weight_low)
    chunks = [(tile, half) for tile in order for half in range(len(HALVES))]
    for k in range(line_x.steps - 1):
        for place, chunk in enumerate(chunks):
            line_x.rhs_merge(k, *chunk)
            if place == 1 and k + 1 < line_x.steps - 1:
                line_x.mat_merge(k + 1)
        if k < line_y.steps:
            line_y.mat_merge(k)
    if line_x.steps > 1:
        line_x.mat_merge(line_x.steps - 1)
    for k in range(line_x.steps - 1, line_y.steps):
        line_y.mat_merge(k)
    inv, gain_in, gain_out = line_y.plan[last, 0], line_y.plan[last, 5], line_y.plan[last, 6]
    for j in range(cy):
        left, right = left_y[j], right_y[j]
        for slot, value in enumerate((left, right, (left * gain_in + right * gain_out) * inv)):
            for tile in range(tiles_y):
                packed[pl.ds((j * cx + tile * TILE) * 8 + slot, TILE, stride=8), :] = (
                    value[tile * TILE:(tile + 1) * TILE])
    find.wait()
    weights = gathered(packed, spots_smem)
    factors[...] = weights[2:3]
    tell[1].start()
    carry = (jnp.zeros((cx, cz), jnp.float32),) * 6
    for tile in order:
        for half in range(len(HALVES)):
            line_x.rhs_merge(line_x.steps - 1, tile, half)
        finish_x(tile)
        if tile == 0:
            mid_halo[1]()
            carry = lax.fori_loop(0, edge, forward_y, carry, unroll=6)
        if tile == tiles_x - 1:
            mid_halo[0]()
            lax.fori_loop(cy - edge, cy, prepare_y, 0, unroll=6)
    carry = lax.fori_loop(edge, cy - edge, forward_y, carry, unroll=6)
    lax.fori_loop(cy - edge, cy, resume_y, carry, unroll=6)
    sweep_back(cy, gain_y, solved_y, pl.ds(0, cx), 12)
    mid_halo[2]()

    def ghosts(tile):
        rows = tile_rows(tile)
        found = []
        for ref, at, sign in ((mid_low, 0, 1.0), (mid_high, cy - 1, -1.0)):
            side = sign * half_side / coef_y[at, rows]
            found.append({
                0: ref[5, rows] * (-sign * 0.5 / half_step),
                2: ref[3, rows] * (sign * 0.5 / half_step),
                3: ref[2, rows] * side,
                5: ref[0, rows] * -side,
            })
        return found

    added = [ghosts(tile) for tile in range(tiles_y)]
    for tile in range(tiles_y):
        rows = tile_rows(tile)
        low, high = added[tile]

        def outer(m, at):
            value = solved_y[m, at, rows]
            return value + left_y[at, rows] * low[m] + right_y[at, rows] * high[m] if m in low else value

        for half, members in enumerate(HALVES):
            line_y.rhs_start(tile, half, [outer(m, 0) for m in members], [outer(m, cy - 1) for m in members])
    for tile in range(tiles_y):
        for j in range(cy):
            for m in range(6):
                packed[pl.ds((j * cx + tile * TILE) * 8 + m, TILE, stride=8), :] = solved_y[m, j, tile_rows(tile)]
    values = gathered(packed, spots_smem)
    for k in range(line_y.steps - 1):
        for tile in range(tiles_y):
            for half in range(len(HALVES)):
                line_y.rhs_merge(k, tile, half)
    for tile in range(tiles_y):
        for m in range(6):
            rows = pl.ds(tile * TILE * 8 + m, TILE, stride=8)
            ends = line_y.known_ends(tile, m)
            if m in added[tile][0]:
                ends = [ends[end] + added[tile][end][m] for end in range(2)]
            low_packed[rows, :] = ends[0]
            high_packed[rows, :] = ends[1]
            near_packed[rows, :] = line_y.near_value(tile, m)
    for one in tell:
        one.wait_recv()
    values = (values + weights[0:1] * at_columns(low_packed, at_x, at_z)
              + weights[1:2] * at_columns(high_packed, at_x, at_z))
    theirs = at_columns(near_packed, other_facts[0:1], other_facts[1:2]) * other_factors[...]
    other_hot = (lax.broadcasted_iota(jnp.int32, (count, patches), 0) == other_facts[2:3])
    other_hot = jnp.where(other_hot, 1.0, 0.0).astype(jnp.bfloat16)
    value_send[0](by_owner(hot, rank, [values[m:m + 1] for m in range(6)]),
                  by_owner(other_hot, other_facts[3:4], [theirs[m:m + 1] for m in range(6)]))
    for tile in range(tiles_y):
        for half in range(len(HALVES)):
            line_y.rhs_merge(line_y.steps - 1, tile, half)
        rows = tile_rows(tile)
        ends = [[line_y.ends[end, m, rows] + added[tile][end][m] if m in added[tile][end]
                 else line_y.ends[end, m, rows] for m in range(6)] for end in range(2)]
        for j in range(cy):
            left, right = left_y[j, rows], right_y[j, rows]
            for m in range(6):
                out_ref[pl.ds((m * cx + tile * TILE) * cy + j, TILE, stride=cy), :] = (
                    solved_y[m, j, rows] + left * ends[0][m] + right * ends[1][m])
    for one in tell:
        one.wait_send()
    for halo in [*first_halos, mid_halo]:
        halo[3]()
    line_x.drain()
    line_y.drain()
    place_send[2]()
    value_send[1]()
    high, low = split_bf16(fields_on_rows(value_in, ny))
    both = jnp.concatenate([high, low], axis=0)
    product = dot_rows(both, weight_high[...]) + dot_rows(both, weight_low[...])
    product = (product[:8] + product[8:]) * scale
    angles = far_ref.shape[1]
    for s in range(2):
        far_ref[pl.ds(s * 6, 6), :] = product[:6, s * angles:(s + 1) * angles]
    value_send[2]()


def store_kernel(new_ref, far_ref, new_hbm, far_hbm, sems):
    rows = new_ref.shape[0] // 6
    for m in range(6):
        part = pl.ds(m * rows, rows)
        pltpu.make_async_copy(new_ref.at[part], new_hbm.at[part], sems.at[0]).start()
    far = pltpu.make_async_copy(far_ref, far_hbm, sems.at[1])
    far.start()
    pltpu.make_async_copy(new_ref, new_hbm, sems.at[0]).wait()
    far.wait()


def line_scratch(count, rows, lanes):
    steps = count.bit_length() - 1
    chunks = rows // TILE * len(HALVES)
    f32 = jnp.float32
    return [
        pltpu.VMEM((steps, 4, rows, lanes), f32),
        pltpu.VMEM((steps, 4, rows, lanes), f32),
        pltpu.VMEM((steps, chunks, 2, len(HALVES[0]), TILE, lanes), f32),
        pltpu.VMEM((steps, chunks, 2, len(HALVES[0]), TILE, lanes), f32),
        pltpu.VMEM((steps, 7, rows, lanes), f32),
        pltpu.VMEM((4, rows, lanes), f32),
        pltpu.VMEM((2, 6, rows, lanes), f32),
        pltpu.SemaphoreType.DMA((4,)),
        pltpu.SemaphoreType.DMA((steps,)),
        pltpu.SemaphoreType.DMA((steps, chunks)),
    ]


def local(nx, ny, fields, material, permittivity, patch_cell, patch_owner):
    _, cx, cy, cz = fields.shape
    f32 = jnp.float32
    count = nx * ny
    patches = patch_cell.shape[0]
    vmem = pl.BlockSpec(memory_space=pltpu.VMEM)
    smem = pl.BlockSpec(memory_space=pltpu.SMEM)
    hbm = pl.BlockSpec(memory_space=pltpu.HBM)
    x_lines = [pltpu.VMEM((cx, cy, cz), f32)] * 4
    y_lines = [pltpu.VMEM((cy, cx, cz), f32)] * 4
    pinned = lambda value: pltpu.with_memory_space_constraint(value, pltpu.HBM)
    new_flat, far_field = pl.pallas_call(
        functools.partial(step_kernel, nx, ny, cx, cy, cz, 1.0 / math.sqrt(patches)),
        out_shape=(
            jax.ShapeDtypeStruct((6 * cx * cy, cz), f32),
            jax.ShapeDtypeStruct((12, ANG_DEV), f32),
        ),
        in_specs=[hbm, hbm, smem, vmem, vmem],
        out_specs=(vmem, vmem),
        scratch_shapes=[
            pltpu.VMEM((cx, cy, cz), jnp.int32),
            pltpu.VMEM((6, cx + 2, cy + 2 * TILE, cz), f32),
            pltpu.VMEM((6, (cy + 2) * padded_rows(cx), cz), f32),
            pltpu.VMEM((2, 4, cx, cz), f32),
            pltpu.VMEM((4, cx, cz), f32),
            pltpu.VMEM((4, cx, cz), f32),
            pltpu.VMEM((6, cx, cz), f32),
            pltpu.VMEM((6, cx, cz), f32),
            pltpu.VMEM((cx * cy, cz), f32),
            *x_lines,
            pltpu.VMEM((6, cx, cy, cz), f32),
            pltpu.VMEM((cy, cx, cz), f32),
            *y_lines,
            pltpu.VMEM((6, cy, cx, cz), f32),
            pltpu.VMEM((2 * ANG_DEV, SLOTS * count), jnp.bfloat16),
            pltpu.VMEM((2 * ANG_DEV, SLOTS * count), jnp.bfloat16),
            *[pltpu.VMEM((count, 1, 8 * SLOTS), f32)] * 2,
            *[pltpu.VMEM((count, 2, 8 * SLOTS), f32)] * 2,
            pltpu.VMEM((cx * cy * 8, cz), f32),
            *[pltpu.VMEM((cx * 8, cz), f32)] * 3,
            pltpu.VMEM((2, patches), jnp.int32),
            pltpu.SMEM((2, patches), jnp.int32),
            pltpu.VMEM((4, patches), jnp.int32),
            pltpu.VMEM((4, patches), jnp.int32),
            pltpu.VMEM((1, patches), f32),
            pltpu.VMEM((1, patches), f32),
            pltpu.SemaphoreType.DMA,
            pltpu.SemaphoreType.DMA((2,)),
            pltpu.SemaphoreType.DMA((4, 4)),
            pltpu.SemaphoreType.DMA((2,)),
            pltpu.SemaphoreType.DMA((2,)),
            pltpu.SemaphoreType.DMA((4,)),
            *line_scratch(nx, cy, cz),
            *line_scratch(ny, cx, cz),
        ],
        compiler_params=pltpu.CompilerParams(
            collective_id=0, has_side_effects=True, vmem_limit_bytes=40 * 2**20),
        name="split_step",
    )(pinned(fields), pinned(material), pinned(permittivity), pinned(patch_cell[None, :]),
      pinned(patch_owner.reshape(1, patches)))
    new_flat, far_field = pl.pallas_call(
        store_kernel,
        out_shape=(
            jax.ShapeDtypeStruct((6 * cx * cy, cz), f32),
            jax.ShapeDtypeStruct((12, ANG_DEV), f32),
        ),
        in_specs=[vmem, vmem],
        out_specs=(hbm, hbm),
        scratch_shapes=[pltpu.SemaphoreType.DMA((2,))],
        compiler_params=pltpu.CompilerParams(vmem_limit_bytes=4 * 2**20),
        name="store",
    )(new_flat, far_field)
    return new_flat.reshape(fields.shape), far_field


def solution(mesh):
    return jax.shard_map(
        functools.partial(local, mesh.shape["gx"], mesh.shape["gy"]),
        mesh=mesh,
        in_specs=(
            P(None, "gx", "gy", None),
            P("gx", "gy", None),
            P(),
            P(("gx", "gy")),
            P(("gx", "gy"), None),
        ),
        out_specs=(P(None, "gx", "gy", None), P(None, ("gx", "gy"))),
        check_vma=False,
    )
```

```python
import functools
import math

import jax
import jax.numpy as jnp
from jax import lax
from jax.experimental import pallas as pl
from jax.experimental.pallas import tpu as pltpu
from jax.sharding import PartitionSpec as P

ANG_DEV = 128
COURANT = 64
KAPPA = 0.5
MESH = pl.DeviceIdType.MESH
X_MEMBERS = (1, 2, 4, 5)
Y_MEMBERS = (0, 2, 3, 5)
Z_MEMBERS = (0, 1, 3, 4)
TILE = 8
HALVES = ((0, 1, 2), (3, 4, 5))
SLOTS = 16


def lane_difference(value):
    lanes = value.shape[1]
    at = lax.broadcasted_iota(jnp.int32, value.shape, 1)
    below = jnp.where(at == 0, 0.0, pltpu.roll(value, 1, 1))
    above = jnp.where(at == lanes - 1, 0.0, pltpu.roll(value, lanes - 1, 1))
    return above - below


def updated(centre, dx, dy, half_curl, half_side):
    dz = {m: lane_difference(centre[m]) for m in Z_MEMBERS}
    curl_h = [dy[5] - dz[4], dz[3] - dx[5], dx[4] - dy[3]]
    curl_e = [dy[2] - dz[1], dz[0] - dx[2], dx[1] - dy[0]]
    return [centre[m] + half_curl * curl_h[m] for m in range(3)] + [
        centre[3 + m] - half_side * curl_e[m] for m in range(3)
    ]


def factor(length, coef_at, gain_ref, pivot_ref, left_ref, right_ref):
    zero = jnp.zeros(gain_ref.shape[1:], jnp.float32)

    def forward(i, carry):
        gain_prev, left_prev = carry
        coef = coef_at(i)
        pivot = 1.0 / (1.0 + 2.0 * coef - coef * gain_prev)
        gain = coef * pivot
        left = gain * left_prev
        gain_ref[i] = gain
        pivot_ref[i] = pivot
        left_ref[i] = left
        return gain, left

    lax.fori_loop(0, length, forward, (zero, jnp.ones_like(zero)), unroll=2)

    def backward(k, carry):
        left_next, right_next = carry
        i = length - 1 - k
        gain = gain_ref[i]
        left = left_ref[i] + gain * left_next
        right = gain * right_next
        left_ref[i] = left
        right_ref[i] = right
        return left, right

    lax.fori_loop(0, length, backward, (zero, jnp.ones_like(zero)), unroll=4)


def sweep_back(length, gain_ref, solved_ref, rows, unroll):
    def backward(k, carry):
        i = length - 1 - k
        gain = gain_ref[i, rows]
        now = [solved_ref[m, i, rows] + gain * carry[m] for m in range(6)]
        for m in range(6):
            solved_ref[m, i, rows] = now[m]
        return tuple(now)

    zero = jnp.zeros((rows.size, gain_ref.shape[2]), jnp.float32)
    lax.fori_loop(0, length, backward, (zero,) * 6, unroll=unroll)


def padded_rows(rows):
    return (rows // TILE + 2 | 1) * TILE


def tile_rows(tile):
    return pl.ds(tile * TILE, TILE)


class Line:
    def __init__(self, axis, count, refs):
        (self.mat_out, self.mat_in, self.rhs_out, self.rhs_in, self.plan, self.gains, self.ends,
         self.sent, self.mat_sems, self.rhs_sems) = refs
        self.axis = axis
        self.count = count
        self.steps = count.bit_length() - 1
        self.chunks = self.rhs_out.shape[1]
        self.me = lax.axis_index(axis)

    def near(self, k):
        return 1 - (self.me // 2**k) % 2

    def partner(self, k):
        return {self.axis: self.me + (2 * self.near(k) - 1) * 2**k}

    def mat_copy(self, k):
        source, target, sent = self.mat_out.at[k], self.mat_in.at[k], 0
        if k == self.steps - 1:
            source, target, sent = source.at[3 * self.near(k)], target.at[0], 3
        return pltpu.make_async_remote_copy(
            source, target, self.sent.at[sent], self.mat_sems.at[k],
            device_id=self.partner(k), device_id_type=MESH)

    def rhs_copy(self, k, chunk):
        source, target = self.rhs_out.at[k, chunk], self.rhs_in.at[k, chunk]
        if k == self.steps - 1:
            source, target = source.at[self.near(k)], target.at[0]
        return pltpu.make_async_remote_copy(
            source, target, self.sent.at[1 if k < self.steps - 1 else 2], self.rhs_sems.at[k, chunk],
            device_id=self.partner(k), device_id_type=MESH)

    def mat_start(self, left_ref, right_ref):
        last = left_ref.shape[0] - 1
        for end, at in ((0, 0), (1, last)):
            self.mat_out[0, 2 * end] = left_ref[at]
            self.mat_out[0, 2 * end + 1] = right_ref[at]
        one, zero = jnp.ones(left_ref.shape[1:], jnp.float32), jnp.zeros(left_ref.shape[1:], jnp.float32)
        self.gains[0] = one
        self.gains[1] = zero
        self.gains[2] = zero
        self.gains[3] = one
        self.mat_copy(0).start()

    def mat_merge(self, k):
        self.mat_copy(k).wait_recv()
        n = self.near(k)
        f = 1 - n
        mine = lambda end, side: self.mat_out[k, 2 * end + side]
        other = lambda end, side: self.mat_in[k, 2 * end + side]
        gain_in, gain_out = self.gains[n], self.gains[2 + n]
        if k == self.steps - 1:
            m_nn, o_nn = mine(n, n), self.mat_in[k, 0]
            inv = 1.0 / (1.0 - m_nn * o_nn)
            for slot, value in ((0, inv), (1, o_nn * inv), (5, gain_in), (6, gain_out)):
                self.plan[k, slot] = value
            return
        m_nn, m_fn, m_nf, m_ff = mine(n, n), mine(f, n), mine(n, f), mine(f, f)
        o_nn, o_fn, o_nf, o_ff = other(f, f), other(n, f), other(f, n), other(n, n)
        inv = 1.0 / (1.0 - m_nn * o_nn)
        o_by_m = o_nn * m_nf * inv
        o_by_o = o_nf * inv
        m_by_m = m_nf * inv
        m_by_o = m_nn * o_nf * inv
        for slot, value in enumerate((inv, o_nn * inv, m_nn * inv, m_fn, o_fn, gain_in, gain_out)):
            self.plan[k, slot] = value
        self.mat_out[k + 1, 2 * f + f] = m_ff + m_fn * o_by_m
        self.mat_out[k + 1, 2 * f + n] = m_fn * o_by_o
        self.mat_out[k + 1, 2 * n + n] = o_ff + o_fn * m_by_o
        self.mat_out[k + 1, 2 * n + f] = o_fn * m_by_m
        self.mat_copy(k + 1).start()
        self.gains[f] = self.gains[f] + gain_in * o_by_m
        self.gains[2 + f] = self.gains[2 + f] + gain_out * o_by_m
        self.gains[n] = gain_in * o_by_o
        self.gains[2 + n] = gain_out * o_by_o

    def rhs_start(self, tile, half, firsts, lasts):
        chunk = tile * len(HALVES) + half
        for at in range(len(HALVES[half])):
            self.rhs_out[0, chunk, 0, at] = firsts[at]
            self.rhs_out[0, chunk, 1, at] = lasts[at]
        self.rhs_copy(0, chunk).start()

    def rhs_merge(self, k, tile, half):
        chunk = tile * len(HALVES) + half
        rows = tile_rows(tile)
        self.rhs_copy(k, chunk).wait_recv()
        n = self.near(k)
        f = 1 - n
        ending = k == self.steps - 1
        inv, o_nn, gain_in, gain_out = [self.plan[k, slot, rows] for slot in (0, 1, 5, 6)]
        m_nn, m_fn, o_fn = [None if ending else self.plan[k, slot, rows] for slot in (2, 3, 4)]
        for at, m in enumerate(HALVES[half]):
            mine = self.rhs_out[k, chunk, n, at]
            other = self.rhs_in[k, chunk, 0, at] if ending else self.rhs_in[k, chunk, f, at]
            o_value = other * inv + o_nn * mine
            if not ending:
                m_value = mine * inv + m_nn * other
                self.rhs_out[k + 1, chunk, f, at] = self.rhs_out[k, chunk, f, at] + m_fn * o_value
                self.rhs_out[k + 1, chunk, n, at] = self.rhs_in[k, chunk, n, at] + o_fn * m_value
            into, out_of = gain_in * o_value, gain_out * o_value
            if k > 0:
                into, out_of = self.ends[0, m, rows] + into, self.ends[1, m, rows] + out_of
            self.ends[0, m, rows] = into
            self.ends[1, m, rows] = out_of
        if not ending:
            self.rhs_copy(k + 1, chunk).start()

    def known_ends(self, tile, m):
        k, rows = self.steps - 1, tile_rows(tile)
        scaled = self.plan[k, 1, rows] * self.near_value(tile, m)
        ends = [self.plan[k, 5 + end, rows] * scaled for end in range(2)]
        return [self.ends[end, m, rows] + ends[end] for end in range(2)] if k > 0 else ends

    def place_of(self, tile, m):
        half = next(h for h, members in enumerate(HALVES) if m in members)
        return tile * len(HALVES) + half, HALVES[half].index(m)

    def near_value(self, tile, m):
        k = self.steps - 1
        chunk, at = self.place_of(tile, m)
        return self.rhs_out[k, chunk, self.near(k), at]

    def drain(self):
        early = pl.ds(0, self.steps - 1)
        last = self.steps - 1
        for slot, source, target in (
            (0, self.mat_out.at[early], self.mat_in.at[early]),
            (3, self.mat_out.at[last, 0], self.mat_in.at[last, 0]),
            (1, self.rhs_out.at[early], self.rhs_in.at[early]),
            (2, self.rhs_out.at[last, :, 0], self.rhs_in.at[last, :, 0]),
        ):
            pltpu.make_async_remote_copy(
                source, target, self.sent.at[slot], self.mat_sems.at[0],
                device_id=self.partner(0), device_id_type=MESH).wait_send()


def both_ways(axis, count, out_low, out_high, in_low, in_high, sems):
    me = lax.axis_index(axis)
    up = lambda: pltpu.make_async_remote_copy(
        out_high, in_low, sems.at[0], sems.at[1], device_id={axis: me + 1}, device_id_type=MESH)
    down = lambda: pltpu.make_async_remote_copy(
        out_low, in_high, sems.at[2], sems.at[3], device_id={axis: me - 1}, device_id_type=MESH)

    def start_up():
        @pl.when(me < count - 1)
        def _():
            up().start()

        @pl.when(me == 0)
        def _():
            in_low[...] = jnp.zeros(in_low.shape, jnp.float32)

    def start_down():
        @pl.when(me > 0)
        def _():
            down().start()

        @pl.when(me == count - 1)
        def _():
            in_high[...] = jnp.zeros(in_high.shape, jnp.float32)

    def wait():
        @pl.when(me > 0)
        def _():
            up().wait_recv()

        @pl.when(me < count - 1)
        def _():
            down().wait_recv()

    def drain():
        @pl.when(me < count - 1)
        def _():
            up().wait_send()

        @pl.when(me > 0)
        def _():
            down().wait_send()

    return start_up, start_down, wait, drain


def in_fours(count, act):
    head = (count - 1) % 4
    for k in range(1, 1 + head):
        act(k)

    def four(g, carry):
        for u in range(4):
            act(1 + head + 4 * g + u)
        return carry

    lax.fori_loop(0, (count - 1) // 4, four, 0)


def greet_all(count, ny, me, barrier):
    def hello(k):
        to = lax.rem(me + k, count)
        pl.semaphore_signal(
            barrier, inc=1, device_id=(lax.div(to, ny), lax.rem(to, ny)), device_id_type=MESH)

    def pair(i):
        hello(i)
        hello(count - i)

    in_fours(count // 2, pair)
    hello(count // 2)


def cos_sin(angle):
    turns = jnp.floor(angle * (2.0 / math.pi) + 0.5)
    rest = ((angle - turns * 1.5703125) - turns * 4.837512969970703125e-4) - turns * 7.54978995489188216e-8
    square = rest * rest
    sine = ((-1.9515295891e-4 * square + 8.3321608736e-3) * square - 1.6666654611e-1) * square * rest + rest
    cosine = (
        (2.443315711809948e-5 * square - 1.388731625493765e-3) * square + 4.166664568298827e-2
    ) * square * square - 0.5 * square + 1.0
    quarter = turns.astype(jnp.int32) & 3
    swap = (quarter & 1) == 1
    plain_cos = jnp.where(swap, sine, cosine)
    plain_sin = jnp.where(swap, cosine, sine)
    minus_cos = (quarter == 1) | (quarter == 2)
    return jnp.where(minus_cos, -plain_cos, plain_cos), jnp.where(quarter >= 2, -plain_sin, plain_sin)


def split_bf16(value):
    high = value.astype(jnp.bfloat16)
    return high, (value - high.astype(jnp.float32)).astype(jnp.bfloat16)


def dot_rows(left, right):
    return lax.dot_general(left, right, (((1,), (1,)), ((), ())), preferred_element_type=jnp.float32)


def at_columns(table_ref, at_x, at_z):
    lanes = table_ref.shape[1]
    groups = []
    for first in range(0, at_x.shape[1], lanes):
        here = slice(first, first + lanes)
        where_x = jnp.broadcast_to(at_x[:, here], (8, lanes))
        where_z = jnp.broadcast_to(at_z[:, here], (8, lanes))
        kept = jnp.zeros((8, lanes), jnp.float32)
        for x in range(table_ref.shape[0] // 8):
            found = jnp.take_along_axis(table_ref[x * 8:(x + 1) * 8], where_z, axis=1, mode="promise_in_bounds")
            kept = jnp.where(where_x == x, found, kept)
        groups.append(kept)
    return jnp.concatenate(groups, axis=1)


def slot_ranks(count, owner):
    patches = owner.shape[1]
    hot = lax.broadcasted_iota(jnp.int32, (count, patches), 0) == owner
    before = lax.broadcasted_iota(jnp.int32, (patches, patches), 0) < lax.broadcasted_iota(
        jnp.int32, (patches, patches), 1)
    as_bf16 = lambda mask: jnp.where(mask, 1.0, 0.0).astype(jnp.bfloat16)
    ahead = lax.dot_general(as_bf16(hot), as_bf16(before), (((1,), (0,)), ((), ())),
                            preferred_element_type=jnp.float32)
    rank = jnp.sum(jnp.where(hot, ahead, 0.0), axis=0, keepdims=True)
    return as_bf16(hot), rank.astype(jnp.int32)


def by_owner(hot, rank, values):
    slots = lax.broadcasted_iota(jnp.int32, (SLOTS, rank.shape[1]), 0) == rank
    rows = [jnp.where(slots, value, 0.0) for value in values]
    rows += [jnp.zeros_like(rows[0])] * (8 - len(rows))
    high, low = split_bf16(jnp.concatenate(rows, axis=0))
    both = dot_rows(hot, jnp.concatenate([high, low], axis=0))
    return both[:, :8 * SLOTS] + both[:, 8 * SLOTS:]


def fields_on_rows(landed_ref, ny):
    count, kinds, lanes = landed_ref.shape

    def of(device):
        if kinds == 1:
            return landed_ref[device]
        partner = device + ny // 2 if device % ny < ny // 2 else device - ny // 2
        return landed_ref[device, 0:1] + landed_ref[partner, 1:2]

    row = lax.broadcasted_iota(jnp.int32, (8, lanes), 0)
    block = lax.shift_right_logical(
        lax.broadcasted_iota(jnp.int32, (8, lanes), 1), jnp.full((8, lanes), SLOTS.bit_length() - 1, jnp.int32))
    groups = []
    for g in range(count // 8):
        value = jnp.concatenate([of(g * 8 + i) for i in range(8)], axis=0)
        for bit in (1, 2, 4):
            later = pltpu.roll(pltpu.roll(value, 8 - bit, 0), SLOTS * bit, 1)
            sooner = pltpu.roll(pltpu.roll(value, bit, 0), lanes - SLOTS * bit, 1)
            row_bit, block_bit = row & bit, block & bit
            value = jnp.where(row_bit == block_bit, value, jnp.where(row_bit == 0, later, sooner))
        groups.append(value)
    return jnp.concatenate(groups, axis=1)


def fill_weights(count, me, places, high_ref, low_ref):
    angles = high_ref.shape[0] // 2
    slots = places.shape[1]
    azimuth = jnp.full((16, 128), me.astype(jnp.float32) * (2.0 * math.pi / count))
    cos_phi, sin_phi = cos_sin(azimuth)
    pos = [jnp.broadcast_to(places[c:c + 1], (16, slots)) for c in range(3)]

    def group(g, carry):
        start = pl.multiple_of(g * 16, 16)
        index = (lax.broadcasted_iota(jnp.int32, (16, 128), 0) + start).astype(jnp.float32)
        cos_theta, sin_theta = cos_sin(math.pi * (index + 0.5) / angles)
        for part in range(0, slots, 128):
            at = slice(part, part + 128)
            phase = KAPPA * (pos[0][:, at] * sin_theta * cos_phi + pos[1][:, at] * sin_theta * sin_phi
                             + pos[2][:, at] * cos_theta)
            for s, value in enumerate(cos_sin(phase)):
                high, low = split_bf16(value)
                rows = pl.ds(pl.multiple_of(start + s * angles, 16), 16)
                high_ref[rows, at] = high
                low_ref[rows, at] = low
        return carry

    lax.fori_loop(0, angles // 16, group, 0)


def to_owners(count, ny, me, out_ref, landed_ref, sems):
    def copy(k):
        to = lax.rem(me + k, count)
        return pltpu.make_async_remote_copy(
            out_ref.at[to], landed_ref.at[me], sems.at[0], sems.at[1],
            device_id=(lax.div(to, ny), lax.rem(to, ny)), device_id_type=MESH)

    def start(*kinds):
        for i in range(count):
            for kind, rows in enumerate(kinds):
                out_ref[i, kind:kind + 1] = rows[i:i + 1]
        landed_ref[me] = out_ref[me]
        in_fours(count, lambda k: copy(k).start())

    others = pl.ds(0, count - 1)
    whole = pltpu.make_async_remote_copy(
        out_ref.at[others], landed_ref.at[others], sems.at[0], sems.at[1],
        device_id=(me // ny, me % ny), device_id_type=MESH)
    return start, whole.wait_recv, whole.wait_send


def step_kernel(nx, ny, cx, cy, cz, scale, fields_hbm, material_hbm, permit_hbm,
                cell_hbm, owner_hbm, out_ref, far_ref, material_ref, permit_ref, cell_row, owner_row,
                grid_x, grid_y, y_out, y_low, y_high, mid_low, mid_high, coef_x,
                gain_x, pivot_x, left_x, right_x, solved_x,
                coef_y, gain_y, pivot_y, left_y, right_y, solved_y,
                weight_high, weight_low, place_out, place_in, value_out, value_in, packed, near_packed, low_packed, high_packed, spots, spots_smem,
                facts, other_facts, factors, other_factors,
                load_sem, move_sems, halo_sems, place_sems, value_sems, fact_sems, small_sems, *line_refs):
    half_step = COURANT / 2.0
    half_side = 0.5 * half_step
    count = nx * ny
    wide = padded_rows(cx)
    tiles_x, tiles_y = cy // TILE, cx // TILE
    me = lax.axis_index("gx") * ny + lax.axis_index("gy")
    barrier = pltpu.get_barrier_semaphore()
    inner = grid_x.at[:, pl.ds(1, cx), pl.ds(TILE, cy)]
    load = pltpu.make_async_copy(fields_hbm, inner, load_sem)
    for m in range(6):
        pltpu.make_async_copy(fields_hbm.at[m], inner.at[m], load_sem).start()
    load_material = pltpu.make_async_copy(material_hbm, material_ref, move_sems.at[0])
    load_material.start()
    load_small = [
        pltpu.make_async_copy(source, target, small_sems.at[i])
        for i, (source, target) in enumerate(
            ((permit_hbm, permit_ref), (cell_hbm, cell_row), (owner_hbm, owner_row)))
    ]
    for one in load_small:
        one.start()
    greet_all(count, ny, me, barrier)
    line_x = Line("gx", nx, line_refs[:10])
    line_y = Line("gy", ny, line_refs[10:])

    def x_halo(first, sems):
        plane = lambda i: grid_x.at[pl.ds(first, 2), i, pl.ds(TILE, cy)]
        return both_ways("gx", nx, plane(1), plane(cx), plane(0), plane(cx + 1), sems)

    mid_plane = lambda j: grid_y.at[:, pl.ds((j + 1) * wide + TILE, cx)]
    first_halos = [
        both_ways("gy", ny, y_out.at[0], y_out.at[1], y_low, y_high, halo_sems.at[0]),
        x_halo(1, halo_sems.at[1]),
        x_halo(4, halo_sems.at[2]),
    ]
    mid_halo = both_ways("gy", ny, mid_plane(0), mid_plane(cy - 1), mid_low, mid_high, halo_sems.at[3])

    def coefs(i, carry):
        which = material_ref[i]
        permit = jnp.zeros(which.shape, jnp.float32)
        for entry in range(permit_ref.shape[0]):
            permit = jnp.where(which == entry, permit_ref[entry], permit)
        coef_x[pl.ds(pl.multiple_of(i * cy, 8), cy), :] = (half_step * half_step) / permit
        return carry

    load.wait()
    for slot, member in enumerate(Y_MEMBERS):
        for end, row in ((0, TILE), (1, TILE + cy - 1)):
            y_out[end, slot] = jnp.concatenate(
                [grid_x[member, 1 + i, row:row + 1] for i in range(cx)], axis=0)
    pl.semaphore_wait(barrier, count - 1)
    for halo in first_halos:
        halo[0]()
        halo[1]()
    load_material.wait()
    for one in load_small:
        one.wait()
    lax.fori_loop(0, cx, coefs, 0, unroll=2)
    coef_plane = lambda i: coef_x[pl.ds(pl.multiple_of(i * cy, 8), cy), :]
    factor(cx, coef_plane, gain_x, pivot_x, left_x, right_x)
    line_x.mat_start(left_x, right_x)
    for j in range(cy):
        coef_y[j] = coef_x[pl.ds(j, cx, stride=cy), :]
    for m in range(6):
        for plane in (0, cy + 1):
            grid_y[m, pl.ds(plane * wide, wide), :] = jnp.zeros((wide, cz), jnp.float32)
    patches = cell_row.shape[1]
    cell = cell_row[...]
    line = lax.shift_right_logical(cell, jnp.full_like(cell, cz.bit_length() - 1))
    at_x = jnp.zeros_like(cell)
    for i in range(1, cx):
        at_x = at_x + jnp.where(line >= i * cy, 1, 0)
    at_y, at_z = line - at_x * cy, cell - line * cz
    lanes = lax.broadcasted_iota(jnp.int32, cell.shape, 1)
    spots[0:1] = (at_y * cx + at_x) * 8
    spots[1:2] = (lanes - at_z) & (cz - 1)
    find = pltpu.make_async_copy(spots, spots_smem, move_sems.at[1])
    find.start()
    places = [at_x + lax.axis_index("gx") * cx, at_y + lax.axis_index("gy") * cy, at_z]
    hot, rank = slot_ranks(count, owner_row[...])
    place_send = to_owners(count, ny, me, place_out, place_in, place_sems)
    value_send = to_owners(count, ny, me, value_out, value_in, value_sems)
    place_send[0](by_owner(hot, rank, [place.astype(jnp.float32) for place in places]))
    facts[0:1] = at_x
    facts[1:2] = at_z
    facts[2:3] = owner_row[...]
    facts[3:4] = rank
    last = line_y.steps - 1
    tell = [
        pltpu.make_async_remote_copy(
            source, target, fact_sems.at[2 * i], fact_sems.at[2 * i + 1],
            device_id=line_y.partner(last), device_id_type=MESH)
        for i, (source, target) in enumerate(((facts, other_facts), (factors, other_factors)))
    ]
    tell[0].start()

    def gathered(ref, where_ref):
        lane = lax.broadcasted_iota(jnp.int32, (8, cz), 1)
        found = []
        for first in range(0, patches, cz):
            kept = jnp.zeros((8, cz), jnp.float32)
            for at in range(cz):
                rows = ref[pl.ds(where_ref[0, first + at], 8), :]
                kept = jnp.where(lane == at, pltpu.roll(rows, where_ref[1, first + at], 1), kept)
            found.append(kept)
        return jnp.concatenate(found, axis=1)

    factor(cy, lambda j: coef_y[j], gain_y, pivot_y, left_y, right_y)
    line_y.mat_start(left_y, right_y)
    for halo in first_halos:
        halo[2]()

    def solve_x(tile):
        row = (tile + 1) * TILE
        for at, side, need in ((TILE - 1, y_low, tile == 0), (TILE + cy, y_high, tile == tiles_x - 1)):
            for slot, member in enumerate(Y_MEMBERS if need else ()):
                for i in range(cx):
                    grid_x[member, i + 1, at:at + 1] = side[slot, i:i + 1]

        def forward(i, carry):
            near = lambda m, plane, shift: grid_x[m, i + 1 + plane, row + shift:row + shift + TILE]
            centre = [near(m, 0, 0) for m in range(6)]
            dx = {m: near(m, 1, 0) - near(m, -1, 0) for m in X_MEMBERS}
            dy = {m: near(m, 0, 1) - near(m, 0, -1) for m in Y_MEMBERS}
            coef = coef_x[pl.ds(pl.multiple_of(i * cy + tile * TILE, 8), TILE), :]
            right = updated(centre, dx, dy, coef * (0.5 / half_step), half_side)
            gain, pivot = gain_x[i, tile_rows(tile)], pivot_x[i, tile_rows(tile)]
            now = [right[m] * pivot + gain * carry[m] for m in range(6)]
            for m in range(6):
                solved_x[m, i, tile_rows(tile)] = now[m]
            return tuple(now)

        lax.fori_loop(0, cx, forward, (jnp.zeros((TILE, cz), jnp.float32),) * 6, unroll=8)
        sweep_back(cx, gain_x, solved_x, tile_rows(tile), 16)
        for half, members in enumerate(HALVES):
            line_x.rhs_start(tile, half, [solved_x[m, 0, tile_rows(tile)] for m in members],
                             [solved_x[m, cx - 1, tile_rows(tile)] for m in members])

    def finish_x(tile):
        rows = tile_rows(tile)
        planes = lambda i: pl.ds((tile * TILE + 1) * wide + TILE + i, TILE, stride=wide)
        ends = [[line_x.ends[end, m, rows] for m in range(6)] for end in range(2)]
        for m in range(6):
            grid_y[m, planes(-1), :] = ends[0][m]
            grid_y[m, planes(cx), :] = ends[1][m]
        for i in range(cx):
            left, right = left_x[i, rows], right_x[i, rows]
            for m in range(6):
                grid_y[m, planes(i), :] = solved_x[m, i, rows] + left * ends[0][m] + right * ends[1][m]

    def scaled_side(j):
        near = lambda m, plane, shift: grid_y[m, pl.ds((j + 1 + plane) * wide + TILE + shift, cx), :]
        centre = [near(m, 0, 0) for m in range(6)]
        dx = {m: near(m, 0, 1) - near(m, 0, -1) for m in X_MEMBERS}
        dy = {m: near(m, 1, 0) - near(m, -1, 0) for m in Y_MEMBERS}
        right = updated(centre, dx, dy, coef_y[j] * (0.5 / half_step), half_side)
        pivot = pivot_y[j]
        return [right[m] * pivot for m in range(6)]

    def advance(j, scaled, carry):
        gain = gain_y[j]
        now = [scaled[m] + gain * carry[m] for m in range(6)]
        for m in range(6):
            solved_y[m, j] = now[m]
        return tuple(now)

    def forward_y(j, carry):
        return advance(j, scaled_side(j), carry)

    def prepare_y(j, carry):
        for m, value in enumerate(scaled_side(j)):
            solved_y[m, j] = value
        return carry

    def resume_y(j, carry):
        return advance(j, [solved_y[m, j] for m in range(6)], carry)

    edge = TILE - 2
    order = [0, tiles_x - 1] + list(range(1, tiles_x - 1))
    for place, tile in enumerate(order):
        solve_x(tile)
        if place == 1:
            line_x.mat_merge(0)
    place_send[1]()
    fill_weights(count, me, fields_on_rows(place_in, ny), weight_high, weight_low)
    chunks = [(tile, half) for tile in order for half in range(len(HALVES))]
    for k in range(line_x.steps - 1):
        for place, chunk in enumerate(chunks):
            line_x.rhs_merge(k, *chunk)
            if place == 1 and k + 1 < line_x.steps - 1:
                line_x.mat_merge(k + 1)
        if k < line_y.steps:
            line_y.mat_merge(k)
    if line_x.steps > 1:
        line_x.mat_merge(line_x.steps - 1)
    for k in range(line_x.steps - 1, line_y.steps):
        line_y.mat_merge(k)
    inv, gain_in, gain_out = line_y.plan[last, 0], line_y.plan[last, 5], line_y.plan[last, 6]
    for j in range(cy):
        left, right = left_y[j], right_y[j]
        for slot, value in enumerate((left, right, (left * gain_in + right * gain_out) * inv)):
            for tile in range(tiles_y):
                packed[pl.ds((j * cx + tile * TILE) * 8 + slot, TILE, stride=8), :] = (
                    value[tile * TILE:(tile + 1) * TILE])
    find.wait()
    weights = gathered(packed, spots_smem)
    factors[...] = weights[2:3]
    tell[1].start()
    carry = (jnp.zeros((cx, cz), jnp.float32),) * 6
    for tile in order:
        for half in range(len(HALVES)):
            line_x.rhs_merge(line_x.steps - 1, tile, half)
        finish_x(tile)
        if tile == 0:
            mid_halo[1]()
            carry = lax.fori_loop(0, edge, forward_y, carry, unroll=6)
        if tile == tiles_x - 1:
            mid_halo[0]()
            lax.fori_loop(cy - edge, cy, prepare_y, 0, unroll=6)
    carry = lax.fori_loop(edge, cy - edge, forward_y, carry, unroll=6)
    lax.fori_loop(cy - edge, cy, resume_y, carry, unroll=6)
    sweep_back(cy, gain_y, solved_y, pl.ds(0, cx), 12)
    mid_halo[2]()

    def ghosts(tile):
        rows = tile_rows(tile)
        found = []
        for ref, at, sign in ((mid_low, 0, 1.0), (mid_high, cy - 1, -1.0)):
            side = sign * half_side / coef_y[at, rows]
            found.append({
                0: ref[5, rows] * (-sign * 0.5 / half_step),
                2: ref[3, rows] * (sign * 0.5 / half_step),
                3: ref[2, rows] * side,
                5: ref[0, rows] * -side,
            })
        return found

    added = [ghosts(tile) for tile in range(tiles_y)]
    for tile in range(tiles_y):
        rows = tile_rows(tile)
        low, high = added[tile]

        def outer(m, at):
            value = solved_y[m, at, rows]
            return value + left_y[at, rows] * low[m] + right_y[at, rows] * high[m] if m in low else value

        for half, members in enumerate(HALVES):
            line_y.rhs_start(tile, half, [outer(m, 0) for m in members], [outer(m, cy - 1) for m in members])
    for tile in range(tiles_y):
        for j in range(cy):
            for m in range(6):
                packed[pl.ds((j * cx + tile * TILE) * 8 + m, TILE, stride=8), :] = solved_y[m, j, tile_rows(tile)]
    values = gathered(packed, spots_smem)
    for k in range(line_y.steps - 1):
        for tile in range(tiles_y):
            for half in range(len(HALVES)):
                line_y.rhs_merge(k, tile, half)
    for tile in range(tiles_y):
        for m in range(6):
            rows = pl.ds(tile * TILE * 8 + m, TILE, stride=8)
            ends = line_y.known_ends(tile, m)
            if m in added[tile][0]:
                ends = [ends[end] + added[tile][end][m] for end in range(2)]
            low_packed[rows, :] = ends[0]
            high_packed[rows, :] = ends[1]
            near_packed[rows, :] = line_y.near_value(tile, m)
    for one in tell:
        one.wait_recv()
    values = (values + weights[0:1] * at_columns(low_packed, at_x, at_z)
              + weights[1:2] * at_columns(high_packed, at_x, at_z))
    theirs = at_columns(near_packed, other_facts[0:1], other_facts[1:2]) * other_factors[...]
    other_hot = (lax.broadcasted_iota(jnp.int32, (count, patches), 0) == other_facts[2:3])
    other_hot = jnp.where(other_hot, 1.0, 0.0).astype(jnp.bfloat16)
    value_send[0](by_owner(hot, rank, [values[m:m + 1] for m in range(6)]),
                  by_owner(other_hot, other_facts[3:4], [theirs[m:m + 1] for m in range(6)]))
    for tile in range(tiles_y):
        for half in range(len(HALVES)):
            line_y.rhs_merge(line_y.steps - 1, tile, half)
        rows = tile_rows(tile)
        ends = [[line_y.ends[end, m, rows] + added[tile][end][m] if m in added[tile][end]
                 else line_y.ends[end, m, rows] for m in range(6)] for end in range(2)]
        for j in range(cy):
            left, right = left_y[j, rows], right_y[j, rows]
            for m in range(6):
                out_ref[pl.ds((m * cx + tile * TILE) * cy + j, TILE, stride=cy), :] = (
                    solved_y[m, j, rows] + left * ends[0][m] + right * ends[1][m])
    for one in tell:
        one.wait_send()
    for halo in [*first_halos, mid_halo]:
        halo[3]()
    line_x.drain()
    line_y.drain()
    place_send[2]()
    value_send[1]()
    high, low = split_bf16(fields_on_rows(value_in, ny))
    both = jnp.concatenate([high, low], axis=0)
    product = dot_rows(both, weight_high[...]) + dot_rows(both, weight_low[...])
    product = (product[:8] + product[8:]) * scale
    angles = far_ref.shape[1]
    for s in range(2):
        far_ref[pl.ds(s * 6, 6), :] = product[:6, s * angles:(s + 1) * angles]
    value_send[2]()


def store_kernel(new_ref, far_ref, new_hbm, far_hbm, sems):
    rows = new_ref.shape[0] // 6
    for m in range(6):
        part = pl.ds(m * rows, rows)
        pltpu.make_async_copy(new_ref.at[part], new_hbm.at[part], sems.at[0]).start()
    far = pltpu.make_async_copy(far_ref, far_hbm, sems.at[1])
    far.start()
    pltpu.make_async_copy(new_ref, new_hbm, sems.at[0]).wait()
    far.wait()


def line_scratch(count, rows, lanes):
    steps = count.bit_length() - 1
    chunks = rows // TILE * len(HALVES)
    f32 = jnp.float32
    return [
        pltpu.VMEM((steps, 4, rows, lanes), f32),
        pltpu.VMEM((steps, 4, rows, lanes), f32),
        pltpu.VMEM((steps, chunks, 2, len(HALVES[0]), TILE, lanes), f32),
        pltpu.VMEM((steps, chunks, 2, len(HALVES[0]), TILE, lanes), f32),
        pltpu.VMEM((steps, 7, rows, lanes), f32),
        pltpu.VMEM((4, rows, lanes), f32),
        pltpu.VMEM((2, 6, rows, lanes), f32),
        pltpu.SemaphoreType.DMA((4,)),
        pltpu.SemaphoreType.DMA((steps,)),
        pltpu.SemaphoreType.DMA((steps, chunks)),
    ]


def local(nx, ny, fields, material, permittivity, patch_cell, patch_owner):
    _, cx, cy, cz = fields.shape
    f32 = jnp.float32
    count = nx * ny
    patches = patch_cell.shape[0]
    vmem = pl.BlockSpec(memory_space=pltpu.VMEM)
    hbm = pl.BlockSpec(memory_space=pltpu.HBM)
    x_lines = [pltpu.VMEM((cx, cy, cz), f32)] * 4
    y_lines = [pltpu.VMEM((cy, cx, cz), f32)] * 4
    pinned = lambda value: pltpu.with_memory_space_constraint(value, pltpu.HBM)
    new_flat, far_field = pl.pallas_call(
        functools.partial(step_kernel, nx, ny, cx, cy, cz, 1.0 / math.sqrt(patches)),
        out_shape=(
            jax.ShapeDtypeStruct((6 * cx * cy, cz), f32),
            jax.ShapeDtypeStruct((12, ANG_DEV), f32),
        ),
        in_specs=[hbm] * 5,
        out_specs=(vmem, vmem),
        scratch_shapes=[
            pltpu.VMEM((cx, cy, cz), jnp.int32),
            pltpu.SMEM(permittivity.shape, f32),
            pltpu.VMEM((1, patches), jnp.int32),
            pltpu.VMEM((1, patches), jnp.int32),
            pltpu.VMEM((6, cx + 2, cy + 2 * TILE, cz), f32),
            pltpu.VMEM((6, (cy + 2) * padded_rows(cx), cz), f32),
            pltpu.VMEM((2, 4, cx, cz), f32),
            pltpu.VMEM((4, cx, cz), f32),
            pltpu.VMEM((4, cx, cz), f32),
            pltpu.VMEM((6, cx, cz), f32),
            pltpu.VMEM((6, cx, cz), f32),
            pltpu.VMEM((cx * cy, cz), f32),
            *x_lines,
            pltpu.VMEM((6, cx, cy, cz), f32),
            pltpu.VMEM((cy, cx, cz), f32),
            *y_lines,
            pltpu.VMEM((6, cy, cx, cz), f32),
            pltpu.VMEM((2 * ANG_DEV, SLOTS * count), jnp.bfloat16),
            pltpu.VMEM((2 * ANG_DEV, SLOTS * count), jnp.bfloat16),
            *[pltpu.VMEM((count, 1, 8 * SLOTS), f32)] * 2,
            *[pltpu.VMEM((count, 2, 8 * SLOTS), f32)] * 2,
            pltpu.VMEM((cx * cy * 8, cz), f32),
            *[pltpu.VMEM((cx * 8, cz), f32)] * 3,
            pltpu.VMEM((2, patches), jnp.int32),
            pltpu.SMEM((2, patches), jnp.int32),
            pltpu.VMEM((4, patches), jnp.int32),
            pltpu.VMEM((4, patches), jnp.int32),
            pltpu.VMEM((1, patches), f32),
            pltpu.VMEM((1, patches), f32),
            pltpu.SemaphoreType.DMA,
            pltpu.SemaphoreType.DMA((2,)),
            pltpu.SemaphoreType.DMA((4, 4)),
            pltpu.SemaphoreType.DMA((2,)),
            pltpu.SemaphoreType.DMA((2,)),
            pltpu.SemaphoreType.DMA((4,)),
            pltpu.SemaphoreType.DMA((3,)),
            *line_scratch(nx, cy, cz),
            *line_scratch(ny, cx, cz),
        ],
        compiler_params=pltpu.CompilerParams(
            collective_id=0, has_side_effects=True, vmem_limit_bytes=40 * 2**20),
        name="split_step",
    )(pinned(fields), pinned(material), pinned(permittivity), pinned(patch_cell[None, :]),
      pinned(patch_owner.reshape(1, patches)))
    new_flat, far_field = pl.pallas_call(
        store_kernel,
        out_shape=(
            jax.ShapeDtypeStruct((6 * cx * cy, cz), f32),
            jax.ShapeDtypeStruct((12, ANG_DEV), f32),
        ),
        in_specs=[vmem, vmem],
        out_specs=(hbm, hbm),
        scratch_shapes=[pltpu.SemaphoreType.DMA((2,))],
        compiler_params=pltpu.CompilerParams(vmem_limit_bytes=4 * 2**20),
        name="store",
    )(new_flat, far_field)
    return new_flat.reshape(fields.shape), far_field


def solution(mesh):
    return jax.shard_map(
        functools.partial(local, mesh.shape["gx"], mesh.shape["gy"]),
        mesh=mesh,
        in_specs=(
            P(None, "gx", "gy", None),
            P("gx", "gy", None),
            P(),
            P(("gx", "gy")),
            P(("gx", "gy"), None),
        ),
        out_specs=(P(None, "gx", "gy", None), P(None, ("gx", "gy"))),
        check_vma=False,
    )
```

```python
import functools
import math

import jax
import jax.numpy as jnp
from jax import lax
from jax.experimental import pallas as pl
from jax.experimental.pallas import tpu as pltpu
from jax.sharding import PartitionSpec as P

ANG_DEV = 128
COURANT = 64
KAPPA = 0.5
MESH = pl.DeviceIdType.MESH
X_MEMBERS = (1, 2, 4, 5)
Y_MEMBERS = (0, 2, 3, 5)
Z_MEMBERS = (0, 1, 3, 4)
TILE = 8
HALVES = ((0, 1, 2), (3, 4, 5))
SLOTS = 16


def lane_difference(value):
    lanes = value.shape[1]
    at = lax.broadcasted_iota(jnp.int32, value.shape, 1)
    below = jnp.where(at == 0, 0.0, pltpu.roll(value, 1, 1))
    above = jnp.where(at == lanes - 1, 0.0, pltpu.roll(value, lanes - 1, 1))
    return above - below


def updated(centre, dx, dy, dz, half_curl, half_side):
    curl_h = [dy[5] - dz[4], dz[3] - dx[5], dx[4] - dy[3]]
    curl_e = [dy[2] - dz[1], dz[0] - dx[2], dx[1] - dy[0]]
    return [centre[m] + half_curl * curl_h[m] for m in range(3)] + [
        centre[3 + m] - half_side * curl_e[m] for m in range(3)
    ]


def factor(length, coef_at, gain_ref, pivot_ref, left_ref, right_ref):
    zero = jnp.zeros(gain_ref.shape[1:], jnp.float32)

    def forward(i, carry):
        gain_prev, left_prev = carry
        coef = coef_at(i)
        pivot = 1.0 / (1.0 + 2.0 * coef - coef * gain_prev)
        gain = coef * pivot
        left = gain * left_prev
        gain_ref[i] = gain
        pivot_ref[i] = pivot
        left_ref[i] = left
        return gain, left

    lax.fori_loop(0, length, forward, (zero, jnp.ones_like(zero)), unroll=2)

    def backward(k, carry):
        left_next, right_next = carry
        i = length - 1 - k
        gain = gain_ref[i]
        left = left_ref[i] + gain * left_next
        right = gain * right_next
        left_ref[i] = left
        right_ref[i] = right
        return left, right

    lax.fori_loop(0, length, backward, (zero, jnp.ones_like(zero)), unroll=4)


def sweep_back(length, gain_ref, solved_ref, rows, unroll):
    def backward(k, carry):
        i = length - 1 - k
        gain = gain_ref[i, rows]
        now = [solved_ref[m, i, rows] + gain * carry[m] for m in range(6)]
        for m in range(6):
            solved_ref[m, i, rows] = now[m]
        return tuple(now)

    zero = jnp.zeros((rows.size, gain_ref.shape[2]), jnp.float32)
    lax.fori_loop(0, length, backward, (zero,) * 6, unroll=unroll)


def padded_rows(rows):
    return (rows // TILE + 2 | 1) * TILE


def tile_rows(tile):
    return pl.ds(tile * TILE, TILE)


class Line:
    def __init__(self, axis, count, refs):
        (self.mat_out, self.mat_in, self.rhs_out, self.rhs_in, self.plan, self.gains, self.ends,
         self.sent, self.mat_sems, self.rhs_sems) = refs
        self.axis = axis
        self.count = count
        self.steps = count.bit_length() - 1
        self.chunks = self.rhs_out.shape[1]
        self.me = lax.axis_index(axis)

    def near(self, k):
        return 1 - (self.me // 2**k) % 2

    def partner(self, k):
        return {self.axis: self.me + (2 * self.near(k) - 1) * 2**k}

    def mat_copy(self, k):
        source, target, sent = self.mat_out.at[k], self.mat_in.at[k], 0
        if k == self.steps - 1:
            source, target, sent = source.at[3 * self.near(k)], target.at[0], 3
        return pltpu.make_async_remote_copy(
            source, target, self.sent.at[sent], self.mat_sems.at[k],
            device_id=self.partner(k), device_id_type=MESH)

    def rhs_copy(self, k, chunk):
        source, target = self.rhs_out.at[k, chunk], self.rhs_in.at[k, chunk]
        if k == self.steps - 1:
            source, target = source.at[self.near(k)], target.at[0]
        return pltpu.make_async_remote_copy(
            source, target, self.sent.at[1 if k < self.steps - 1 else 2], self.rhs_sems.at[k, chunk],
            device_id=self.partner(k), device_id_type=MESH)

    def mat_start(self, left_ref, right_ref):
        last = left_ref.shape[0] - 1
        for end, at in ((0, 0), (1, last)):
            self.mat_out[0, 2 * end] = left_ref[at]
            self.mat_out[0, 2 * end + 1] = right_ref[at]
        one, zero = jnp.ones(left_ref.shape[1:], jnp.float32), jnp.zeros(left_ref.shape[1:], jnp.float32)
        self.gains[0] = one
        self.gains[1] = zero
        self.gains[2] = zero
        self.gains[3] = one
        self.mat_copy(0).start()

    def mat_merge(self, k):
        self.mat_copy(k).wait_recv()
        n = self.near(k)
        f = 1 - n
        mine = lambda end, side: self.mat_out[k, 2 * end + side]
        other = lambda end, side: self.mat_in[k, 2 * end + side]
        gain_in, gain_out = self.gains[n], self.gains[2 + n]
        if k == self.steps - 1:
            m_nn, o_nn = mine(n, n), self.mat_in[k, 0]
            inv = 1.0 / (1.0 - m_nn * o_nn)
            for slot, value in ((0, inv), (1, o_nn * inv), (5, gain_in), (6, gain_out)):
                self.plan[k, slot] = value
            return
        m_nn, m_fn, m_nf, m_ff = mine(n, n), mine(f, n), mine(n, f), mine(f, f)
        o_nn, o_fn, o_nf, o_ff = other(f, f), other(n, f), other(f, n), other(n, n)
        inv = 1.0 / (1.0 - m_nn * o_nn)
        o_by_m = o_nn * m_nf * inv
        o_by_o = o_nf * inv
        m_by_m = m_nf * inv
        m_by_o = m_nn * o_nf * inv
        for slot, value in enumerate((inv, o_nn * inv, m_nn * inv, m_fn, o_fn, gain_in, gain_out)):
            self.plan[k, slot] = value
        self.mat_out[k + 1, 2 * f + f] = m_ff + m_fn * o_by_m
        self.mat_out[k + 1, 2 * f + n] = m_fn * o_by_o
        self.mat_out[k + 1, 2 * n + n] = o_ff + o_fn * m_by_o
        self.mat_out[k + 1, 2 * n + f] = o_fn * m_by_m
        self.mat_copy(k + 1).start()
        self.gains[f] = self.gains[f] + gain_in * o_by_m
        self.gains[2 + f] = self.gains[2 + f] + gain_out * o_by_m
        self.gains[n] = gain_in * o_by_o
        self.gains[2 + n] = gain_out * o_by_o

    def rhs_start(self, tile, half, firsts, lasts):
        chunk = tile * len(HALVES) + half
        for at in range(len(HALVES[half])):
            self.rhs_out[0, chunk, 0, at] = firsts[at]
            self.rhs_out[0, chunk, 1, at] = lasts[at]
        self.rhs_copy(0, chunk).start()

    def rhs_merge(self, k, tile, half):
        chunk = tile * len(HALVES) + half
        rows = tile_rows(tile)
        self.rhs_copy(k, chunk).wait_recv()
        n = self.near(k)
        f = 1 - n
        ending = k == self.steps - 1
        inv, o_nn, gain_in, gain_out = [self.plan[k, slot, rows] for slot in (0, 1, 5, 6)]
        m_nn, m_fn, o_fn = [None if ending else self.plan[k, slot, rows] for slot in (2, 3, 4)]
        for at, m in enumerate(HALVES[half]):
            mine = self.rhs_out[k, chunk, n, at]
            other = self.rhs_in[k, chunk, 0, at] if ending else self.rhs_in[k, chunk, f, at]
            o_value = other * inv + o_nn * mine
            if not ending:
                m_value = mine * inv + m_nn * other
                self.rhs_out[k + 1, chunk, f, at] = self.rhs_out[k, chunk, f, at] + m_fn * o_value
                self.rhs_out[k + 1, chunk, n, at] = self.rhs_in[k, chunk, n, at] + o_fn * m_value
            into, out_of = gain_in * o_value, gain_out * o_value
            if k > 0:
                into, out_of = self.ends[0, m, rows] + into, self.ends[1, m, rows] + out_of
            self.ends[0, m, rows] = into
            self.ends[1, m, rows] = out_of
        if not ending:
            self.rhs_copy(k + 1, chunk).start()

    def known_ends(self, tile, m):
        k, rows = self.steps - 1, tile_rows(tile)
        scaled = self.plan[k, 1, rows] * self.near_value(tile, m)
        ends = [self.plan[k, 5 + end, rows] * scaled for end in range(2)]
        return [self.ends[end, m, rows] + ends[end] for end in range(2)] if k > 0 else ends

    def place_of(self, tile, m):
        half = next(h for h, members in enumerate(HALVES) if m in members)
        return tile * len(HALVES) + half, HALVES[half].index(m)

    def near_value(self, tile, m):
        k = self.steps - 1
        chunk, at = self.place_of(tile, m)
        return self.rhs_out[k, chunk, self.near(k), at]

    def drain(self):
        early = pl.ds(0, self.steps - 1)
        last = self.steps - 1
        for slot, source, target in (
            (0, self.mat_out.at[early], self.mat_in.at[early]),
            (3, self.mat_out.at[last, 0], self.mat_in.at[last, 0]),
            (1, self.rhs_out.at[early], self.rhs_in.at[early]),
            (2, self.rhs_out.at[last, :, 0], self.rhs_in.at[last, :, 0]),
        ):
            pltpu.make_async_remote_copy(
                source, target, self.sent.at[slot], self.mat_sems.at[0],
                device_id=self.partner(0), device_id_type=MESH).wait_send()


def both_ways(axis, count, out_low, out_high, in_low, in_high, sems):
    me = lax.axis_index(axis)
    up = lambda: pltpu.make_async_remote_copy(
        out_high, in_low, sems.at[0], sems.at[1], device_id={axis: me + 1}, device_id_type=MESH)
    down = lambda: pltpu.make_async_remote_copy(
        out_low, in_high, sems.at[2], sems.at[3], device_id={axis: me - 1}, device_id_type=MESH)

    def start_up():
        @pl.when(me < count - 1)
        def _():
            up().start()

        @pl.when(me == 0)
        def _():
            in_low[...] = jnp.zeros(in_low.shape, jnp.float32)

    def start_down():
        @pl.when(me > 0)
        def _():
            down().start()

        @pl.when(me == count - 1)
        def _():
            in_high[...] = jnp.zeros(in_high.shape, jnp.float32)

    def wait():
        @pl.when(me > 0)
        def _():
            up().wait_recv()

        @pl.when(me < count - 1)
        def _():
            down().wait_recv()

    def drain():
        @pl.when(me < count - 1)
        def _():
            up().wait_send()

        @pl.when(me > 0)
        def _():
            down().wait_send()

    return start_up, start_down, wait, drain


def in_fours(count, act):
    head = (count - 1) % 4
    for k in range(1, 1 + head):
        act(k)

    def four(g, carry):
        for u in range(4):
            act(1 + head + 4 * g + u)
        return carry

    lax.fori_loop(0, (count - 1) // 4, four, 0)


def greet_all(count, ny, me, barrier):
    def hello(k):
        to = lax.rem(me + k, count)
        pl.semaphore_signal(
            barrier, inc=1, device_id=(lax.div(to, ny), lax.rem(to, ny)), device_id_type=MESH)

    def pair(i):
        hello(i)
        hello(count - i)

    in_fours(count // 2, pair)
    hello(count // 2)


def cos_sin(angle):
    turns = jnp.floor(angle * (2.0 / math.pi) + 0.5)
    rest = ((angle - turns * 1.5703125) - turns * 4.837512969970703125e-4) - turns * 7.54978995489188216e-8
    square = rest * rest
    sine = ((-1.9515295891e-4 * square + 8.3321608736e-3) * square - 1.6666654611e-1) * square * rest + rest
    cosine = (
        (2.443315711809948e-5 * square - 1.388731625493765e-3) * square + 4.166664568298827e-2
    ) * square * square - 0.5 * square + 1.0
    quarter = turns.astype(jnp.int32) & 3
    swap = (quarter & 1) == 1
    plain_cos = jnp.where(swap, sine, cosine)
    plain_sin = jnp.where(swap, cosine, sine)
    minus_cos = (quarter == 1) | (quarter == 2)
    return jnp.where(minus_cos, -plain_cos, plain_cos), jnp.where(quarter >= 2, -plain_sin, plain_sin)


def split_bf16(value):
    high = value.astype(jnp.bfloat16)
    return high, (value - high.astype(jnp.float32)).astype(jnp.bfloat16)


def dot_rows(left, right):
    return lax.dot_general(left, right, (((1,), (1,)), ((), ())), preferred_element_type=jnp.float32)


def at_columns(table_ref, at_x, at_z):
    lanes = table_ref.shape[1]
    groups = []
    for first in range(0, at_x.shape[1], lanes):
        here = slice(first, first + lanes)
        where_x = jnp.broadcast_to(at_x[:, here], (8, lanes))
        where_z = jnp.broadcast_to(at_z[:, here], (8, lanes))
        kept = jnp.zeros((8, lanes), jnp.float32)
        for x in range(table_ref.shape[0] // 8):
            found = jnp.take_along_axis(table_ref[x * 8:(x + 1) * 8], where_z, axis=1, mode="promise_in_bounds")
            kept = jnp.where(where_x == x, found, kept)
        groups.append(kept)
    return jnp.concatenate(groups, axis=1)


def slot_ranks(count, owner):
    patches = owner.shape[1]
    hot = lax.broadcasted_iota(jnp.int32, (count, patches), 0) == owner
    before = lax.broadcasted_iota(jnp.int32, (patches, patches), 0) < lax.broadcasted_iota(
        jnp.int32, (patches, patches), 1)
    as_bf16 = lambda mask: jnp.where(mask, 1.0, 0.0).astype(jnp.bfloat16)
    ahead = lax.dot_general(as_bf16(hot), as_bf16(before), (((1,), (0,)), ((), ())),
                            preferred_element_type=jnp.float32)
    rank = jnp.sum(jnp.where(hot, ahead, 0.0), axis=0, keepdims=True)
    return as_bf16(hot), rank.astype(jnp.int32)


def by_owner(hot, rank, values):
    slots = lax.broadcasted_iota(jnp.int32, (SLOTS, rank.shape[1]), 0) == rank
    rows = [jnp.where(slots, value, 0.0) for value in values]
    rows += [jnp.zeros_like(rows[0])] * (8 - len(rows))
    high, low = split_bf16(jnp.concatenate(rows, axis=0))
    both = dot_rows(hot, jnp.concatenate([high, low], axis=0))
    return both[:, :8 * SLOTS] + both[:, 8 * SLOTS:]


def fields_on_rows(landed_ref, ny):
    count, kinds, lanes = landed_ref.shape

    def of(device):
        if kinds == 1:
            return landed_ref[device]
        partner = device + ny // 2 if device % ny < ny // 2 else device - ny // 2
        return landed_ref[device, 0:1] + landed_ref[partner, 1:2]

    row = lax.broadcasted_iota(jnp.int32, (8, lanes), 0)
    block = lax.shift_right_logical(
        lax.broadcasted_iota(jnp.int32, (8, lanes), 1), jnp.full((8, lanes), SLOTS.bit_length() - 1, jnp.int32))
    groups = []
    for g in range(count // 8):
        value = jnp.concatenate([of(g * 8 + i) for i in range(8)], axis=0)
        for bit in (1, 2, 4):
            later = pltpu.roll(pltpu.roll(value, 8 - bit, 0), SLOTS * bit, 1)
            sooner = pltpu.roll(pltpu.roll(value, bit, 0), lanes - SLOTS * bit, 1)
            row_bit, block_bit = row & bit, block & bit
            value = jnp.where(row_bit == block_bit, value, jnp.where(row_bit == 0, later, sooner))
        groups.append(value)
    return jnp.concatenate(groups, axis=1)


def fill_weights(count, me, places, high_ref, low_ref):
    angles = high_ref.shape[0] // 2
    slots = places.shape[1]
    azimuth = jnp.full((16, 128), me.astype(jnp.float32) * (2.0 * math.pi / count))
    cos_phi, sin_phi = cos_sin(azimuth)
    pos = [jnp.broadcast_to(places[c:c + 1], (16, slots)) for c in range(3)]

    def group(g, carry):
        start = pl.multiple_of(g * 16, 16)
        index = (lax.broadcasted_iota(jnp.int32, (16, 128), 0) + start).astype(jnp.float32)
        cos_theta, sin_theta = cos_sin(math.pi * (index + 0.5) / angles)
        for part in range(0, slots, 128):
            at = slice(part, part + 128)
            phase = KAPPA * (pos[0][:, at] * sin_theta * cos_phi + pos[1][:, at] * sin_theta * sin_phi
                             + pos[2][:, at] * cos_theta)
            for s, value in enumerate(cos_sin(phase)):
                high, low = split_bf16(value)
                rows = pl.ds(pl.multiple_of(start + s * angles, 16), 16)
                high_ref[rows, at] = high
                low_ref[rows, at] = low
        return carry

    lax.fori_loop(0, angles // 16, group, 0)


def to_owners(count, ny, me, out_ref, landed_ref, sems):
    def copy(k):
        to = lax.rem(me + k, count)
        return pltpu.make_async_remote_copy(
            out_ref.at[to], landed_ref.at[me], sems.at[0], sems.at[1],
            device_id=(lax.div(to, ny), lax.rem(to, ny)), device_id_type=MESH)

    def start(*kinds):
        for i in range(count):
            for kind, rows in enumerate(kinds):
                out_ref[i, kind:kind + 1] = rows[i:i + 1]
        landed_ref[me] = out_ref[me]
        in_fours(count, lambda k: copy(k).start())

    others = pl.ds(0, count - 1)
    whole = pltpu.make_async_remote_copy(
        out_ref.at[others], landed_ref.at[others], sems.at[0], sems.at[1],
        device_id=(me // ny, me % ny), device_id_type=MESH)
    return start, whole.wait_recv, whole.wait_send


def step_kernel(nx, ny, cx, cy, cz, scale, fields_hbm, material_hbm, permit_hbm,
                cell_hbm, owner_hbm, out_ref, far_ref, material_ref, permit_ref, cell_row, owner_row,
                grid_x, slopes_z, grid_y, y_out, y_low, y_high, mid_low, mid_high, coef_x,
                gain_x, pivot_x, left_x, right_x, solved_x,
                coef_y, gain_y, pivot_y, left_y, right_y, solved_y,
                weight_high, weight_low, place_out, place_in, value_out, value_in, packed, near_packed, low_packed, high_packed, spots, spots_smem,
                facts, other_facts, factors, other_factors,
                load_sem, move_sems, halo_sems, place_sems, value_sems, fact_sems, small_sems, *line_refs):
    half_step = COURANT / 2.0
    half_side = 0.5 * half_step
    count = nx * ny
    wide = padded_rows(cx)
    tiles_x, tiles_y = cy // TILE, cx // TILE
    me = lax.axis_index("gx") * ny + lax.axis_index("gy")
    barrier = pltpu.get_barrier_semaphore()
    inner = grid_x.at[:, pl.ds(1, cx), pl.ds(TILE, cy)]
    load = pltpu.make_async_copy(fields_hbm, inner, load_sem)
    for m in range(6):
        pltpu.make_async_copy(fields_hbm.at[m], inner.at[m], load_sem).start()
    load_material = pltpu.make_async_copy(material_hbm, material_ref, move_sems.at[0])
    load_material.start()
    load_small = [
        pltpu.make_async_copy(source, target, small_sems.at[i])
        for i, (source, target) in enumerate(
            ((permit_hbm, permit_ref), (cell_hbm, cell_row), (owner_hbm, owner_row)))
    ]
    for one in load_small:
        one.start()
    greet_all(count, ny, me, barrier)
    line_x = Line("gx", nx, line_refs[:10])
    line_y = Line("gy", ny, line_refs[10:])

    def x_halo(first, sems):
        plane = lambda i: grid_x.at[pl.ds(first, 2), i, pl.ds(TILE, cy)]
        return both_ways("gx", nx, plane(1), plane(cx), plane(0), plane(cx + 1), sems)

    mid_plane = lambda j: grid_y.at[:, pl.ds((j + 1) * wide + TILE, cx)]
    first_halos = [
        both_ways("gy", ny, y_out.at[0], y_out.at[1], y_low, y_high, halo_sems.at[0]),
        x_halo(1, halo_sems.at[1]),
        x_halo(4, halo_sems.at[2]),
    ]
    mid_halo = both_ways("gy", ny, mid_plane(0), mid_plane(cy - 1), mid_low, mid_high, halo_sems.at[3])

    def coefs(i, carry):
        which = material_ref[i]
        permit = jnp.zeros(which.shape, jnp.float32)
        for entry in range(permit_ref.shape[0]):
            permit = jnp.where(which == entry, permit_ref[entry], permit)
        coef_x[pl.ds(pl.multiple_of(i * cy, 8), cy), :] = (half_step * half_step) / permit
        return carry

    load.wait()
    for slot, member in enumerate(Y_MEMBERS):
        for end, row in ((0, TILE), (1, TILE + cy - 1)):
            y_out[end, slot] = jnp.concatenate(
                [grid_x[member, 1 + i, row:row + 1] for i in range(cx)], axis=0)
    pl.semaphore_wait(barrier, count - 1)
    for halo in first_halos:
        halo[0]()
        halo[1]()
    load_material.wait()
    for one in load_small:
        one.wait()
    lax.fori_loop(0, cx, coefs, 0, unroll=2)
    coef_plane = lambda i: coef_x[pl.ds(pl.multiple_of(i * cy, 8), cy), :]
    factor(cx, coef_plane, gain_x, pivot_x, left_x, right_x)
    line_x.mat_start(left_x, right_x)
    for j in range(cy):
        coef_y[j] = coef_x[pl.ds(j, cx, stride=cy), :]
    for m in range(6):
        for plane in (0, cy + 1):
            grid_y[m, pl.ds(plane * wide, wide), :] = jnp.zeros((wide, cz), jnp.float32)
    patches = cell_row.shape[1]
    cell = cell_row[...]
    line = lax.shift_right_logical(cell, jnp.full_like(cell, cz.bit_length() - 1))
    at_x = jnp.zeros_like(cell)
    for i in range(1, cx):
        at_x = at_x + jnp.where(line >= i * cy, 1, 0)
    at_y, at_z = line - at_x * cy, cell - line * cz
    lanes = lax.broadcasted_iota(jnp.int32, cell.shape, 1)
    spots[0:1] = (at_y * cx + at_x) * 8
    spots[1:2] = (lanes - at_z) & (cz - 1)
    find = pltpu.make_async_copy(spots, spots_smem, move_sems.at[1])
    find.start()
    places = [at_x + lax.axis_index("gx") * cx, at_y + lax.axis_index("gy") * cy, at_z]
    hot, rank = slot_ranks(count, owner_row[...])
    place_send = to_owners(count, ny, me, place_out, place_in, place_sems)
    value_send = to_owners(count, ny, me, value_out, value_in, value_sems)
    place_send[0](by_owner(hot, rank, [place.astype(jnp.float32) for place in places]))
    facts[0:1] = at_x
    facts[1:2] = at_z
    facts[2:3] = owner_row[...]
    facts[3:4] = rank
    last = line_y.steps - 1
    tell = [
        pltpu.make_async_remote_copy(
            source, target, fact_sems.at[2 * i], fact_sems.at[2 * i + 1],
            device_id=line_y.partner(last), device_id_type=MESH)
        for i, (source, target) in enumerate(((facts, other_facts), (factors, other_factors)))
    ]
    tell[0].start()

    def gathered(ref, where_ref):
        lane = lax.broadcasted_iota(jnp.int32, (8, cz), 1)
        found = []
        for first in range(0, patches, cz):
            kept = jnp.zeros((8, cz), jnp.float32)
            for at in range(cz):
                rows = ref[pl.ds(where_ref[0, first + at], 8), :]
                kept = jnp.where(lane == at, pltpu.roll(rows, where_ref[1, first + at], 1), kept)
            found.append(kept)
        return jnp.concatenate(found, axis=1)

    factor(cy, lambda j: coef_y[j], gain_y, pivot_y, left_y, right_y)
    line_y.mat_start(left_y, right_y)
    def along_z(i, carry):
        for slot, m in enumerate(Z_MEMBERS):
            slopes_z[slot, i] = lane_difference(grid_x[m, i + 1, pl.ds(TILE, cy)])
        return carry

    lax.fori_loop(0, cx, along_z, 0, unroll=4)
    for halo in first_halos:
        halo[2]()

    def solve_x(tile):
        row = (tile + 1) * TILE
        for at, side, need in ((TILE - 1, y_low, tile == 0), (TILE + cy, y_high, tile == tiles_x - 1)):
            for slot, member in enumerate(Y_MEMBERS if need else ()):
                for i in range(cx):
                    grid_x[member, i + 1, at:at + 1] = side[slot, i:i + 1]

        def forward(i, carry):
            near = lambda m, plane, shift: grid_x[m, i + 1 + plane, row + shift:row + shift + TILE]
            centre = [near(m, 0, 0) for m in range(6)]
            dx = {m: near(m, 1, 0) - near(m, -1, 0) for m in X_MEMBERS}
            dy = {m: near(m, 0, 1) - near(m, 0, -1) for m in Y_MEMBERS}
            coef = coef_x[pl.ds(pl.multiple_of(i * cy + tile * TILE, 8), TILE), :]
            dz = {m: slopes_z[slot, i, tile_rows(tile)] for slot, m in enumerate(Z_MEMBERS)}
            right = updated(centre, dx, dy, dz, coef * (0.5 / half_step), half_side)
            gain, pivot = gain_x[i, tile_rows(tile)], pivot_x[i, tile_rows(tile)]
            now = [right[m] * pivot + gain * carry[m] for m in range(6)]
            for m in range(6):
                solved_x[m, i, tile_rows(tile)] = now[m]
            return tuple(now)

        lax.fori_loop(0, cx, forward, (jnp.zeros((TILE, cz), jnp.float32),) * 6, unroll=8)
        sweep_back(cx, gain_x, solved_x, tile_rows(tile), 16)
        for half, members in enumerate(HALVES):
            line_x.rhs_start(tile, half, [solved_x[m, 0, tile_rows(tile)] for m in members],
                             [solved_x[m, cx - 1, tile_rows(tile)] for m in members])

    def finish_x(tile):
        rows = tile_rows(tile)
        planes = lambda i: pl.ds((tile * TILE + 1) * wide + TILE + i, TILE, stride=wide)
        ends = [[line_x.ends[end, m, rows] for m in range(6)] for end in range(2)]
        for m in range(6):
            grid_y[m, planes(-1), :] = ends[0][m]
            grid_y[m, planes(cx), :] = ends[1][m]
        for i in range(cx):
            left, right = left_x[i, rows], right_x[i, rows]
            for m in range(6):
                grid_y[m, planes(i), :] = solved_x[m, i, rows] + left * ends[0][m] + right * ends[1][m]

    def scaled_side(j):
        near = lambda m, plane, shift: grid_y[m, pl.ds((j + 1 + plane) * wide + TILE + shift, cx), :]
        centre = [near(m, 0, 0) for m in range(6)]
        dx = {m: near(m, 0, 1) - near(m, 0, -1) for m in X_MEMBERS}
        dy = {m: near(m, 1, 0) - near(m, -1, 0) for m in Y_MEMBERS}
        dz = {m: lane_difference(centre[m]) for m in Z_MEMBERS}
        right = updated(centre, dx, dy, dz, coef_y[j] * (0.5 / half_step), half_side)
        pivot = pivot_y[j]
        return [right[m] * pivot for m in range(6)]

    def advance(j, scaled, carry):
        gain = gain_y[j]
        now = [scaled[m] + gain * carry[m] for m in range(6)]
        for m in range(6):
            solved_y[m, j] = now[m]
        return tuple(now)

    def forward_y(j, carry):
        return advance(j, scaled_side(j), carry)

    def prepare_y(j, carry):
        for m, value in enumerate(scaled_side(j)):
            solved_y[m, j] = value
        return carry

    def resume_y(j, carry):
        return advance(j, [solved_y[m, j] for m in range(6)], carry)

    edge = TILE - 2
    order = [0, tiles_x - 1] + list(range(1, tiles_x - 1))
    for place, tile in enumerate(order):
        solve_x(tile)
        if place == 1:
            line_x.mat_merge(0)
    place_send[1]()
    fill_weights(count, me, fields_on_rows(place_in, ny), weight_high, weight_low)
    chunks = [(tile, half) for tile in order for half in range(len(HALVES))]
    for k in range(line_x.steps - 1):
        for place, chunk in enumerate(chunks):
            line_x.rhs_merge(k, *chunk)
            if place == 3 and k + 1 < line_x.steps - 1:
                line_x.mat_merge(k + 1)
        if k < line_y.steps:
            line_y.mat_merge(k)
    if line_x.steps > 1:
        line_x.mat_merge(line_x.steps - 1)
    for k in range(line_x.steps - 1, line_y.steps):
        line_y.mat_merge(k)
    inv, gain_in, gain_out = line_y.plan[last, 0], line_y.plan[last, 5], line_y.plan[last, 6]
    for j in range(cy):
        left, right = left_y[j], right_y[j]
        for slot, value in enumerate((left, right, (left * gain_in + right * gain_out) * inv)):
            for tile in range(tiles_y):
                packed[pl.ds((j * cx + tile * TILE) * 8 + slot, TILE, stride=8), :] = (
                    value[tile * TILE:(tile + 1) * TILE])
    find.wait()
    weights = gathered(packed, spots_smem)
    factors[...] = weights[2:3]
    tell[1].start()
    carry = (jnp.zeros((cx, cz), jnp.float32),) * 6
    for tile in order:
        for half in range(len(HALVES)):
            line_x.rhs_merge(line_x.steps - 1, tile, half)
        finish_x(tile)
        if tile == 0:
            mid_halo[1]()
            carry = lax.fori_loop(0, edge, forward_y, carry, unroll=6)
        if tile == tiles_x - 1:
            mid_halo[0]()
            lax.fori_loop(cy - edge, cy, prepare_y, 0, unroll=6)
    carry = lax.fori_loop(edge, cy - edge, forward_y, carry, unroll=6)
    lax.fori_loop(cy - edge, cy, resume_y, carry, unroll=6)
    sweep_back(cy, gain_y, solved_y, pl.ds(0, cx), 12)
    mid_halo[2]()

    def ghosts(tile):
        rows = tile_rows(tile)
        found = []
        for ref, at, sign in ((mid_low, 0, 1.0), (mid_high, cy - 1, -1.0)):
            side = sign * half_side / coef_y[at, rows]
            found.append({
                0: ref[5, rows] * (-sign * 0.5 / half_step),
                2: ref[3, rows] * (sign * 0.5 / half_step),
                3: ref[2, rows] * side,
                5: ref[0, rows] * -side,
            })
        return found

    added = [ghosts(tile) for tile in range(tiles_y)]
    for tile in range(tiles_y):
        rows = tile_rows(tile)
        low, high = added[tile]

        def outer(m, at):
            value = solved_y[m, at, rows]
            return value + left_y[at, rows] * low[m] + right_y[at, rows] * high[m] if m in low else value

        for half, members in enumerate(HALVES):
            line_y.rhs_start(tile, half, [outer(m, 0) for m in members], [outer(m, cy - 1) for m in members])
    for tile in range(tiles_y):
        for j in range(cy):
            for m in range(6):
                packed[pl.ds((j * cx + tile * TILE) * 8 + m, TILE, stride=8), :] = solved_y[m, j, tile_rows(tile)]
    values = gathered(packed, spots_smem)
    for k in range(line_y.steps - 1):
        for tile in range(tiles_y):
            for half in range(len(HALVES)):
                line_y.rhs_merge(k, tile, half)
    for tile in range(tiles_y):
        for m in range(6):
            rows = pl.ds(tile * TILE * 8 + m, TILE, stride=8)
            ends = line_y.known_ends(tile, m)
            if m in added[tile][0]:
                ends = [ends[end] + added[tile][end][m] for end in range(2)]
            low_packed[rows, :] = ends[0]
            high_packed[rows, :] = ends[1]
            near_packed[rows, :] = line_y.near_value(tile, m)
    for one in tell:
        one.wait_recv()
    values = (values + weights[0:1] * at_columns(low_packed, at_x, at_z)
              + weights[1:2] * at_columns(high_packed, at_x, at_z))
    theirs = at_columns(near_packed, other_facts[0:1], other_facts[1:2]) * other_factors[...]
    other_hot = (lax.broadcasted_iota(jnp.int32, (count, patches), 0) == other_facts[2:3])
    other_hot = jnp.where(other_hot, 1.0, 0.0).astype(jnp.bfloat16)
    value_send[0](by_owner(hot, rank, [values[m:m + 1] for m in range(6)]),
                  by_owner(other_hot, other_facts[3:4], [theirs[m:m + 1] for m in range(6)]))
    for tile in range(tiles_y):
        for half in range(len(HALVES)):
            line_y.rhs_merge(line_y.steps - 1, tile, half)
        rows = tile_rows(tile)
        ends = [[line_y.ends[end, m, rows] + added[tile][end][m] if m in added[tile][end]
                 else line_y.ends[end, m, rows] for m in range(6)] for end in range(2)]
        for j in range(cy):
            left, right = left_y[j, rows], right_y[j, rows]
            for m in range(6):
                out_ref[pl.ds((m * cx + tile * TILE) * cy + j, TILE, stride=cy), :] = (
                    solved_y[m, j, rows] + left * ends[0][m] + right * ends[1][m])
    for one in tell:
        one.wait_send()
    for halo in [*first_halos, mid_halo]:
        halo[3]()
    line_x.drain()
    line_y.drain()
    place_send[2]()
    value_send[1]()
    high, low = split_bf16(fields_on_rows(value_in, ny))
    both = jnp.concatenate([high, low], axis=0)
    product = dot_rows(both, weight_high[...]) + dot_rows(both, weight_low[...])
    product = (product[:8] + product[8:]) * scale
    angles = far_ref.shape[1]
    for s in range(2):
        far_ref[pl.ds(s * 6, 6), :] = product[:6, s * angles:(s + 1) * angles]
    value_send[2]()


def store_kernel(new_ref, far_ref, new_hbm, far_hbm, sems):
    rows = new_ref.shape[0] // 6
    for m in range(6):
        part = pl.ds(m * rows, rows)
        pltpu.make_async_copy(new_ref.at[part], new_hbm.at[part], sems.at[0]).start()
    far = pltpu.make_async_copy(far_ref, far_hbm, sems.at[1])
    far.start()
    pltpu.make_async_copy(new_ref, new_hbm, sems.at[0]).wait()
    far.wait()


def line_scratch(count, rows, lanes):
    steps = count.bit_length() - 1
    chunks = rows // TILE * len(HALVES)
    f32 = jnp.float32
    return [
        pltpu.VMEM((steps, 4, rows, lanes), f32),
        pltpu.VMEM((steps, 4, rows, lanes), f32),
        pltpu.VMEM((steps, chunks, 2, len(HALVES[0]), TILE, lanes), f32),
        pltpu.VMEM((steps, chunks, 2, len(HALVES[0]), TILE, lanes), f32),
        pltpu.VMEM((steps, 7, rows, lanes), f32),
        pltpu.VMEM((4, rows, lanes), f32),
        pltpu.VMEM((2, 6, rows, lanes), f32),
        pltpu.SemaphoreType.DMA((4,)),
        pltpu.SemaphoreType.DMA((steps,)),
        pltpu.SemaphoreType.DMA((steps, chunks)),
    ]


def local(nx, ny, fields, material, permittivity, patch_cell, patch_owner):
    _, cx, cy, cz = fields.shape
    f32 = jnp.float32
    count = nx * ny
    patches = patch_cell.shape[0]
    vmem = pl.BlockSpec(memory_space=pltpu.VMEM)
    hbm = pl.BlockSpec(memory_space=pltpu.HBM)
    x_lines = [pltpu.VMEM((cx, cy, cz), f32)] * 4
    y_lines = [pltpu.VMEM((cy, cx, cz), f32)] * 4
    pinned = lambda value: pltpu.with_memory_space_constraint(value, pltpu.HBM)
    new_flat, far_field = pl.pallas_call(
        functools.partial(step_kernel, nx, ny, cx, cy, cz, 1.0 / math.sqrt(patches)),
        out_shape=(
            jax.ShapeDtypeStruct((6 * cx * cy, cz), f32),
            jax.ShapeDtypeStruct((12, ANG_DEV), f32),
        ),
        in_specs=[hbm] * 5,
        out_specs=(vmem, vmem),
        scratch_shapes=[
            pltpu.VMEM((cx, cy, cz), jnp.int32),
            pltpu.SMEM(permittivity.shape, f32),
            pltpu.VMEM((1, patches), jnp.int32),
            pltpu.VMEM((1, patches), jnp.int32),
            pltpu.VMEM((6, cx + 2, cy + 2 * TILE, cz), f32),
            pltpu.VMEM((len(Z_MEMBERS), cx, cy, cz), f32),
            pltpu.VMEM((6, (cy + 2) * padded_rows(cx), cz), f32),
            pltpu.VMEM((2, 4, cx, cz), f32),
            pltpu.VMEM((4, cx, cz), f32),
            pltpu.VMEM((4, cx, cz), f32),
            pltpu.VMEM((6, cx, cz), f32),
            pltpu.VMEM((6, cx, cz), f32),
            pltpu.VMEM((cx * cy, cz), f32),
            *x_lines,
            pltpu.VMEM((6, cx, cy, cz), f32),
            pltpu.VMEM((cy, cx, cz), f32),
            *y_lines,
            pltpu.VMEM((6, cy, cx, cz), f32),
            pltpu.VMEM((2 * ANG_DEV, SLOTS * count), jnp.bfloat16),
            pltpu.VMEM((2 * ANG_DEV, SLOTS * count), jnp.bfloat16),
            *[pltpu.VMEM((count, 1, 8 * SLOTS), f32)] * 2,
            *[pltpu.VMEM((count, 2, 8 * SLOTS), f32)] * 2,
            pltpu.VMEM((cx * cy * 8, cz), f32),
            *[pltpu.VMEM((cx * 8, cz), f32)] * 3,
            pltpu.VMEM((2, patches), jnp.int32),
            pltpu.SMEM((2, patches), jnp.int32),
            pltpu.VMEM((4, patches), jnp.int32),
            pltpu.VMEM((4, patches), jnp.int32),
            pltpu.VMEM((1, patches), f32),
            pltpu.VMEM((1, patches), f32),
            pltpu.SemaphoreType.DMA,
            pltpu.SemaphoreType.DMA((2,)),
            pltpu.SemaphoreType.DMA((4, 4)),
            pltpu.SemaphoreType.DMA((2,)),
            pltpu.SemaphoreType.DMA((2,)),
            pltpu.SemaphoreType.DMA((4,)),
            pltpu.SemaphoreType.DMA((3,)),
            *line_scratch(nx, cy, cz),
            *line_scratch(ny, cx, cz),
        ],
        compiler_params=pltpu.CompilerParams(
            collective_id=0, has_side_effects=True, vmem_limit_bytes=40 * 2**20),
        name="split_step",
    )(pinned(fields), pinned(material), pinned(permittivity), pinned(patch_cell[None, :]),
      pinned(patch_owner.reshape(1, patches)))
    new_flat, far_field = pl.pallas_call(
        store_kernel,
        out_shape=(
            jax.ShapeDtypeStruct((6 * cx * cy, cz), f32),
            jax.ShapeDtypeStruct((12, ANG_DEV), f32),
        ),
        in_specs=[vmem, vmem],
        out_specs=(hbm, hbm),
        scratch_shapes=[pltpu.SemaphoreType.DMA((2,))],
        compiler_params=pltpu.CompilerParams(vmem_limit_bytes=4 * 2**20),
        name="store",
    )(new_flat, far_field)
    return new_flat.reshape(fields.shape), far_field


def solution(mesh):
    return jax.shard_map(
        functools.partial(local, mesh.shape["gx"], mesh.shape["gy"]),
        mesh=mesh,
        in_specs=(
            P(None, "gx", "gy", None),
            P("gx", "gy", None),
            P(),
            P(("gx", "gy")),
            P(("gx", "gy"), None),
        ),
        out_specs=(P(None, "gx", "gy", None), P(None, ("gx", "gy"))),
        check_vma=False,
    )
```

```python
import functools
import math

import jax
import jax.numpy as jnp
from jax import lax
from jax.experimental import pallas as pl
from jax.experimental.pallas import tpu as pltpu
from jax.sharding import PartitionSpec as P

ANG_DEV = 128
COURANT = 64
KAPPA = 0.5
MESH = pl.DeviceIdType.MESH
X_MEMBERS = (1, 2, 4, 5)
Y_MEMBERS = (0, 2, 3, 5)
Z_MEMBERS = (0, 1, 3, 4)
TILE = 8
HALVES = ((0, 1, 2), (3, 4, 5))
SLOTS = 16


def lane_difference(value):
    lanes = value.shape[1]
    at = lax.broadcasted_iota(jnp.int32, value.shape, 1)
    below = jnp.where(at == 0, 0.0, pltpu.roll(value, 1, 1))
    above = jnp.where(at == lanes - 1, 0.0, pltpu.roll(value, lanes - 1, 1))
    return above - below


def updated(centre, dx, dy, dz, half_curl, half_side):
    curl_h = [dy[5] - dz[4], dz[3] - dx[5], dx[4] - dy[3]]
    curl_e = [dy[2] - dz[1], dz[0] - dx[2], dx[1] - dy[0]]
    return [centre[m] + half_curl * curl_h[m] for m in range(3)] + [
        centre[3 + m] - half_side * curl_e[m] for m in range(3)
    ]


def factor(length, coef_at, gain_ref, pivot_ref, left_ref, right_ref):
    zero = jnp.zeros(gain_ref.shape[1:], jnp.float32)

    def forward(i, carry):
        gain_prev, left_prev = carry
        coef = coef_at(i)
        pivot = 1.0 / (1.0 + 2.0 * coef - coef * gain_prev)
        gain = coef * pivot
        left = gain * left_prev
        gain_ref[i] = gain
        pivot_ref[i] = pivot
        left_ref[i] = left
        return gain, left

    lax.fori_loop(0, length, forward, (zero, jnp.ones_like(zero)), unroll=2)

    def backward(k, carry):
        left_next, right_next = carry
        i = length - 1 - k
        gain = gain_ref[i]
        left = left_ref[i] + gain * left_next
        right = gain * right_next
        left_ref[i] = left
        right_ref[i] = right
        return left, right

    lax.fori_loop(0, length, backward, (zero, jnp.ones_like(zero)), unroll=4)


def sweep_back(length, gain_ref, solved_ref, rows, unroll):
    def backward(k, carry):
        i = length - 1 - k
        gain = gain_ref[i, rows]
        now = [solved_ref[m, i, rows] + gain * carry[m] for m in range(6)]
        for m in range(6):
            solved_ref[m, i, rows] = now[m]
        return tuple(now)

    zero = jnp.zeros((rows.size, gain_ref.shape[2]), jnp.float32)
    lax.fori_loop(0, length, backward, (zero,) * 6, unroll=unroll)


def padded_rows(rows):
    return (rows // TILE + 2 | 1) * TILE


def tile_rows(tile):
    return pl.ds(tile * TILE, TILE)


class Line:
    def __init__(self, axis, count, refs):
        (self.mat_out, self.mat_in, self.rhs_out, self.rhs_in, self.plan, self.gains, self.ends,
         self.sent, self.mat_sems, self.rhs_sems) = refs
        self.axis = axis
        self.count = count
        self.steps = count.bit_length() - 1
        self.chunks = self.rhs_out.shape[1]
        self.me = lax.axis_index(axis)

    def near(self, k):
        return 1 - (self.me // 2**k) % 2

    def partner(self, k):
        return {self.axis: self.me + (2 * self.near(k) - 1) * 2**k}

    def mat_copy(self, k):
        source, target, sent = self.mat_out.at[k], self.mat_in.at[k], 0
        if k == self.steps - 1:
            source, target, sent = source.at[3 * self.near(k)], target.at[0], 3
        return pltpu.make_async_remote_copy(
            source, target, self.sent.at[sent], self.mat_sems.at[k],
            device_id=self.partner(k), device_id_type=MESH)

    def rhs_copy(self, k, chunk):
        source, target = self.rhs_out.at[k, chunk], self.rhs_in.at[k, chunk]
        if k == self.steps - 1:
            source, target = source.at[self.near(k)], target.at[0]
        return pltpu.make_async_remote_copy(
            source, target, self.sent.at[1 if k < self.steps - 1 else 2], self.rhs_sems.at[k, chunk],
            device_id=self.partner(k), device_id_type=MESH)

    def mat_start(self, left_ref, right_ref):
        last = left_ref.shape[0] - 1
        for end, at in ((0, 0), (1, last)):
            self.mat_out[0, 2 * end] = left_ref[at]
            self.mat_out[0, 2 * end + 1] = right_ref[at]
        one, zero = jnp.ones(left_ref.shape[1:], jnp.float32), jnp.zeros(left_ref.shape[1:], jnp.float32)
        self.gains[0] = one
        self.gains[1] = zero
        self.gains[2] = zero
        self.gains[3] = one
        self.mat_copy(0).start()

    def mat_merge(self, k):
        self.mat_copy(k).wait_recv()
        n = self.near(k)
        f = 1 - n
        mine = lambda end, side: self.mat_out[k, 2 * end + side]
        other = lambda end, side: self.mat_in[k, 2 * end + side]
        gain_in, gain_out = self.gains[n], self.gains[2 + n]
        if k == self.steps - 1:
            m_nn, o_nn = mine(n, n), self.mat_in[k, 0]
            inv = 1.0 / (1.0 - m_nn * o_nn)
            for slot, value in ((0, inv), (1, o_nn * inv), (5, gain_in), (6, gain_out)):
                self.plan[k, slot] = value
            return
        m_nn, m_fn, m_nf, m_ff = mine(n, n), mine(f, n), mine(n, f), mine(f, f)
        o_nn, o_fn, o_nf, o_ff = other(f, f), other(n, f), other(f, n), other(n, n)
        inv = 1.0 / (1.0 - m_nn * o_nn)
        o_by_m = o_nn * m_nf * inv
        o_by_o = o_nf * inv
        m_by_m = m_nf * inv
        m_by_o = m_nn * o_nf * inv
        for slot, value in enumerate((inv, o_nn * inv, m_nn * inv, m_fn, o_fn, gain_in, gain_out)):
            self.plan[k, slot] = value
        self.mat_out[k + 1, 2 * f + f] = m_ff + m_fn * o_by_m
        self.mat_out[k + 1, 2 * f + n] = m_fn * o_by_o
        self.mat_out[k + 1, 2 * n + n] = o_ff + o_fn * m_by_o
        self.mat_out[k + 1, 2 * n + f] = o_fn * m_by_m
        self.mat_copy(k + 1).start()
        self.gains[f] = self.gains[f] + gain_in * o_by_m
        self.gains[2 + f] = self.gains[2 + f] + gain_out * o_by_m
        self.gains[n] = gain_in * o_by_o
        self.gains[2 + n] = gain_out * o_by_o

    def rhs_start(self, tile, half, firsts, lasts):
        chunk = tile * len(HALVES) + half
        for at in range(len(HALVES[half])):
            self.rhs_out[0, chunk, 0, at] = firsts[at]
            self.rhs_out[0, chunk, 1, at] = lasts[at]
        self.rhs_copy(0, chunk).start()

    def rhs_merge(self, k, tile, half):
        chunk = tile * len(HALVES) + half
        rows = tile_rows(tile)
        self.rhs_copy(k, chunk).wait_recv()
        n = self.near(k)
        f = 1 - n
        ending = k == self.steps - 1
        inv, o_nn, gain_in, gain_out = [self.plan[k, slot, rows] for slot in (0, 1, 5, 6)]
        m_nn, m_fn, o_fn = [None if ending else self.plan[k, slot, rows] for slot in (2, 3, 4)]
        for at, m in enumerate(HALVES[half]):
            mine = self.rhs_out[k, chunk, n, at]
            other = self.rhs_in[k, chunk, 0, at] if ending else self.rhs_in[k, chunk, f, at]
            o_value = other * inv + o_nn * mine
            if not ending:
                m_value = mine * inv + m_nn * other
                self.rhs_out[k + 1, chunk, f, at] = self.rhs_out[k, chunk, f, at] + m_fn * o_value
                self.rhs_out[k + 1, chunk, n, at] = self.rhs_in[k, chunk, n, at] + o_fn * m_value
            into, out_of = gain_in * o_value, gain_out * o_value
            if k > 0:
                into, out_of = self.ends[0, m, rows] + into, self.ends[1, m, rows] + out_of
            self.ends[0, m, rows] = into
            self.ends[1, m, rows] = out_of
        if not ending:
            self.rhs_copy(k + 1, chunk).start()

    def known_ends(self, tile, m):
        k, rows = self.steps - 1, tile_rows(tile)
        scaled = self.plan[k, 1, rows] * self.near_value(tile, m)
        ends = [self.plan[k, 5 + end, rows] * scaled for end in range(2)]
        return [self.ends[end, m, rows] + ends[end] for end in range(2)] if k > 0 else ends

    def place_of(self, tile, m):
        half = next(h for h, members in enumerate(HALVES) if m in members)
        return tile * len(HALVES) + half, HALVES[half].index(m)

    def near_value(self, tile, m):
        k = self.steps - 1
        chunk, at = self.place_of(tile, m)
        return self.rhs_out[k, chunk, self.near(k), at]

    def drain(self):
        early = pl.ds(0, self.steps - 1)
        last = self.steps - 1
        for slot, source, target in (
            (0, self.mat_out.at[early], self.mat_in.at[early]),
            (3, self.mat_out.at[last, 0], self.mat_in.at[last, 0]),
            (1, self.rhs_out.at[early], self.rhs_in.at[early]),
            (2, self.rhs_out.at[last, :, 0], self.rhs_in.at[last, :, 0]),
        ):
            pltpu.make_async_remote_copy(
                source, target, self.sent.at[slot], self.mat_sems.at[0],
                device_id=self.partner(0), device_id_type=MESH).wait_send()


def both_ways(axis, count, out_low, out_high, in_low, in_high, sems):
    me = lax.axis_index(axis)
    up = lambda: pltpu.make_async_remote_copy(
        out_high, in_low, sems.at[0], sems.at[1], device_id={axis: me + 1}, device_id_type=MESH)
    down = lambda: pltpu.make_async_remote_copy(
        out_low, in_high, sems.at[2], sems.at[3], device_id={axis: me - 1}, device_id_type=MESH)

    def start_up():
        @pl.when(me < count - 1)
        def _():
            up().start()

        @pl.when(me == 0)
        def _():
            in_low[...] = jnp.zeros(in_low.shape, jnp.float32)

    def start_down():
        @pl.when(me > 0)
        def _():
            down().start()

        @pl.when(me == count - 1)
        def _():
            in_high[...] = jnp.zeros(in_high.shape, jnp.float32)

    def wait():
        @pl.when(me > 0)
        def _():
            up().wait_recv()

        @pl.when(me < count - 1)
        def _():
            down().wait_recv()

    def drain():
        @pl.when(me < count - 1)
        def _():
            up().wait_send()

        @pl.when(me > 0)
        def _():
            down().wait_send()

    return start_up, start_down, wait, drain


def in_fours(count, act):
    head = (count - 1) % 4
    for k in range(1, 1 + head):
        act(k)

    def four(g, carry):
        for u in range(4):
            act(1 + head + 4 * g + u)
        return carry

    lax.fori_loop(0, (count - 1) // 4, four, 0)


def greet_all(count, ny, me, barrier):
    def hello(k):
        to = lax.rem(me + k, count)
        pl.semaphore_signal(
            barrier, inc=1, device_id=(lax.div(to, ny), lax.rem(to, ny)), device_id_type=MESH)

    def pair(i):
        hello(i)
        hello(count - i)

    in_fours(count // 2, pair)
    hello(count // 2)


def cos_sin(angle):
    turns = jnp.floor(angle * (2.0 / math.pi) + 0.5)
    rest = ((angle - turns * 1.5703125) - turns * 4.837512969970703125e-4) - turns * 7.54978995489188216e-8
    square = rest * rest
    sine = ((-1.9515295891e-4 * square + 8.3321608736e-3) * square - 1.6666654611e-1) * square * rest + rest
    cosine = (
        (2.443315711809948e-5 * square - 1.388731625493765e-3) * square + 4.166664568298827e-2
    ) * square * square - 0.5 * square + 1.0
    quarter = turns.astype(jnp.int32) & 3
    swap = (quarter & 1) == 1
    plain_cos = jnp.where(swap, sine, cosine)
    plain_sin = jnp.where(swap, cosine, sine)
    minus_cos = (quarter == 1) | (quarter == 2)
    return jnp.where(minus_cos, -plain_cos, plain_cos), jnp.where(quarter >= 2, -plain_sin, plain_sin)


def split_bf16(value):
    high = value.astype(jnp.bfloat16)
    return high, (value - high.astype(jnp.float32)).astype(jnp.bfloat16)


def dot_rows(left, right):
    return lax.dot_general(left, right, (((1,), (1,)), ((), ())), preferred_element_type=jnp.float32)


def at_columns(table_ref, at_x, at_z):
    lanes = table_ref.shape[1]
    groups = []
    for first in range(0, at_x.shape[1], lanes):
        here = slice(first, first + lanes)
        where_x = jnp.broadcast_to(at_x[:, here], (8, lanes))
        where_z = jnp.broadcast_to(at_z[:, here], (8, lanes))
        kept = jnp.zeros((8, lanes), jnp.float32)
        for x in range(table_ref.shape[0] // 8):
            found = jnp.take_along_axis(table_ref[x * 8:(x + 1) * 8], where_z, axis=1, mode="promise_in_bounds")
            kept = jnp.where(where_x == x, found, kept)
        groups.append(kept)
    return jnp.concatenate(groups, axis=1)


def slot_ranks(count, owner):
    patches = owner.shape[1]
    hot = lax.broadcasted_iota(jnp.int32, (count, patches), 0) == owner
    before = lax.broadcasted_iota(jnp.int32, (patches, patches), 0) < lax.broadcasted_iota(
        jnp.int32, (patches, patches), 1)
    as_bf16 = lambda mask: jnp.where(mask, 1.0, 0.0).astype(jnp.bfloat16)
    ahead = lax.dot_general(as_bf16(hot), as_bf16(before), (((1,), (0,)), ((), ())),
                            preferred_element_type=jnp.float32)
    rank = jnp.sum(jnp.where(hot, ahead, 0.0), axis=0, keepdims=True)
    return as_bf16(hot), rank.astype(jnp.int32)


def by_owner(hot, rank, values):
    slots = lax.broadcasted_iota(jnp.int32, (SLOTS, rank.shape[1]), 0) == rank
    rows = [jnp.where(slots, value, 0.0) for value in values]
    rows += [jnp.zeros_like(rows[0])] * (8 - len(rows))
    high, low = split_bf16(jnp.concatenate(rows, axis=0))
    both = dot_rows(hot, jnp.concatenate([high, low], axis=0))
    return both[:, :8 * SLOTS] + both[:, 8 * SLOTS:]


def fields_on_rows(landed_ref, ny):
    count, kinds, lanes = landed_ref.shape

    def of(device):
        if kinds == 1:
            return landed_ref[device]
        partner = device + ny // 2 if device % ny < ny // 2 else device - ny // 2
        return landed_ref[device, 0:1] + landed_ref[partner, 1:2]

    row = lax.broadcasted_iota(jnp.int32, (8, lanes), 0)
    block = lax.shift_right_logical(
        lax.broadcasted_iota(jnp.int32, (8, lanes), 1), jnp.full((8, lanes), SLOTS.bit_length() - 1, jnp.int32))
    groups = []
    for g in range(count // 8):
        value = jnp.concatenate([of(g * 8 + i) for i in range(8)], axis=0)
        for bit in (1, 2, 4):
            later = pltpu.roll(pltpu.roll(value, 8 - bit, 0), SLOTS * bit, 1)
            sooner = pltpu.roll(pltpu.roll(value, bit, 0), lanes - SLOTS * bit, 1)
            row_bit, block_bit = row & bit, block & bit
            value = jnp.where(row_bit == block_bit, value, jnp.where(row_bit == 0, later, sooner))
        groups.append(value)
    return jnp.concatenate(groups, axis=1)


def fill_weights(count, me, places, high_ref, low_ref):
    angles = high_ref.shape[0] // 2
    slots = places.shape[1]
    azimuth = jnp.full((16, 128), me.astype(jnp.float32) * (2.0 * math.pi / count))
    cos_phi, sin_phi = cos_sin(azimuth)
    pos = [jnp.broadcast_to(places[c:c + 1], (16, slots)) for c in range(3)]

    def group(g, carry):
        start = pl.multiple_of(g * 16, 16)
        index = (lax.broadcasted_iota(jnp.int32, (16, 128), 0) + start).astype(jnp.float32)
        cos_theta, sin_theta = cos_sin(math.pi * (index + 0.5) / angles)
        for part in range(0, slots, 128):
            at = slice(part, part + 128)
            phase = KAPPA * (pos[0][:, at] * sin_theta * cos_phi + pos[1][:, at] * sin_theta * sin_phi
                             + pos[2][:, at] * cos_theta)
            for s, value in enumerate(cos_sin(phase)):
                high, low = split_bf16(value)
                rows = pl.ds(pl.multiple_of(start + s * angles, 16), 16)
                high_ref[rows, at] = high
                low_ref[rows, at] = low
        return carry

    lax.fori_loop(0, angles // 16, group, 0)


def to_owners(count, ny, me, out_ref, landed_ref, sems):
    def copy(k):
        to = lax.rem(me + k, count)
        return pltpu.make_async_remote_copy(
            out_ref.at[to], landed_ref.at[me], sems.at[0], sems.at[1],
            device_id=(lax.div(to, ny), lax.rem(to, ny)), device_id_type=MESH)

    def start(*kinds):
        for i in range(count):
            for kind, rows in enumerate(kinds):
                out_ref[i, kind:kind + 1] = rows[i:i + 1]
        landed_ref[me] = out_ref[me]
        in_fours(count, lambda k: copy(k).start())

    others = pl.ds(0, count - 1)
    whole = pltpu.make_async_remote_copy(
        out_ref.at[others], landed_ref.at[others], sems.at[0], sems.at[1],
        device_id=(me // ny, me % ny), device_id_type=MESH)
    return start, whole.wait_recv, whole.wait_send


def step_kernel(nx, ny, cx, cy, cz, scale, fields_hbm, material_hbm, permit_hbm,
                cell_hbm, owner_hbm, out_ref, far_ref, material_ref, permit_ref, cell_row, owner_row,
                grid_x, slopes_z, grid_y, y_out, y_low, y_high, mid_low, mid_high, coef_x,
                gain_x, pivot_x, left_x, right_x, solved_x,
                coef_y, gain_y, pivot_y, left_y, right_y, solved_y,
                weight_high, weight_low, place_out, place_in, value_out, value_in, packed, near_packed, low_packed, high_packed, spots, spots_smem,
                facts, other_facts, factors, other_factors,
                load_sem, move_sems, halo_sems, place_sems, value_sems, fact_sems, small_sems, *line_refs):
    half_step = COURANT / 2.0
    half_side = 0.5 * half_step
    count = nx * ny
    wide = padded_rows(cx)
    tiles_x, tiles_y = cy // TILE, cx // TILE
    me = lax.axis_index("gx") * ny + lax.axis_index("gy")
    barrier = pltpu.get_barrier_semaphore()
    inner = grid_x.at[:, pl.ds(1, cx), pl.ds(TILE, cy)]
    load = pltpu.make_async_copy(fields_hbm, inner, load_sem)
    for m in range(6):
        pltpu.make_async_copy(fields_hbm.at[m], inner.at[m], load_sem).start()
    greet_all(count, ny, me, barrier)
    load_material = pltpu.make_async_copy(material_hbm, material_ref, move_sems.at[0])
    load_material.start()
    load_small = [
        pltpu.make_async_copy(source, target, small_sems.at[i])
        for i, (source, target) in enumerate(
            ((permit_hbm, permit_ref), (cell_hbm, cell_row), (owner_hbm, owner_row)))
    ]
    for one in load_small:
        one.start()
    line_x = Line("gx", nx, line_refs[:10])
    line_y = Line("gy", ny, line_refs[10:])

    def x_halo(first, sems):
        plane = lambda i: grid_x.at[pl.ds(first, 2), i, pl.ds(TILE, cy)]
        return both_ways("gx", nx, plane(1), plane(cx), plane(0), plane(cx + 1), sems)

    mid_plane = lambda j: grid_y.at[:, pl.ds((j + 1) * wide + TILE, cx)]
    first_halos = [
        both_ways("gy", ny, y_out.at[0], y_out.at[1], y_low, y_high, halo_sems.at[0]),
        x_halo(1, halo_sems.at[1]),
        x_halo(4, halo_sems.at[2]),
    ]
    mid_halo = both_ways("gy", ny, mid_plane(0), mid_plane(cy - 1), mid_low, mid_high, halo_sems.at[3])

    def coefs(i, carry):
        which = material_ref[i]
        permit = jnp.zeros(which.shape, jnp.float32)
        for entry in range(permit_ref.shape[0]):
            permit = jnp.where(which == entry, permit_ref[entry], permit)
        coef_x[pl.ds(pl.multiple_of(i * cy, 8), cy), :] = (half_step * half_step) / permit
        return carry

    load.wait()
    for slot, member in enumerate(Y_MEMBERS):
        for end, row in ((0, TILE), (1, TILE + cy - 1)):
            y_out[end, slot] = jnp.concatenate(
                [grid_x[member, 1 + i, row:row + 1] for i in range(cx)], axis=0)
    pl.semaphore_wait(barrier, count - 1)
    for halo in first_halos:
        halo[0]()
        halo[1]()
    load_material.wait()
    for one in load_small:
        one.wait()
    lax.fori_loop(0, cx, coefs, 0, unroll=2)
    coef_plane = lambda i: coef_x[pl.ds(pl.multiple_of(i * cy, 8), cy), :]
    factor(cx, coef_plane, gain_x, pivot_x, left_x, right_x)
    line_x.mat_start(left_x, right_x)
    for j in range(cy):
        coef_y[j] = coef_x[pl.ds(j, cx, stride=cy), :]
    for m in range(6):
        for plane in (0, cy + 1):
            grid_y[m, pl.ds(plane * wide, wide), :] = jnp.zeros((wide, cz), jnp.float32)
    patches = cell_row.shape[1]
    cell = cell_row[...]
    line = lax.shift_right_logical(cell, jnp.full_like(cell, cz.bit_length() - 1))
    at_x = jnp.zeros_like(cell)
    for i in range(1, cx):
        at_x = at_x + jnp.where(line >= i * cy, 1, 0)
    at_y, at_z = line - at_x * cy, cell - line * cz
    lanes = lax.broadcasted_iota(jnp.int32, cell.shape, 1)
    spots[0:1] = (at_y * cx + at_x) * 8
    spots[1:2] = (lanes - at_z) & (cz - 1)
    find = pltpu.make_async_copy(spots, spots_smem, move_sems.at[1])
    find.start()
    places = [at_x + lax.axis_index("gx") * cx, at_y + lax.axis_index("gy") * cy, at_z]
    hot, rank = slot_ranks(count, owner_row[...])
    place_send = to_owners(count, ny, me, place_out, place_in, place_sems)
    value_send = to_owners(count, ny, me, value_out, value_in, value_sems)
    place_send[0](by_owner(hot, rank, [place.astype(jnp.float32) for place in places]))
    facts[0:1] = at_x
    facts[1:2] = at_z
    facts[2:3] = owner_row[...]
    facts[3:4] = rank
    last = line_y.steps - 1
    tell = [
        pltpu.make_async_remote_copy(
            source, target, fact_sems.at[2 * i], fact_sems.at[2 * i + 1],
            device_id=line_y.partner(last), device_id_type=MESH)
        for i, (source, target) in enumerate(((facts, other_facts), (factors, other_factors)))
    ]
    tell[0].start()

    def gathered(ref, where_ref):
        lane = lax.broadcasted_iota(jnp.int32, (8, cz), 1)
        found = []
        for first in range(0, patches, cz):
            kept = jnp.zeros((8, cz), jnp.float32)
            for at in range(cz):
                rows = ref[pl.ds(where_ref[0, first + at], 8), :]
                kept = jnp.where(lane == at, pltpu.roll(rows, where_ref[1, first + at], 1), kept)
            found.append(kept)
        return jnp.concatenate(found, axis=1)

    factor(cy, lambda j: coef_y[j], gain_y, pivot_y, left_y, right_y)
    line_y.mat_start(left_y, right_y)
    def along_z(i, carry):
        for slot, m in enumerate(Z_MEMBERS):
            slopes_z[slot, i] = lane_difference(grid_x[m, i + 1, pl.ds(TILE, cy)])
        return carry

    lax.fori_loop(0, cx, along_z, 0, unroll=4)
    for halo in first_halos:
        halo[2]()

    def solve_x(tile):
        row = (tile + 1) * TILE
        for at, side, need in ((TILE - 1, y_low, tile == 0), (TILE + cy, y_high, tile == tiles_x - 1)):
            for slot, member in enumerate(Y_MEMBERS if need else ()):
                for i in range(cx):
                    grid_x[member, i + 1, at:at + 1] = side[slot, i:i + 1]

        def forward(i, carry):
            near = lambda m, plane, shift: grid_x[m, i + 1 + plane, row + shift:row + shift + TILE]
            centre = [near(m, 0, 0) for m in range(6)]
            dx = {m: near(m, 1, 0) - near(m, -1, 0) for m in X_MEMBERS}
            dy = {m: near(m, 0, 1) - near(m, 0, -1) for m in Y_MEMBERS}
            coef = coef_x[pl.ds(pl.multiple_of(i * cy + tile * TILE, 8), TILE), :]
            dz = {m: slopes_z[slot, i, tile_rows(tile)] for slot, m in enumerate(Z_MEMBERS)}
            right = updated(centre, dx, dy, dz, coef * (0.5 / half_step), half_side)
            gain, pivot = gain_x[i, tile_rows(tile)], pivot_x[i, tile_rows(tile)]
            now = [right[m] * pivot + gain * carry[m] for m in range(6)]
            for m in range(6):
                solved_x[m, i, tile_rows(tile)] = now[m]
            return tuple(now)

        lax.fori_loop(0, cx, forward, (jnp.zeros((TILE, cz), jnp.float32),) * 6, unroll=8)
        sweep_back(cx, gain_x, solved_x, tile_rows(tile), 16)
        for half, members in enumerate(HALVES):
            line_x.rhs_start(tile, half, [solved_x[m, 0, tile_rows(tile)] for m in members],
                             [solved_x[m, cx - 1, tile_rows(tile)] for m in members])

    def finish_x(tile):
        rows = tile_rows(tile)
        planes = lambda i: pl.ds((tile * TILE + 1) * wide + TILE + i, TILE, stride=wide)
        ends = [[line_x.ends[end, m, rows] for m in range(6)] for end in range(2)]
        for m in range(6):
            grid_y[m, planes(-1), :] = ends[0][m]
            grid_y[m, planes(cx), :] = ends[1][m]
        for i in range(cx):
            left, right = left_x[i, rows], right_x[i, rows]
            for m in range(6):
                grid_y[m, planes(i), :] = solved_x[m, i, rows] + left * ends[0][m] + right * ends[1][m]

    def scaled_side(j):
        near = lambda m, plane, shift: grid_y[m, pl.ds((j + 1 + plane) * wide + TILE + shift, cx), :]
        centre = [near(m, 0, 0) for m in range(6)]
        dx = {m: near(m, 0, 1) - near(m, 0, -1) for m in X_MEMBERS}
        dy = {m: near(m, 1, 0) - near(m, -1, 0) for m in Y_MEMBERS}
        dz = {m: lane_difference(centre[m]) for m in Z_MEMBERS}
        right = updated(centre, dx, dy, dz, coef_y[j] * (0.5 / half_step), half_side)
        pivot = pivot_y[j]
        return [right[m] * pivot for m in range(6)]

    def advance(j, scaled, carry):
        gain = gain_y[j]
        now = [scaled[m] + gain * carry[m] for m in range(6)]
        for m in range(6):
            solved_y[m, j] = now[m]
        return tuple(now)

    def forward_y(j, carry):
        return advance(j, scaled_side(j), carry)

    def prepare_y(j, carry):
        for m, value in enumerate(scaled_side(j)):
            solved_y[m, j] = value
        return carry

    def resume_y(j, carry):
        return advance(j, [solved_y[m, j] for m in range(6)], carry)

    edge = TILE - 2
    order = [0, tiles_x - 1] + list(range(1, tiles_x - 1))
    for place, tile in enumerate(order):
        solve_x(tile)
        if place == 1:
            line_x.mat_merge(0)
    place_send[1]()
    fill_weights(count, me, fields_on_rows(place_in, ny), weight_high, weight_low)
    chunks = [(tile, half) for tile in order for half in range(len(HALVES))]
    for k in range(line_x.steps - 1):
        for place, chunk in enumerate(chunks):
            line_x.rhs_merge(k, *chunk)
            if place == 3 and k + 1 < line_x.steps - 1:
                line_x.mat_merge(k + 1)
        if k < line_y.steps:
            line_y.mat_merge(k)
    if line_x.steps > 1:
        line_x.mat_merge(line_x.steps - 1)
    for k in range(line_x.steps - 1, line_y.steps):
        line_y.mat_merge(k)
    inv, gain_in, gain_out = line_y.plan[last, 0], line_y.plan[last, 5], line_y.plan[last, 6]
    for j in range(cy):
        left, right = left_y[j], right_y[j]
        for slot, value in enumerate((left, right, (left * gain_in + right * gain_out) * inv)):
            for tile in range(tiles_y):
                packed[pl.ds((j * cx + tile * TILE) * 8 + slot, TILE, stride=8), :] = (
                    value[tile * TILE:(tile + 1) * TILE])
    find.wait()
    weights = gathered(packed, spots_smem)
    factors[...] = weights[2:3]
    tell[1].start()
    carry = (jnp.zeros((cx, cz), jnp.float32),) * 6
    for tile in order:
        for half in range(len(HALVES)):
            line_x.rhs_merge(line_x.steps - 1, tile, half)
        finish_x(tile)
        if tile == 0:
            mid_halo[1]()
            carry = lax.fori_loop(0, edge, forward_y, carry, unroll=6)
        if tile == tiles_x - 1:
            mid_halo[0]()
            lax.fori_loop(cy - edge, cy, prepare_y, 0, unroll=6)
    carry = lax.fori_loop(edge, cy - edge, forward_y, carry, unroll=6)
    lax.fori_loop(cy - edge, cy, resume_y, carry, unroll=6)
    sweep_back(cy, gain_y, solved_y, pl.ds(0, cx), 24)
    mid_halo[2]()

    def ghosts(tile):
        rows = tile_rows(tile)
        found = []
        for ref, at, sign in ((mid_low, 0, 1.0), (mid_high, cy - 1, -1.0)):
            side = sign * half_side / coef_y[at, rows]
            found.append({
                0: ref[5, rows] * (-sign * 0.5 / half_step),
                2: ref[3, rows] * (sign * 0.5 / half_step),
                3: ref[2, rows] * side,
                5: ref[0, rows] * -side,
            })
        return found

    added = [ghosts(tile) for tile in range(tiles_y)]
    for tile in range(tiles_y):
        rows = tile_rows(tile)
        low, high = added[tile]

        def outer(m, at):
            value = solved_y[m, at, rows]
            return value + left_y[at, rows] * low[m] + right_y[at, rows] * high[m] if m in low else value

        for half, members in enumerate(HALVES):
            line_y.rhs_start(tile, half, [outer(m, 0) for m in members], [outer(m, cy - 1) for m in members])
    for tile in range(tiles_y):
        for j in range(cy):
            for m in range(6):
                packed[pl.ds((j * cx + tile * TILE) * 8 + m, TILE, stride=8), :] = solved_y[m, j, tile_rows(tile)]
    values = gathered(packed, spots_smem)
    for k in range(line_y.steps - 1):
        for tile in range(tiles_y):
            for half in range(len(HALVES)):
                line_y.rhs_merge(k, tile, half)
    for tile in range(tiles_y):
        for m in range(6):
            rows = pl.ds(tile * TILE * 8 + m, TILE, stride=8)
            ends = line_y.known_ends(tile, m)
            if m in added[tile][0]:
                ends = [ends[end] + added[tile][end][m] for end in range(2)]
            low_packed[rows, :] = ends[0]
            high_packed[rows, :] = ends[1]
            near_packed[rows, :] = line_y.near_value(tile, m)
    for one in tell:
        one.wait_recv()
    values = (values + weights[0:1] * at_columns(low_packed, at_x, at_z)
              + weights[1:2] * at_columns(high_packed, at_x, at_z))
    theirs = at_columns(near_packed, other_facts[0:1], other_facts[1:2]) * other_factors[...]
    other_hot = (lax.broadcasted_iota(jnp.int32, (count, patches), 0) == other_facts[2:3])
    other_hot = jnp.where(other_hot, 1.0, 0.0).astype(jnp.bfloat16)
    value_send[0](by_owner(hot, rank, [values[m:m + 1] for m in range(6)]),
                  by_owner(other_hot, other_facts[3:4], [theirs[m:m + 1] for m in range(6)]))
    for tile in range(tiles_y):
        for half in range(len(HALVES)):
            line_y.rhs_merge(line_y.steps - 1, tile, half)
        rows = tile_rows(tile)
        ends = [[line_y.ends[end, m, rows] + added[tile][end][m] if m in added[tile][end]
                 else line_y.ends[end, m, rows] for m in range(6)] for end in range(2)]
        for j in range(cy):
            left, right = left_y[j, rows], right_y[j, rows]
            for m in range(6):
                out_ref[pl.ds((m * cx + tile * TILE) * cy + j, TILE, stride=cy), :] = (
                    solved_y[m, j, rows] + left * ends[0][m] + right * ends[1][m])
    for one in tell:
        one.wait_send()
    for halo in [*first_halos, mid_halo]:
        halo[3]()
    line_x.drain()
    line_y.drain()
    place_send[2]()
    value_send[1]()
    high, low = split_bf16(fields_on_rows(value_in, ny))
    both = jnp.concatenate([high, low], axis=0)
    product = dot_rows(both, weight_high[...]) + dot_rows(both, weight_low[...])
    product = (product[:8] + product[8:]) * scale
    angles = far_ref.shape[1]
    for s in range(2):
        far_ref[pl.ds(s * 6, 6), :] = product[:6, s * angles:(s + 1) * angles]
    value_send[2]()


def store_kernel(new_ref, far_ref, new_hbm, far_hbm, sems):
    rows = new_ref.shape[0] // 6
    for m in range(6):
        part = pl.ds(m * rows, rows)
        pltpu.make_async_copy(new_ref.at[part], new_hbm.at[part], sems.at[0]).start()
    far = pltpu.make_async_copy(far_ref, far_hbm, sems.at[1])
    far.start()
    pltpu.make_async_copy(new_ref, new_hbm, sems.at[0]).wait()
    far.wait()


def line_scratch(count, rows, lanes):
    steps = count.bit_length() - 1
    chunks = rows // TILE * len(HALVES)
    f32 = jnp.float32
    return [
        pltpu.VMEM((steps, 4, rows, lanes), f32),
        pltpu.VMEM((steps, 4, rows, lanes), f32),
        pltpu.VMEM((steps, chunks, 2, len(HALVES[0]), TILE, lanes), f32),
        pltpu.VMEM((steps, chunks, 2, len(HALVES[0]), TILE, lanes), f32),
        pltpu.VMEM((steps, 7, rows, lanes), f32),
        pltpu.VMEM((4, rows, lanes), f32),
        pltpu.VMEM((2, 6, rows, lanes), f32),
        pltpu.SemaphoreType.DMA((4,)),
        pltpu.SemaphoreType.DMA((steps,)),
        pltpu.SemaphoreType.DMA((steps, chunks)),
    ]


def local(nx, ny, fields, material, permittivity, patch_cell, patch_owner):
    _, cx, cy, cz = fields.shape
    f32 = jnp.float32
    count = nx * ny
    patches = patch_cell.shape[0]
    vmem = pl.BlockSpec(memory_space=pltpu.VMEM)
    hbm = pl.BlockSpec(memory_space=pltpu.HBM)
    x_lines = [pltpu.VMEM((cx, cy, cz), f32)] * 4
    y_lines = [pltpu.VMEM((cy, cx, cz), f32)] * 4
    pinned = lambda value: pltpu.with_memory_space_constraint(value, pltpu.HBM)
    new_flat, far_field = pl.pallas_call(
        functools.partial(step_kernel, nx, ny, cx, cy, cz, 1.0 / math.sqrt(patches)),
        out_shape=(
            jax.ShapeDtypeStruct((6 * cx * cy, cz), f32),
            jax.ShapeDtypeStruct((12, ANG_DEV), f32),
        ),
        in_specs=[hbm] * 5,
        out_specs=(vmem, vmem),
        scratch_shapes=[
            pltpu.VMEM((cx, cy, cz), jnp.int32),
            pltpu.SMEM(permittivity.shape, f32),
            pltpu.VMEM((1, patches), jnp.int32),
            pltpu.VMEM((1, patches), jnp.int32),
            pltpu.VMEM((6, cx + 2, cy + 2 * TILE, cz), f32),
            pltpu.VMEM((len(Z_MEMBERS), cx, cy, cz), f32),
            pltpu.VMEM((6, (cy + 2) * padded_rows(cx), cz), f32),
            pltpu.VMEM((2, 4, cx, cz), f32),
            pltpu.VMEM((4, cx, cz), f32),
            pltpu.VMEM((4, cx, cz), f32),
            pltpu.VMEM((6, cx, cz), f32),
            pltpu.VMEM((6, cx, cz), f32),
            pltpu.VMEM((cx * cy, cz), f32),
            *x_lines,
            pltpu.VMEM((6, cx, cy, cz), f32),
            pltpu.VMEM((cy, cx, cz), f32),
            *y_lines,
            pltpu.VMEM((6, cy, cx, cz), f32),
            pltpu.VMEM((2 * ANG_DEV, SLOTS * count), jnp.bfloat16),
            pltpu.VMEM((2 * ANG_DEV, SLOTS * count), jnp.bfloat16),
            *[pltpu.VMEM((count, 1, 8 * SLOTS), f32)] * 2,
            *[pltpu.VMEM((count, 2, 8 * SLOTS), f32)] * 2,
            pltpu.VMEM((cx * cy * 8, cz), f32),
            *[pltpu.VMEM((cx * 8, cz), f32)] * 3,
            pltpu.VMEM((2, patches), jnp.int32),
            pltpu.SMEM((2, patches), jnp.int32),
            pltpu.VMEM((4, patches), jnp.int32),
            pltpu.VMEM((4, patches), jnp.int32),
            pltpu.VMEM((1, patches), f32),
            pltpu.VMEM((1, patches), f32),
            pltpu.SemaphoreType.DMA,
            pltpu.SemaphoreType.DMA((2,)),
            pltpu.SemaphoreType.DMA((4, 4)),
            pltpu.SemaphoreType.DMA((2,)),
            pltpu.SemaphoreType.DMA((2,)),
            pltpu.SemaphoreType.DMA((4,)),
            pltpu.SemaphoreType.DMA((3,)),
            *line_scratch(nx, cy, cz),
            *line_scratch(ny, cx, cz),
        ],
        compiler_params=pltpu.CompilerParams(
            collective_id=0, has_side_effects=True, vmem_limit_bytes=40 * 2**20),
        name="split_step",
    )(pinned(fields), pinned(material), pinned(permittivity), pinned(patch_cell[None, :]),
      pinned(patch_owner.reshape(1, patches)))
    new_flat, far_field = pl.pallas_call(
        store_kernel,
        out_shape=(
            jax.ShapeDtypeStruct((6 * cx * cy, cz), f32),
            jax.ShapeDtypeStruct((12, ANG_DEV), f32),
        ),
        in_specs=[vmem, vmem],
        out_specs=(hbm, hbm),
        scratch_shapes=[pltpu.SemaphoreType.DMA((2,))],
        compiler_params=pltpu.CompilerParams(vmem_limit_bytes=4 * 2**20),
        name="store",
    )(new_flat, far_field)
    return new_flat.reshape(fields.shape), far_field


def solution(mesh):
    return jax.shard_map(
        functools.partial(local, mesh.shape["gx"], mesh.shape["gy"]),
        mesh=mesh,
        in_specs=(
            P(None, "gx", "gy", None),
            P("gx", "gy", None),
            P(),
            P(("gx", "gy")),
            P(("gx", "gy"), None),
        ),
        out_specs=(P(None, "gx", "gy", None), P(None, ("gx", "gy"))),
        check_vma=False,
    )
```
